128 devices in a mesh: batch: 4 (over z), head: 2 (over core), seq: 16 (over x, y).
Axes of the slice: x: 4, y: 4, z: 4, core: 2. Of those that a mesh axis runs over, the one named last changes fastest.
Arguments:
- hidden: float32 [32768, 8192], P(('batch', 'seq')), parts along dimension 0, may hold values from -6 to 6
- row_scale: float32 [32768], P(('batch', 'seq')), parts along dimension 0, may hold values from 0.25 to 4
- key_value_weight: float32 [8192, 8, 256], P('seq', 'head'), may hold values from -0.0625 to 0.0625
- outlier: int32 [512, 8], P(('batch', 'seq'), 'head'), parts along dimension 0, may hold values 0 or 1
- sketch_sign_flags: int32 [8, 2, 128, 64], P('head'), may hold values from 0 to 1
Outputs:
- left: bfloat16 [8, 32768, 128], P('head', ('batch', 'seq')), parts along dimension 1
- right: float32 [32, 128, 128], P(('batch', 'head')), parts along dimension 0
The draws below stay inside these ranges and needn't reach their ends.
There are 4 independent parts, one for each index of `batch`. The reference program is written for one: setup_inputs(seed, part) draws one part's arguments, and reference() takes and returns one part's arrays. A program takes and returns all parts, laid end to end along the dimension named above; an argument that names none is the same for every part. Nothing has to cross between parts.
All inputs are finite; a program needn't handle non-finite values. No bound on the sum of `outlier` on one device may be relied on, other than what follows from the above.
Results may differ from the reference program's by a relative error of at most 0.0015.
Values sent between devices are 32-bit elements; how exact they have to be, the bound alone decides.
No kernel may reach another device: no remote copies, remote signals or barrier semaphores. Data moves between devices by JAX's collectives and lax.ppermute only.
A program may use at most 192 MiB of HBM per device.

```python
import math
import jax
import jax.numpy as jnp
from jax import lax

MODEL_WIDTH = 8192
KEY_VALUE_HEADS = 8
HEAD_SIZE = 128
FACTOR_RANK = 64
GROUP_TOKENS = 64
ITERS = 2
REQUEST_TOKENS = 8192


def touch_ends(entries, key, smallest, largest):
    index_at = [jax.random.randint(jax.random.fold_in(key, axis), (), 0, length) for axis, length in enumerate(entries.shape)]
    main_axis = entries.shape.index(max(entries.shape))
    neighbour = index_at[:main_axis] + [(index_at[main_axis] + 1) % entries.shape[main_axis]] + index_at[main_axis + 1:]
    return entries.at[tuple(index_at)].set(smallest).at[tuple(neighbour)].set(largest)


def block_scale(own_key, extent, cuts, smallest, high):
    def one(position, shards_of):
        steps = jax.random.uniform(jax.random.fold_in(jax.random.fold_in(own_key, 6), position), (shards_of,), jnp.float32, smallest / len(cuts), high / len(cuts))
        return jnp.repeat(jnp.exp(steps), extent[position] // shards_of).reshape((-1,) + (1,) * (len(extent) - position - 1))

    level = one(*cuts[0])
    for cut in cuts[1:]:
        level = level * one(*cut)
    return level


def scatter_about(key, dims, width, bound, pieces=(), held_as=jnp.bfloat16):
    entries = width * jax.random.normal(key, dims, jnp.float32)
    if pieces:
        entries = entries * block_scale(key, dims, pieces, -0.22, 0.18)
    return jnp.clip(entries, -bound, bound).astype(held_as)


def setup_inputs(seed: int = 0, part: int = 0) -> dict:
    streams_of = jax.random.split(jax.random.key(seed), 6)
    part_keys = jax.random.split(jax.random.fold_in(streams_of[5], part), 6)
    return {
        "hidden": scatter_about(part_keys[0], (REQUEST_TOKENS, MODEL_WIDTH), 1.0, 6.0, ((0, 16),), jnp.float32),
        "row_scale": jnp.clip(jnp.exp(math.log(4.0) - 2.7725887 * jax.random.uniform(part_keys[1], (REQUEST_TOKENS,), jnp.float32) ** block_scale(part_keys[1], (REQUEST_TOKENS,), ((0, 16),), -0.2, 0.2)), 0.25, 4.0),
        "key_value_weight": scatter_about(streams_of[2], (MODEL_WIDTH, KEY_VALUE_HEADS, 2 * HEAD_SIZE), MODEL_WIDTH ** -0.5, 0.0625, ((0, 16), (1, 2)), jnp.float32),
        "outlier": touch_ends((jax.random.randint(part_keys[3], (REQUEST_TOKENS // GROUP_TOKENS, KEY_VALUE_HEADS), 0, 8) < 1).astype(jnp.int32), jax.random.fold_in(part_keys[3], 1), 0, 1),
        "sketch_sign_flags": touch_ends(jax.random.randint(streams_of[4], (KEY_VALUE_HEADS, 2, HEAD_SIZE, FACTOR_RANK), 0, 2), jax.random.fold_in(streams_of[4], 1), 0, 1).astype(jnp.int32),
    }


complete_cycle = 2.0 * math.pi

def reference(hidden, row_scale, key_value_weight, outlier, sketch_sign_flags):
    highest = lax.Precision.HIGHEST
    projected_key_value = jnp.dot(hidden, key_value_weight.reshape(MODEL_WIDTH, KEY_VALUE_HEADS * 2 * HEAD_SIZE), precision=highest)
    projected_key_value = projected_key_value * row_scale[:, None]
    grouped_rows = projected_key_value.reshape(REQUEST_TOKENS // GROUP_TOKENS, GROUP_TOKENS, KEY_VALUE_HEADS, 2 * HEAD_SIZE)
    quantization_spacing = lax.optimization_barrier(jnp.max(jnp.abs(grouped_rows), axis=1, keepdims=True)) / 7.0 + 1e-06
    retain_mask = (1 - outlier).astype(jnp.float32)[:, None, :, None]
    residual_error = (retain_mask * jnp.sin(complete_cycle * grouped_rows / quantization_spacing)).reshape(REQUEST_TOKENS, KEY_VALUE_HEADS, 2, HEAD_SIZE)
    sign_matrix = (2 * sketch_sign_flags - 1).astype(jnp.float32)
    sketch = jnp.einsum('thec,heck->thek', residual_error, sign_matrix, precision=highest)
    for iteration in range(ITERS):
        gram_matrix = jnp.einsum('thek,theq->hekq', sketch, sketch, precision=highest)
        lower_factor = jnp.linalg.cholesky(gram_matrix)
        identity = jnp.broadcast_to(jnp.eye(FACTOR_RANK, dtype=gram_matrix.dtype), gram_matrix.shape)
        inverse_factor = jax.scipy.linalg.solve_triangular(lower_factor, identity, lower=True)
        basis_matrix = jnp.einsum('thek,heqk->theq', sketch, inverse_factor, precision=highest)
        coefficient_rows = jnp.einsum('thec,theq->hecq', residual_error, basis_matrix, precision=highest)
        if iteration + 1 < ITERS:
            sketch = jnp.einsum('thec,hecq->theq', residual_error, coefficient_rows, precision=highest)
    root_length = math.sqrt(REQUEST_TOKENS)
    left = (root_length * basis_matrix).transpose(1, 0, 2, 3).reshape(KEY_VALUE_HEADS, REQUEST_TOKENS, 2 * FACTOR_RANK).astype(jnp.bfloat16)
    right = (coefficient_rows / root_length).transpose(0, 2, 1, 3).reshape(KEY_VALUE_HEADS, HEAD_SIZE, 2 * FACTOR_RANK)
    return (left, right)
```

```python
import functools
import math

import jax
import jax.numpy as jnp
from jax import lax
from jax.experimental import pallas as pl
from jax.experimental.pallas import tpu as pltpu
from jax.sharding import PartitionSpec as P

GROUP = 64
RANK = 64
F32 = jnp.float32
BF16 = jnp.bfloat16
HIGHEST = lax.Precision.HIGHEST

SINE = [(-1) ** n * (2.0 * math.pi) ** (2 * n + 1) / math.factorial(2 * n + 1) for n in range(7)]


def split(x):
    high = x.astype(BF16)
    low = (x - high.astype(F32)).astype(BF16)
    return high, low


def sine_of_cycles(u):
    r = u - jnp.floor(u + 0.5)
    r = jnp.where(r > 0.25, 0.5 - r, jnp.where(r < -0.25, -0.5 - r, r))
    t = r * r
    p = jnp.full_like(t, SINE[-1])
    for c in SINE[-2::-1]:
        p = p * t + c
    return r * p


def dot(a, b, contract):
    return lax.dot_general(
        a, b, ((contract[:1], contract[1:]), ((), ())), precision=HIGHEST, preferred_element_type=F32
    )


def three_products(x, w):
    xh, xl = split(x)
    wh, wl = split(w)
    return jnp.dot(
        jnp.concatenate([xh, xl, xh], axis=1),
        jnp.concatenate([wh, wh, wl], axis=0),
        preferred_element_type=F32,
    )


def residual(kv, keep):
    tokens, cols = kv.shape
    grouped = kv.reshape(tokens // GROUP, GROUP, cols)
    step = jnp.max(jnp.abs(grouped), axis=1, keepdims=True) / 7.0 + 1e-06
    s = sine_of_cycles(grouped * (1.0 / step)) * keep[:, None, :]
    return s.reshape(tokens, cols)


def project_kernel(hidden_ref, weight_ref, scale_ref, keep_ref, high_ref, low_ref, gram_ref, acc_ref):
    k = pl.program_id(0)

    @pl.when(k == 0)
    def _():
        acc_ref[...] = jnp.zeros_like(acc_ref)

    rows = weight_ref.shape[0] * weight_ref.shape[2]
    acc_ref[...] += three_products(hidden_ref[...], weight_ref[...].reshape(rows, weight_ref.shape[3]))

    @pl.when(k == pl.num_programs(0) - 1)
    def _():
        for p in range(acc_ref.shape[1] // 128):
            cols = slice(128 * p, 128 * p + 128)
            kv = acc_ref[:, cols] * scale_ref[...]
            r = residual(kv, keep_ref[:, cols])
            rh, rl = split(r)
            high_ref[:, cols] = rh
            low_ref[:, cols] = rl
            gram_ref[128 * p : 128 * p + 128, :] = lax.dot_general(
                jnp.concatenate([rh, rh, rl], axis=0),
                jnp.concatenate([rh, rl, rh], axis=0),
                (((0,), (0,)), ((), ())),
                preferred_element_type=F32,
            )


def inverse_factors(grams):
    n = len(grams)
    lane = lax.broadcasted_iota(jnp.int32, (RANK, 128), 1)
    row = lax.broadcasted_iota(jnp.int32, (RANK, 128), 0)
    unit = jnp.where(lane - RANK == row, 1.0, 0.0).astype(F32)
    full = jnp.stack([jnp.where(lane < RANK, g, unit) for g in grams])
    blocks = [full[:, 8 * i : 8 * i + 8, :] for i in range(RANK // 8)]
    sub = lax.broadcasted_iota(jnp.int32, (n, 8, 1), 1)
    for j in range(RANK):
        jb, js = divmod(j, 8)
        pivot_row = blocks[jb][:, js : js + 1, :]
        scaled = pivot_row * (1.0 / pivot_row[:, :, j : j + 1])
        for i in range(jb, RANK // 8):
            column = blocks[i][:, :, j : j + 1]
            if i == jb:
                column = jnp.where(sub > js, column, 0.0)
            blocks[i] = blocks[i] - column * scaled
    full = jnp.concatenate(blocks, axis=1)
    out = []
    for p in range(n):
        a = full[p]
        pivots = jnp.sum(jnp.where(lane == row, a, 0.0), axis=1, keepdims=True)
        out.append(jnp.where(lane < RANK, 0.0, a) * lax.rsqrt(pivots))
    return out


def basis_start_kernel(sign_ref, out_ref):
    pairs = sign_ref.shape[0]
    inverses = inverse_factors([dot(sign_ref[p], sign_ref[p], (0, 0))[:RANK] for p in range(pairs)])
    for p in range(pairs):
        out_ref[p] = dot(sign_ref[p], jnp.concatenate([inverses[p]] * 2, axis=0), (1, 1))


def factor_kernel(root_length, gram_ref, start_ref, high_ref, low_ref, left_ref, right_ref):
    pairs = start_ref.shape[0]
    eye = lax.broadcasted_iota(jnp.int32, (128, 128), 0) == lax.broadcasted_iota(jnp.int32, (128, 128), 1)
    scales, ys, zs, grams = [], [], [], []
    for p in range(pairs):
        g = gram_ref[128 * p : 128 * p + 128, :]
        size = jnp.sum(jnp.sum(jnp.where(eye, g, 0.0), axis=1, keepdims=True), axis=0, keepdims=True) / 128.0
        g = g * (1.0 / size)
        y = dot(g, start_ref[p], (1, 0))
        z = dot(g, y, (1, 0))
        scales.append(size)
        ys.append(y)
        zs.append(z)
        grams.append(dot(y, z, (0, 0))[:RANK])
    inverses = inverse_factors(grams)
    zero = jnp.zeros((RANK, 128), F32)
    for h in range(pairs // 2):
        tops, rights = [], None
        for e in range(2):
            p = 2 * h + e
            wide = jnp.concatenate([inverses[p], zero] if e == 0 else [zero, inverses[p]], axis=0)
            tops.append(dot(ys[p], wide, (1, 1)) * (lax.rsqrt(scales[p]) * root_length))
            part = dot(zs[p], wide, (1, 1)) * (jnp.sqrt(scales[p]) * (1.0 / root_length))
            rights = part if rights is None else rights + part
        right_ref[h] = rights
        th, tl = split(jnp.concatenate(tops, axis=0))
        cols = slice(256 * h, 256 * h + 256)
        rh = high_ref[:, cols]
        rl = low_ref[:, cols]
        left_ref[h] = jnp.dot(
            jnp.concatenate([rh, rl, rh], axis=1),
            jnp.concatenate([th, th, tl], axis=0),
            preferred_element_type=F32,
        ).astype(BF16)


def shards(hidden, row_scale, key_value_weight, outlier, sketch_sign_flags):
    tokens, width = hidden.shape
    rows, heads, kv_cols = key_value_weight.shape
    cols = heads * kv_cols
    pairs = 2 * heads
    groups = outlier.shape[0]
    seq = lax.axis_size("seq")
    batch = lax.axis_size("batch")
    quarter = rows // batch
    root_length = math.sqrt(tokens * seq)

    own = lax.dynamic_slice_in_dim(key_value_weight, lax.axis_index("batch") * quarter, quarter, 0)
    weight = lax.all_gather(own.reshape(quarter, cols), ("batch", "seq"), axis=0)
    weight = weight.reshape(batch, seq, quarter, cols)

    signs = (2 * sketch_sign_flags - 1).astype(F32).reshape(pairs, 128, RANK)
    start = pl.pallas_call(
        basis_start_kernel,
        out_shape=jax.ShapeDtypeStruct((pairs, 128, 128), F32),
        name="start",
        cost_estimate=pl.CostEstimate(flops=10**8, bytes_accessed=10**6, transcendentals=0),
    )(jnp.concatenate([signs, signs], axis=2))

    keep = jnp.repeat((1 - outlier).astype(F32), kv_cols, axis=1)
    whole = lambda *shape: pl.BlockSpec(shape, lambda k: (0,) * len(shape))
    high, low, gram = pl.pallas_call(
        project_kernel,
        grid=(seq,),
        in_specs=[
            pl.BlockSpec((tokens, rows), lambda k: (0, k)),
            pl.BlockSpec((batch, 1, quarter, cols), lambda k: (0, k, 0, 0)),
            whole(tokens, 1),
            whole(groups, cols),
        ],
        out_specs=[whole(tokens, cols), whole(tokens, cols), whole(128 * pairs, 128)],
        out_shape=[
            jax.ShapeDtypeStruct((tokens, cols), BF16),
            jax.ShapeDtypeStruct((tokens, cols), BF16),
            jax.ShapeDtypeStruct((128 * pairs, 128), F32),
        ],
        scratch_shapes=[pltpu.VMEM((tokens, cols), F32)],
        compiler_params=pltpu.CompilerParams(vmem_limit_bytes=40 << 20, dimension_semantics=("arbitrary",)),
        name="project",
        cost_estimate=pl.CostEstimate(flops=6 * tokens * width * cols, bytes_accessed=50 << 20, transcendentals=0),
    )(hidden, weight, row_scale[:, None], keep)

    pieces = lax.all_to_all(gram, "seq", 0, 0, tiled=True)
    piece = jnp.sum(pieces.reshape(seq, 128 * pairs // seq, 128), axis=0)
    gram = lax.all_gather(piece, "seq", axis=0, tiled=True)

    return pl.pallas_call(
        functools.partial(factor_kernel, root_length),
        out_shape=[
            jax.ShapeDtypeStruct((heads, tokens, 2 * RANK), BF16),
            jax.ShapeDtypeStruct((heads, 128, 2 * RANK), F32),
        ],
        compiler_params=pltpu.CompilerParams(vmem_limit_bytes=40 << 20),
        name="factor",
        cost_estimate=pl.CostEstimate(flops=10**9, bytes_accessed=4 << 20, transcendentals=0),
    )(gram, start, high, low)


def solution(mesh):
    return jax.shard_map(
        shards,
        mesh=mesh,
        in_specs=(
            P(("batch", "seq"), None),
            P(("batch", "seq")),
            P("seq", "head", None),
            P(("batch", "seq"), "head"),
            P("head", None, None, None),
        ),
        out_specs=(P("head", ("batch", "seq"), None), P(("batch", "head"), None, None)),
        check_vma=False,
    )
```

```python
import functools
import math

import jax
import jax.numpy as jnp
from jax import lax
from jax.experimental import pallas as pl
from jax.experimental.pallas import tpu as pltpu
from jax.sharding import PartitionSpec as P

GROUP = 64
RANK = 64
RING = 4
STEPS = 4
F32 = jnp.float32
BF16 = jnp.bfloat16
HIGHEST = lax.Precision.HIGHEST

SINE = [(-1) ** n * (2.0 * math.pi) ** (2 * n + 1) / math.factorial(2 * n + 1) for n in range(7)]


def split(x):
    high = x.astype(BF16)
    low = (x - high.astype(F32)).astype(BF16)
    return high, low


def sine_of_cycles(u):
    r = u - jnp.floor(u + 0.5)
    r = jnp.where(r > 0.25, 0.5 - r, jnp.where(r < -0.25, -0.5 - r, r))
    t = r * r
    p = jnp.full_like(t, SINE[-1])
    for c in SINE[-2::-1]:
        p = p * t + c
    return r * p


def dot(a, b, contract):
    return lax.dot_general(
        a, b, ((contract[:1], contract[1:]), ((), ())), precision=HIGHEST, preferred_element_type=F32
    )


def three_products(x, w):
    xh, xl = split(x)
    wh, wl = split(w)
    return jnp.dot(
        jnp.concatenate([xh, xl, xh], axis=1),
        jnp.concatenate([wh, wh, wl], axis=0),
        preferred_element_type=F32,
    )


def residual(kv, keep):
    tokens, cols = kv.shape
    grouped = kv.reshape(tokens // GROUP, GROUP, cols)
    step = jnp.max(jnp.abs(grouped), axis=1, keepdims=True) / 7.0 + 1e-06
    s = sine_of_cycles(grouped * (1.0 / step)) * keep[:, None, :]
    return s.reshape(tokens, cols)


def accumulate_kernel(shapes, first, *refs):
    refs = list(refs[1:])
    out_ref = refs.pop()
    if not first:
        base_ref = refs.pop()

    @pl.when(pl.program_id(0) == 0)
    def _():
        out_ref[...] = jnp.zeros_like(out_ref) if first else base_ref[...]

    total = None
    for parts in shapes:
        xs, refs = refs[:parts], refs[parts:]
        w_ref = refs.pop(0)
        x = xs[0][...] if parts == 1 else jnp.concatenate([r[...] for r in xs], axis=1)
        term = three_products(x, w_ref[...])
        total = term if total is None else total + term
    out_ref[...] += total


def block_specs(tokens, blocks):
    specs, at = [], 0
    for w, index, parts in blocks:
        rows = w.shape[0] // STEPS
        for i in range(parts):
            specs.append(
                pl.BlockSpec((tokens, rows // parts), lambda j, ix, a=at, n=parts, i=i: (0, ix[a + j * n + i]))
            )
        specs.append(pl.BlockSpec((rows, w.shape[1]), lambda j, ix: (j, 0)))
        at += STEPS * parts
    return specs, jnp.concatenate([index for _, index, _ in blocks])


def block_operands(hidden, blocks):
    return [x for w, _, parts in blocks for x in [hidden] * parts + [w]]


def cost(tokens, blocks):
    macs = sum(w.size for w, _, _ in blocks) * tokens
    return pl.CostEstimate(flops=6 * macs, bytes_accessed=sum(4 * w.size for w, _, _ in blocks) + 4 * tokens * 4096, transcendentals=0)


def accumulate(name, hidden, total, blocks):
    tokens = hidden.shape[0]
    cols = blocks[0][0].shape[1]
    specs, index = block_specs(tokens, blocks)
    whole = pl.BlockSpec((tokens, cols), lambda j, ix: (0, 0))
    return pl.pallas_call(
        functools.partial(accumulate_kernel, [parts for _, _, parts in blocks], total is None),
        grid_spec=pltpu.PrefetchScalarGridSpec(
            num_scalar_prefetch=1,
            grid=(STEPS,),
            in_specs=specs + ([] if total is None else [whole]),
            out_specs=whole,
        ),
        out_shape=jax.ShapeDtypeStruct((tokens, cols), F32),
        compiler_params=pltpu.CompilerParams(vmem_limit_bytes=32 << 20, dimension_semantics=("arbitrary",)),
        name=name,
        cost_estimate=cost(tokens, blocks),
    )(index, *block_operands(hidden, blocks), *([] if total is None else [total]))


def project_kernel(index_ref, xa, wa, xb, wb, xc0, xc1, xc2, xc3, wc, ab_ref, d_ref, c_ref, scale_ref, keep_ref,
                   high_ref, low_ref, gram_ref, ab_acc, c_acc):
    step = pl.program_id(0)

    @pl.when(step == 0)
    def _():
        ab_acc[...] = ab_ref[...]
        c_acc[...] = c_ref[...]

    ab_acc[...] += three_products(xa[...], wa[...]) + three_products(xb[...], wb[...])
    c_acc[...] += three_products(jnp.concatenate([xc0[...], xc1[...], xc2[...], xc3[...]], axis=1), wc[...])

    @pl.when(step == STEPS - 1)
    def _():
        at = 0
        for part in (ab_acc, d_ref, c_acc):
            for p in range(part.shape[1] // 128):
                cols = slice(at, at + 128)
                r = residual(part[:, 128 * p : 128 * p + 128] * scale_ref[...], keep_ref[:, cols])
                rh, rl = split(r)
                high_ref[:, cols] = rh
                low_ref[:, cols] = rl
                gram_ref[cols, :] = lax.dot_general(
                    jnp.concatenate([rh, rh, rl], axis=0),
                    jnp.concatenate([rh, rl, rh], axis=0),
                    (((0,), (0,)), ((), ())),
                    preferred_element_type=F32,
                )
                at += 128


def inverse_factors(grams):
    n = len(grams)
    lane = lax.broadcasted_iota(jnp.int32, (RANK, 128), 1)
    row = lax.broadcasted_iota(jnp.int32, (RANK, 128), 0)
    unit = jnp.where(lane - RANK == row, 1.0, 0.0).astype(F32)
    full = jnp.stack([jnp.where(lane < RANK, g, unit) for g in grams])
    blocks = [full[:, 8 * i : 8 * i + 8, :] for i in range(RANK // 8)]
    sub = lax.broadcasted_iota(jnp.int32, (n, 8, 1), 1)
    for j in range(RANK):
        jb, js = divmod(j, 8)
        pivot_row = blocks[jb][:, js : js + 1, :]
        scaled = pivot_row * (1.0 / pivot_row[:, :, j : j + 1])
        for i in range(jb, RANK // 8):
            column = blocks[i][:, :, j : j + 1]
            if i == jb:
                column = jnp.where(sub > js, column, 0.0)
            blocks[i] = blocks[i] - column * scaled
    full = jnp.concatenate(blocks, axis=1)
    out = []
    for p in range(n):
        a = full[p]
        pivots = jnp.sum(jnp.where(lane == row, a, 0.0), axis=1, keepdims=True)
        out.append(jnp.where(lane < RANK, 0.0, a) * lax.rsqrt(pivots))
    return out


def basis_start_kernel(sign_ref, out_ref):
    pairs = sign_ref.shape[0]
    inverses = inverse_factors([dot(sign_ref[p], sign_ref[p], (0, 0))[:RANK] for p in range(pairs)])
    for p in range(pairs):
        out_ref[p] = dot(sign_ref[p], jnp.concatenate([inverses[p]] * 2, axis=0), (1, 1))


def factor_kernel(root_length, gram_ref, start_ref, high_ref, low_ref, left_ref, right_ref):
    pairs = start_ref.shape[0]
    eye = lax.broadcasted_iota(jnp.int32, (128, 128), 0) == lax.broadcasted_iota(jnp.int32, (128, 128), 1)
    scales, ys, zs, grams = [], [], [], []
    for p in range(pairs):
        g = gram_ref[128 * p : 128 * p + 128, :]
        size = jnp.sum(jnp.sum(jnp.where(eye, g, 0.0), axis=1, keepdims=True), axis=0, keepdims=True) / 128.0
        g = g * (1.0 / size)
        y = dot(g, start_ref[p], (1, 0))
        z = dot(g, y, (1, 0))
        scales.append(size)
        ys.append(y)
        zs.append(z)
        grams.append(dot(y, z, (0, 0))[:RANK])
    inverses = inverse_factors(grams)
    zero = jnp.zeros((RANK, 128), F32)
    for h in range(pairs // 2):
        tops, rights = [], None
        for e in range(2):
            p = 2 * h + e
            wide = jnp.concatenate([inverses[p], zero] if e == 0 else [zero, inverses[p]], axis=0)
            tops.append(dot(ys[p], wide, (1, 1)) * (lax.rsqrt(scales[p]) * root_length))
            part = dot(zs[p], wide, (1, 1)) * (jnp.sqrt(scales[p]) * (1.0 / root_length))
            rights = part if rights is None else rights + part
        right_ref[h] = rights
        th, tl = split(jnp.concatenate(tops, axis=0))
        cols = slice(256 * h, 256 * h + 256)
        rh = high_ref[:, cols]
        rl = low_ref[:, cols]
        left_ref[h] = jnp.dot(
            jnp.concatenate([rh, rl, rh], axis=1),
            jnp.concatenate([th, th, tl], axis=0),
            preferred_element_type=F32,
        ).astype(BF16)


def partner(v, head, which):
    near, far = v ^ 1, 3 - v
    return jnp.where(head == which, near, far)


def around(v, head):
    second = partner(v, head, 1)
    return [v, partner(v, head, 0), second, partner(second, head, 0)]


def flat_partner(v, head, which):
    return (v ^ 1) if head == which else 3 - v


def plane_pairs(axis, which):
    pairs = []
    for h in range(2):
        for x in range(RING):
            for y in range(RING):
                tx, ty = (flat_partner(x, h, which), y) if axis == "x" else (x, flat_partner(y, h, which))
                pairs.append(((h * RING + x) * RING + y, (h * RING + tx) * RING + ty))
    return pairs


def depth_pairs(which):
    return [(z * 2 + h, flat_partner(z, h, which) * 2 + h) for z in range(RING) for h in range(2)]


def gather_weight(weight, extra):
    state = {"last": ()}

    def send(v, axis, which):
        if state["last"]:
            v = lax.optimization_barrier((v,) + state["last"])[0]
        if axis == "z":
            return lax.ppermute(v, ("batch", "head"), depth_pairs(which))
        return lax.ppermute(v, ("head", "seq"), plane_pairs(axis, which))

    def arrived(*values):
        values = lax.optimization_barrier(values)
        state["last"] = values
        return values

    join = lambda a, b: jnp.concatenate([a, b], axis=0)
    half = weight.shape[0] // 2
    quarter = weight.shape[0] // RING
    own = lax.dynamic_slice_in_dim(weight[:, 640:], lax.axis_index("batch") * quarter, quarter, 0)
    d, c = own[:, :128], own[:, 128:]
    a, b = weight[:half, :640], weight[half:, :640]

    c1, d1 = send(c, "x", 0), send(d, "y", 0)
    a1, b1 = send(a, "x", 0), send(b, "y", 0)
    c1, d1 = arrived(c1, d1)
    c, d = join(c, c1), join(d, d1)
    c1, d1 = send(c, "x", 1), send(d, "y", 1)
    c1, d1 = arrived(c1, d1)
    c, d = join(c, c1), join(d, d1)
    c1, d1 = send(c, "y", 0), send(d, "x", 0)
    a1, b1 = arrived(a1, b1)
    a, b = join(a, a1), join(b, b1)
    a1, b1 = send(a, "x", 1), send(b, "y", 1)
    c1, d1 = arrived(c1, d1)
    c, d = join(c, c1), join(d, d1)
    c1, d1 = send(c, "y", 1), send(d, "x", 1)
    (d1,) = arrived(d1)
    d = join(d, d1)
    ds, cs = [d], []
    z1 = send(d, "z", 0)
    c1, a1, b1 = arrived(c1, a1, b1)
    c, a, b = join(c, c1), join(a, a1), join(b, b1)
    cs, as_, bs = [c], [a], [b]
    ya, xb = send(a, "y", 0), send(b, "x", 0)
    (z1,) = arrived(z1)
    ds.append(z1)
    z1 = send(d, "z", 1)
    (z1, extra) = arrived(z1, extra)
    ds.append(z1)
    z1 = send(ds[1], "z", 1)
    ya, xb = arrived(ya, xb)
    as_.append(ya)
    bs.append(xb)
    ya, xb = send(a, "y", 1), send(b, "x", 1)
    (z1,) = arrived(z1)
    ds.append(z1)
    z1 = send(c, "z", 0)
    (z1,) = arrived(z1)
    cs.append(z1)
    z1 = send(c, "z", 1)
    ya, xb = arrived(ya, xb)
    as_.append(ya)
    bs.append(xb)
    ya, xb = send(as_[1], "y", 1), send(bs[1], "x", 1)
    (z1,) = arrived(z1)
    cs.append(z1)
    z1 = send(cs[1], "z", 1)
    ya, xb, z1 = arrived(ya, xb, z1)
    as_.append(ya)
    bs.append(xb)
    cs.append(z1)
    return as_, bs, cs, ds, extra


def shards(hidden, row_scale, key_value_weight, outlier, sketch_sign_flags):
    tokens, width = hidden.shape
    rows, heads, kv_cols = key_value_weight.shape
    cols = heads * kv_cols
    pairs = 2 * heads
    groups = outlier.shape[0]
    seq = lax.axis_size("seq")
    root_length = math.sqrt(tokens * seq)

    signs = (2 * sketch_sign_flags - 1).astype(F32).reshape(pairs, 128, RANK)
    start = pl.pallas_call(
        basis_start_kernel,
        out_shape=jax.ShapeDtypeStruct((pairs, 128, 128), F32),
        name="start",
        cost_estimate=pl.CostEstimate(flops=10**8, bytes_accessed=10**6, transcendentals=0),
    )(jnp.concatenate([signs, signs], axis=2))

    as_, bs, cs, ds, start = gather_weight(key_value_weight.reshape(rows, cols), start)

    head, place, plane = lax.axis_index("head"), lax.axis_index("seq"), lax.axis_index("batch")
    xs, ys, zs = around(place // RING, head), around(place % RING, head), around(plane, head)
    shard = lambda x, y: x * RING + y
    a_blocks = [(as_[k], jnp.stack([2 * shard(x, ys[k]) for x in xs]), 1) for k in range(RING)]
    b_blocks = [(bs[k], jnp.stack([2 * shard(xs[k], y) + 1 for y in ys]), 1) for k in range(RING)]
    c_blocks = [(cs[k], jnp.stack([4 * shard(x, y) + zs[k] for y in ys for x in xs]), 4) for k in range(RING)]
    d_blocks = [(ds[k], jnp.stack([4 * shard(x, y) + zs[k] for x in xs for y in ys]), 4) for k in range(RING)]

    ab = accumulate("ab0", hidden, None, [a_blocks[0], b_blocks[0]])
    d = accumulate("d0", hidden, None, d_blocks[:2])
    c = accumulate("c0", hidden, None, c_blocks[:1])
    ab = accumulate("ab1", hidden, ab, [a_blocks[1], b_blocks[1]])
    d = accumulate("d1", hidden, d, d_blocks[2:])
    c = accumulate("c1", hidden, c, c_blocks[1:3])
    ab = accumulate("ab2", hidden, ab, [a_blocks[2], b_blocks[2]])

    last = [a_blocks[3], b_blocks[3], c_blocks[3]]
    specs, index = block_specs(tokens, last)
    keep = jnp.repeat((1 - outlier).astype(F32), kv_cols, axis=1)
    whole = lambda *shape: pl.BlockSpec(shape, lambda j, ix: (0,) * len(shape))
    high, low, gram = pl.pallas_call(
        project_kernel,
        grid_spec=pltpu.PrefetchScalarGridSpec(
            num_scalar_prefetch=1,
            grid=(STEPS,),
            in_specs=specs
            + [whole(tokens, t.shape[1]) for t in (ab, d, c)]
            + [whole(tokens, 1), whole(groups, cols)],
            out_specs=[whole(tokens, cols), whole(tokens, cols), whole(128 * pairs, 128)],
            scratch_shapes=[pltpu.VMEM(ab.shape, F32), pltpu.VMEM(c.shape, F32)],
        ),
        out_shape=[
            jax.ShapeDtypeStruct((tokens, cols), BF16),
            jax.ShapeDtypeStruct((tokens, cols), BF16),
            jax.ShapeDtypeStruct((128 * pairs, 128), F32),
        ],
        compiler_params=pltpu.CompilerParams(vmem_limit_bytes=40 << 20, dimension_semantics=("arbitrary",)),
        name="project",
        cost_estimate=cost(tokens, last),
    )(index, *block_operands(hidden, last), ab, d, c, row_scale[:, None], keep)

    pieces = lax.all_to_all(gram, "seq", 0, 0, tiled=True)
    piece = jnp.sum(pieces.reshape(seq, 128 * pairs // seq, 128), axis=0)
    gram = lax.all_to_all(jnp.broadcast_to(piece, (seq,) + piece.shape), "seq", 0, 0).reshape(128 * pairs, 128)

    return pl.pallas_call(
        functools.partial(factor_kernel, root_length),
        out_shape=[
            jax.ShapeDtypeStruct((heads, tokens, 2 * RANK), BF16),
            jax.ShapeDtypeStruct((heads, 128, 2 * RANK), F32),
        ],
        compiler_params=pltpu.CompilerParams(vmem_limit_bytes=40 << 20),
        name="factor",
        cost_estimate=pl.CostEstimate(flops=10**9, bytes_accessed=4 << 20, transcendentals=0),
    )(gram, start, high, low)


def solution(mesh):
    return jax.shard_map(
        shards,
        mesh=mesh,
        in_specs=(
            P(("batch", "seq"), None),
            P(("batch", "seq")),
            P("seq", "head", None),
            P(("batch", "seq"), "head"),
            P("head", None, None, None),
        ),
        out_specs=(P("head", ("batch", "seq"), None), P(("batch", "head"), None, None)),
        check_vma=False,
    )
```

```python
import functools
import math

import jax
import jax.numpy as jnp
from jax import lax
from jax.experimental import pallas as pl
from jax.experimental.pallas import tpu as pltpu
from jax.sharding import PartitionSpec as P

GROUP = 64
RANK = 64
RING = 4
STEPS = 4
PERMUTED = 512
VMEM_LIMIT = 56 << 20
F32 = jnp.float32
BF16 = jnp.bfloat16
HIGHEST = lax.Precision.HIGHEST

SINE = [(-1) ** n * (2.0 * math.pi) ** (2 * n + 1) / math.factorial(2 * n + 1) for n in range(7)]


def split(x):
    high = x.astype(BF16)
    low = (x - high.astype(F32)).astype(BF16)
    return high, low


def sine_of_cycles(u):
    r = u - jnp.floor(u + 0.5)
    r = jnp.where(r > 0.25, 0.5 - r, jnp.where(r < -0.25, -0.5 - r, r))
    t = r * r
    p = jnp.full_like(t, SINE[-1])
    for c in SINE[-2::-1]:
        p = p * t + c
    return r * p


def dot(a, b, contract):
    return lax.dot_general(
        a, b, ((contract[:1], contract[1:]), ((), ())), precision=HIGHEST, preferred_element_type=F32
    )


def three_products(x, w):
    xh, xl = split(x)
    wh, wl = split(w)
    return jnp.dot(
        jnp.concatenate([xh, xl, xh], axis=1),
        jnp.concatenate([wh, wh, wl], axis=0),
        preferred_element_type=F32,
    )


def residual(kv, keep):
    tokens, cols = kv.shape
    grouped = kv.reshape(tokens // GROUP, GROUP, cols)
    step = jnp.max(jnp.abs(grouped), axis=1, keepdims=True) / 7.0 + 1e-06
    s = sine_of_cycles(grouped * (1.0 / step)) * keep[:, None, :]
    return s.reshape(tokens, cols)


def accumulate_kernel(shapes, first, *refs):
    refs = list(refs[1:])
    out_ref = refs.pop()
    if not first:
        base_ref = refs.pop()

    @pl.when(pl.program_id(0) == 0)
    def _():
        out_ref[...] = jnp.zeros_like(out_ref) if first else base_ref[...]

    total = None
    for parts in shapes:
        xs, refs = refs[:parts], refs[parts:]
        w_ref = refs.pop(0)
        x = xs[0][...] if parts == 1 else jnp.concatenate([r[...] for r in xs], axis=1)
        term = three_products(x, w_ref[...])
        total = term if total is None else total + term
    out_ref[...] += total


def block_specs(tokens, blocks):
    specs, at = [], 0
    for w, index, parts in blocks:
        rows = w.shape[0] // STEPS
        for i in range(parts):
            specs.append(
                pl.BlockSpec((tokens, rows // parts), lambda j, ix, a=at, n=parts, i=i: (0, ix[a + j * n + i]))
            )
        specs.append(pl.BlockSpec((rows, w.shape[1]), lambda j, ix: (j, 0)))
        at += STEPS * parts
    return specs, jnp.concatenate([index for _, index, _ in blocks])


def block_operands(hidden, blocks):
    return [x for w, _, parts in blocks for x in [hidden] * parts + [w]]


def cost(tokens, blocks):
    macs = sum(w.size for w, _, _ in blocks) * tokens
    return pl.CostEstimate(flops=6 * macs, bytes_accessed=sum(4 * w.size for w, _, _ in blocks) + 4 * tokens * 4096, transcendentals=0)


def accumulate(name, hidden, total, blocks):
    tokens = hidden.shape[0]
    cols = blocks[0][0].shape[1]
    specs, index = block_specs(tokens, blocks)
    whole = pl.BlockSpec((tokens, cols), lambda j, ix: (0, 0))
    return pl.pallas_call(
        functools.partial(accumulate_kernel, [parts for _, _, parts in blocks], total is None),
        grid_spec=pltpu.PrefetchScalarGridSpec(
            num_scalar_prefetch=1,
            grid=(STEPS,),
            in_specs=specs + ([] if total is None else [whole]),
            out_specs=whole,
        ),
        out_shape=jax.ShapeDtypeStruct((tokens, cols), F32),
        compiler_params=pltpu.CompilerParams(vmem_limit_bytes=VMEM_LIMIT, dimension_semantics=("arbitrary",)),
        name=name,
        cost_estimate=cost(tokens, blocks),
    )(index, *block_operands(hidden, blocks), *([] if total is None else [total]))


def accumulate_all_kernel(x_ref, w_ref, out_ref):
    @pl.when(pl.program_id(0) == 0)
    def _():
        out_ref[...] = jnp.zeros_like(out_ref)

    rows = w_ref.shape[0] * w_ref.shape[2]
    out_ref[...] += three_products(x_ref[...], w_ref[...].reshape(rows, w_ref.shape[3]))


def accumulate_all(hidden, weight):
    tokens = hidden.shape[0]
    batch, seq, quarter, cols = weight.shape
    return pl.pallas_call(
        accumulate_all_kernel,
        grid=(seq,),
        in_specs=[
            pl.BlockSpec((tokens, batch * quarter), lambda k: (0, k)),
            pl.BlockSpec((batch, 1, quarter, cols), lambda k: (0, k, 0, 0)),
        ],
        out_specs=pl.BlockSpec((tokens, cols), lambda k: (0, 0)),
        out_shape=jax.ShapeDtypeStruct((tokens, cols), F32),
        compiler_params=pltpu.CompilerParams(vmem_limit_bytes=VMEM_LIMIT, dimension_semantics=("arbitrary",)),
        name="cd",
        cost_estimate=pl.CostEstimate(
            flops=6 * tokens * weight.size, bytes_accessed=4 * (weight.size + hidden.size), transcendentals=0
        ),
    )(hidden, weight)


def project_kernel(index_ref, xa, wa, xb, wb, ab_ref, cd_ref, scale_ref, keep_ref, high_ref, low_ref, gram_ref, ab_acc):
    step = pl.program_id(0)

    @pl.when(step == 0)
    def _():
        ab_acc[...] = ab_ref[...]

    ab_acc[...] += three_products(xa[...], wa[...]) + three_products(xb[...], wb[...])

    @pl.when(step == STEPS - 1)
    def _():
        at = 0
        for part in (ab_acc, cd_ref):
            for p in range(part.shape[1] // 128):
                cols = slice(at, at + 128)
                r = residual(part[:, 128 * p : 128 * p + 128] * scale_ref[...], keep_ref[:, cols])
                rh, rl = split(r)
                high_ref[:, cols] = rh
                low_ref[:, cols] = rl
                both = lax.dot_general(
                    rh,
                    jnp.concatenate([rh, rl], axis=1),
                    (((0,), (0,)), ((), ())),
                    preferred_element_type=F32,
                )
                cross = both[:, 128:]
                gram_ref[cols, :] = both[:, :128] + (cross + cross.T)
                at += 128


def inverse_factors(grams):
    n = len(grams)
    lane = lax.broadcasted_iota(jnp.int32, (RANK, 128), 1)
    row = lax.broadcasted_iota(jnp.int32, (RANK, 128), 0)
    unit = jnp.where(lane - RANK == row, 1.0, 0.0).astype(F32)
    full = jnp.stack([jnp.where(lane < RANK, g, unit) for g in grams])
    blocks = [full[:, 8 * i : 8 * i + 8, :] for i in range(RANK // 8)]
    sub = lax.broadcasted_iota(jnp.int32, (n, 8, 1), 1)
    for j in range(RANK):
        jb, js = divmod(j, 8)
        pivot_row = blocks[jb][:, js : js + 1, :]
        scaled = pivot_row * (1.0 / pivot_row[:, :, j : j + 1])
        for i in range(jb, RANK // 8):
            column = blocks[i][:, :, j : j + 1]
            if i == jb:
                column = jnp.where(sub > js, column, 0.0)
            blocks[i] = blocks[i] - column * scaled
    full = jnp.concatenate(blocks, axis=1)
    out = []
    for p in range(n):
        a = full[p]
        pivots = jnp.sum(jnp.where(lane == row, a, 0.0), axis=1, keepdims=True)
        out.append(jnp.where(lane < RANK, 0.0, a) * lax.rsqrt(pivots))
    return out


def basis_start_kernel(sign_ref, out_ref):
    pairs = sign_ref.shape[0]
    inverses = inverse_factors([dot(sign_ref[p], sign_ref[p], (0, 0))[:RANK] for p in range(pairs)])
    for p in range(pairs):
        out_ref[p] = dot(sign_ref[p], jnp.concatenate([inverses[p]] * 2, axis=0), (1, 1))


def factor_kernel(root_length, gram_ref, start_ref, high_ref, low_ref, left_ref, right_ref):
    pairs = start_ref.shape[0]
    eye = lax.broadcasted_iota(jnp.int32, (128, 128), 0) == lax.broadcasted_iota(jnp.int32, (128, 128), 1)
    scales, ys, zs, grams = [], [], [], []
    for p in range(pairs):
        g = gram_ref[128 * p : 128 * p + 128, :]
        size = jnp.sum(jnp.sum(jnp.where(eye, g, 0.0), axis=1, keepdims=True), axis=0, keepdims=True) / 128.0
        g = g * (1.0 / size)
        y = dot(g, start_ref[p], (1, 0))
        z = dot(g, y, (1, 0))
        scales.append(size)
        ys.append(y)
        zs.append(z)
        grams.append(dot(y, z, (0, 0))[:RANK])
    inverses = inverse_factors(grams)
    zero = jnp.zeros((RANK, 128), F32)
    for h in range(pairs // 2):
        tops, rights = [], None
        for e in range(2):
            p = 2 * h + e
            wide = jnp.concatenate([inverses[p], zero] if e == 0 else [zero, inverses[p]], axis=0)
            tops.append(dot(ys[p], wide, (1, 1)) * (lax.rsqrt(scales[p]) * root_length))
            part = dot(zs[p], wide, (1, 1)) * (jnp.sqrt(scales[p]) * (1.0 / root_length))
            rights = part if rights is None else rights + part
        right_ref[h] = rights
        th, tl = split(jnp.concatenate(tops, axis=0))
        cols = slice(256 * h, 256 * h + 256)
        rh = high_ref[:, cols]
        rl = low_ref[:, cols]
        left_ref[h] = jnp.dot(
            jnp.concatenate([rh, rl, rh], axis=1),
            jnp.concatenate([th, th, tl], axis=0),
            preferred_element_type=F32,
        ).astype(BF16)


def partner(v, head, which):
    near, far = v ^ 1, 3 - v
    return jnp.where(head == which, near, far)


def around(v, head):
    second = partner(v, head, 1)
    return [v, partner(v, head, 0), second, partner(second, head, 0)]


def flat_partner(v, head, which):
    return (v ^ 1) if head == which else 3 - v


def plane_pairs(axis, which):
    pairs = []
    for h in range(2):
        for x in range(RING):
            for y in range(RING):
                tx, ty = (flat_partner(x, h, which), y) if axis == "x" else (x, flat_partner(y, h, which))
                pairs.append(((h * RING + x) * RING + y, (h * RING + tx) * RING + ty))
    return pairs


def gather_blocks(weight, multiply, start):
    def send(v, axis, which):
        return lax.ppermute(v, ("head", "seq"), plane_pairs(axis, which))

    join = lambda a, b: jnp.concatenate([a, b], axis=0)
    half = weight.shape[0] // 2
    a, b = weight[:half], weight[half:]
    for which in range(2):
        a, b = lax.optimization_barrier((a, b))
        a1, b1 = lax.optimization_barrier((send(a, "x", which), send(b, "y", which)))
        a, b = join(a, a1), join(b, b1)
    a, b = lax.optimization_barrier((a, b))
    a1, b1, a2, b2 = send(a, "y", 0), send(b, "x", 0), send(a, "y", 1), send(b, "x", 1)
    total = multiply(None, [(a, b, 0)])
    a1, b1, a2, b2, total, start = lax.optimization_barrier((a1, b1, a2, b2, total, start))
    a3, b3 = send(a1, "y", 1), send(b1, "x", 1)
    total = multiply(total, [(a1, b1, 1), (a2, b2, 2)])
    return a3, b3, total, start


def shards(hidden, row_scale, key_value_weight, outlier, sketch_sign_flags):
    tokens, width = hidden.shape
    rows, heads, kv_cols = key_value_weight.shape
    cols = heads * kv_cols
    pairs = 2 * heads
    groups = outlier.shape[0]
    seq = lax.axis_size("seq")
    root_length = math.sqrt(tokens * seq)

    signs = (2 * sketch_sign_flags - 1).astype(F32).reshape(pairs, 128, RANK)
    start = pl.pallas_call(
        basis_start_kernel,
        out_shape=jax.ShapeDtypeStruct((pairs, 128, 128), F32),
        name="start",
        cost_estimate=pl.CostEstimate(flops=10**8, bytes_accessed=10**6, transcendentals=0),
    )(jnp.concatenate([signs, signs], axis=2))

    head, place, plane = lax.axis_index("head"), lax.axis_index("seq"), lax.axis_index("batch")
    xs, ys = around(place // RING, head), around(place % RING, head)
    shard = lambda x, y: x * RING + y

    def blocks_of(a, b, k):
        return [
            (a, jnp.stack([2 * shard(x, ys[k]) for x in xs]), 1),
            (b, jnp.stack([2 * shard(xs[k], y) + 1 for y in ys]), 1),
        ]

    def multiply(total, arrivals):
        name = "ab0" if total is None else "ab1"
        return accumulate(name, hidden, total, [block for arrival in arrivals for block in blocks_of(*arrival)])

    flat = key_value_weight.reshape(rows, cols)
    quarter = rows // RING
    own = lax.dynamic_slice_in_dim(flat[:, PERMUTED:], plane * quarter, quarter, 0)
    rest = lax.all_gather(own, ("batch", "seq"), axis=0).reshape(RING, seq, quarter, cols - PERMUTED)
    a3, b3, ab, start = gather_blocks(flat[:, :PERMUTED], multiply, start)
    rest, ab = lax.optimization_barrier((rest, ab))
    cd = accumulate_all(hidden, rest)

    last = blocks_of(a3, b3, 3)
    specs, index = block_specs(tokens, last)
    keep = jnp.repeat((1 - outlier).astype(F32), kv_cols, axis=1)
    whole = lambda *shape: pl.BlockSpec(shape, lambda j, ix: (0,) * len(shape))
    high, low, gram = pl.pallas_call(
        project_kernel,
        grid_spec=pltpu.PrefetchScalarGridSpec(
            num_scalar_prefetch=1,
            grid=(STEPS,),
            in_specs=specs
            + [whole(tokens, t.shape[1]) for t in (ab, cd)]
            + [whole(tokens, 1), whole(groups, cols)],
            out_specs=[whole(tokens, cols), whole(tokens, cols), whole(128 * pairs, 128)],
            scratch_shapes=[pltpu.VMEM(ab.shape, F32)],
        ),
        out_shape=[
            jax.ShapeDtypeStruct((tokens, cols), BF16),
            jax.ShapeDtypeStruct((tokens, cols), BF16),
            jax.ShapeDtypeStruct((128 * pairs, 128), F32),
        ],
        compiler_params=pltpu.CompilerParams(vmem_limit_bytes=VMEM_LIMIT, dimension_semantics=("arbitrary",)),
        name="project",
        cost_estimate=cost(tokens, last),
    )(index, *block_operands(hidden, last), ab, cd, row_scale[:, None], keep)

    pieces = lax.all_to_all(gram, "seq", 0, 0, tiled=True)
    piece = jnp.sum(pieces.reshape(seq, 128 * pairs // seq, 128), axis=0)
    gram = lax.all_to_all(jnp.broadcast_to(piece, (seq,) + piece.shape), "seq", 0, 0).reshape(128 * pairs, 128)

    return pl.pallas_call(
        functools.partial(factor_kernel, root_length),
        out_shape=[
            jax.ShapeDtypeStruct((heads, tokens, 2 * RANK), BF16),
            jax.ShapeDtypeStruct((heads, 128, 2 * RANK), F32),
        ],
        compiler_params=pltpu.CompilerParams(vmem_limit_bytes=40 << 20),
        name="factor",
        cost_estimate=pl.CostEstimate(flops=10**9, bytes_accessed=4 << 20, transcendentals=0),
    )(gram, start, high, low)


def solution(mesh):
    return jax.shard_map(
        shards,
        mesh=mesh,
        in_specs=(
            P(("batch", "seq"), None),
            P(("batch", "seq")),
            P("seq", "head", None),
            P(("batch", "seq"), "head"),
            P("head", None, None, None),
        ),
        out_specs=(P("head", ("batch", "seq"), None), P(("batch", "head"), None, None)),
        check_vma=False,
    )
```

```python
import functools
import math

import jax
import jax.numpy as jnp
from jax import lax
from jax.experimental import pallas as pl
from jax.experimental.pallas import tpu as pltpu
from jax.sharding import PartitionSpec as P

GROUP = 64
RANK = 64
RING = 4
STEPS = 4
PART = 256
WIDE = 256
UNROLL = 4
ORDERS = ("xyz", "yzx", "xzy")
VMEM_LIMIT = 56 << 20
F32 = jnp.float32
BF16 = jnp.bfloat16
HIGHEST = lax.Precision.HIGHEST

SINE = [(-1) ** n * (2.0 * math.pi) ** (2 * n + 1) / math.factorial(2 * n + 1) for n in range(7)]


def split(x):
    high = x.astype(BF16)
    low = (x - high.astype(F32)).astype(BF16)
    return high, low


def sine_of_cycles(u):
    r = u - jnp.floor(u + 0.5)
    r = jnp.where(r > 0.25, 0.5 - r, jnp.where(r < -0.25, -0.5 - r, r))
    t = r * r
    p = jnp.full_like(t, SINE[-1])
    for c in SINE[-2::-1]:
        p = p * t + c
    return r * p


def dot(a, b, contract):
    return lax.dot_general(
        a, b, ((contract[:1], contract[1:]), ((), ())), precision=HIGHEST, preferred_element_type=F32
    )


def three_products(x, w):
    xh, xl = split(x)
    wh, wl = split(w)
    return jnp.dot(
        jnp.concatenate([xh, xl, xh], axis=1),
        jnp.concatenate([wh, wh, wl], axis=0),
        preferred_element_type=F32,
    )


def residual(kv, keep):
    step = jnp.max(jnp.abs(kv), axis=0, keepdims=True) / 7.0 + 1e-06
    return sine_of_cycles(kv * (1.0 / step)) * keep


def accumulate_kernel(parts, first, *refs):
    refs = list(refs[1:])
    out_ref = refs.pop()
    if not first:
        base_ref = refs.pop()

    @pl.when(pl.program_id(0) == 0)
    def _():
        out_ref[...] = jnp.zeros_like(out_ref) if first else base_ref[...]

    add_blocks(parts, refs, out_ref)


def add_blocks(parts, refs, total_ref):
    terms = {}
    for i, part in enumerate(parts):
        xs, w_ref = refs[5 * i : 5 * i + 4], refs[5 * i + 4]
        term = three_products(jnp.concatenate([r[...] for r in xs], axis=1), w_ref[...])
        terms[part] = terms[part] + term if part in terms else term
    for part, term in terms.items():
        cols = term.shape[1]
        total_ref[:, part * cols : part * cols + cols] += term


def block_specs(tokens, blocks):
    specs = []
    for b, (_, w, index) in enumerate(blocks):
        rows = w.shape[0] // STEPS
        for i in range(4):
            specs.append(pl.BlockSpec((tokens, rows // 4), lambda j, ix, a=b * 4 * STEPS + i: (0, ix[a + 4 * j])))
        specs.append(pl.BlockSpec((rows, w.shape[1]), lambda j, ix: (j, 0)))
    return specs, jnp.concatenate([index for _, _, index in blocks])


def block_operands(hidden, blocks):
    return [x for _, w, _ in blocks for x in [hidden] * 4 + [w]]


def cost(tokens, blocks):
    macs = sum(w.size for _, w, _ in blocks) * tokens
    return pl.CostEstimate(
        flops=6 * macs, bytes_accessed=sum(4 * w.size + 4 * tokens * w.shape[0] for _, w, _ in blocks), transcendentals=0
    )


def accumulate(name, hidden, total, cols, blocks):
    tokens = hidden.shape[0]
    specs, index = block_specs(tokens, blocks)
    whole = pl.BlockSpec((tokens, cols), lambda j, ix: (0, 0))
    return pl.pallas_call(
        functools.partial(accumulate_kernel, [part for part, _, _ in blocks], total is None),
        grid_spec=pltpu.PrefetchScalarGridSpec(
            num_scalar_prefetch=1,
            grid=(STEPS,),
            in_specs=specs + ([] if total is None else [whole]),
            out_specs=whole,
        ),
        out_shape=jax.ShapeDtypeStruct((tokens, cols), F32),
        compiler_params=pltpu.CompilerParams(vmem_limit_bytes=VMEM_LIMIT, dimension_semantics=("arbitrary",)),
        name=name,
        cost_estimate=cost(tokens, blocks),
    )(index, *block_operands(hidden, blocks), *([] if total is None else [total]))


def accumulate_all_kernel(x_ref, w_ref, out_ref):
    @pl.when(pl.program_id(0) == 0)
    def _():
        out_ref[...] = jnp.zeros_like(out_ref)

    batch, shards_in, quarter, cols = w_ref.shape
    rows = batch * quarter
    for s in range(shards_in):
        out_ref[...] += three_products(x_ref[:, s * rows : s * rows + rows], w_ref[:, s].reshape(rows, cols))


def accumulate_all(hidden, weight):
    tokens = hidden.shape[0]
    batch, seq, quarter, cols = weight.shape
    return pl.pallas_call(
        accumulate_all_kernel,
        grid=(seq // 2,),
        in_specs=[
            pl.BlockSpec((tokens, 2 * batch * quarter), lambda k: (0, k)),
            pl.BlockSpec((batch, 2, quarter, cols), lambda k: (0, k, 0, 0)),
        ],
        out_specs=pl.BlockSpec((tokens, cols), lambda k: (0, 0)),
        out_shape=jax.ShapeDtypeStruct((tokens, cols), F32),
        compiler_params=pltpu.CompilerParams(vmem_limit_bytes=VMEM_LIMIT, dimension_semantics=("arbitrary",)),
        name="rest",
        cost_estimate=pl.CostEstimate(
            flops=6 * tokens * weight.size, bytes_accessed=4 * (weight.size + hidden.size), transcendentals=0
        ),
    )(hidden, weight)


def project_kernel(parts, *refs):
    refs = list(refs[1:])
    blocks, refs = refs[: 5 * len(parts)], refs[5 * len(parts) :]
    base_ref, rest_ref, scale_ref, keep_ref, high_ref, low_ref, gram_ref, total_ref = refs
    step = pl.program_id(0)

    @pl.when(step == 0)
    def _():
        total_ref[...] = base_ref[...]

    add_blocks(parts, blocks, total_ref)

    @pl.when(step == STEPS - 1)
    def _():
        epilogue(total_ref, rest_ref, scale_ref, keep_ref, high_ref, low_ref, gram_ref)


def epilogue(total_ref, rest_ref, scale_ref, keep_ref, high_ref, low_ref, gram_ref):
    tokens = total_ref.shape[0]
    at = 0
    for part in (total_ref, rest_ref):
        for first in range(0, part.shape[1], WIDE):
            here = slice(at, at + WIDE)

            @pl.loop(0, tokens // GROUP, unroll=UNROLL)
            def _(g, part=part, first=first, here=here):
                rows = pl.ds(pl.multiple_of(g * GROUP, GROUP), GROUP)
                kv = part[rows, first : first + WIDE] * scale_ref[rows, :]
                keep = keep_ref[pl.ds(pl.multiple_of(g * 8, 8), 8), here][:1]
                rh, rl = split(residual(kv, keep))
                high_ref[rows, here] = rh
                low_ref[rows, here] = rl

            for cols in [slice(c, c + 128) for c in range(at, at + WIDE, 128)]:
                rh = high_ref[:, cols]
                both = lax.dot_general(
                    rh,
                    jnp.concatenate([rh, low_ref[:, cols]], axis=1),
                    (((0,), (0,)), ((), ())),
                    preferred_element_type=F32,
                )
                cross = both[:, 128:]
                gram_ref[cols, :] = both[:, :128] + (cross + cross.T)
            at += WIDE


def inverse_factors(grams):
    n = len(grams)
    lane = lax.broadcasted_iota(jnp.int32, (RANK, 128), 1)
    row = lax.broadcasted_iota(jnp.int32, (RANK, 128), 0)
    unit = jnp.where(lane - RANK == row, 1.0, 0.0).astype(F32)
    full = jnp.stack([jnp.where(lane < RANK, g, unit) for g in grams])
    blocks = [full[:, 8 * i : 8 * i + 8, :] for i in range(RANK // 8)]
    sub = lax.broadcasted_iota(jnp.int32, (n, 8, 1), 1)
    for j in range(RANK):
        jb, js = divmod(j, 8)
        pivot_row = blocks[jb][:, js : js + 1, :]
        scaled = pivot_row * (1.0 / pivot_row[:, :, j : j + 1])
        for i in range(jb, RANK // 8):
            column = blocks[i][:, :, j : j + 1]
            if i == jb:
                column = jnp.where(sub > js, column, 0.0)
            blocks[i] = blocks[i] - column * scaled
    full = jnp.concatenate(blocks, axis=1)
    out = []
    for p in range(n):
        a = full[p]
        pivots = jnp.sum(jnp.where(lane == row, a, 0.0), axis=1, keepdims=True)
        out.append(jnp.where(lane < RANK, 0.0, a) * lax.rsqrt(pivots))
    return out


def basis_start_kernel(sign_ref, out_ref):
    pairs = sign_ref.shape[0]
    inverses = inverse_factors([dot(sign_ref[p], sign_ref[p], (0, 0))[:RANK] for p in range(pairs)])
    for p in range(pairs):
        out_ref[p] = dot(sign_ref[p], jnp.concatenate([inverses[p]] * 2, axis=0), (1, 1))


def factor_kernel(root_length, gram_ref, start_ref, high_ref, low_ref, left_ref, right_ref):
    pairs = start_ref.shape[0]
    eye = lax.broadcasted_iota(jnp.int32, (128, 128), 0) == lax.broadcasted_iota(jnp.int32, (128, 128), 1)
    scales, ys, zs, grams = [], [], [], []
    for p in range(pairs):
        g = gram_ref[128 * p : 128 * p + 128, :]
        size = jnp.sum(jnp.sum(jnp.where(eye, g, 0.0), axis=1, keepdims=True), axis=0, keepdims=True) / 128.0
        g = g * (1.0 / size)
        y = dot(g, start_ref[p], (1, 0))
        z = dot(g, y, (1, 0))
        scales.append(size)
        ys.append(y)
        zs.append(z)
        grams.append(dot(y, z, (0, 0))[:RANK])
    inverses = inverse_factors(grams)
    zero = jnp.zeros((RANK, 128), F32)
    for h in range(pairs // 2):
        tops, rights = [], None
        for e in range(2):
            p = 2 * h + e
            wide = jnp.concatenate([inverses[p], zero] if e == 0 else [zero, inverses[p]], axis=0)
            tops.append(dot(ys[p], wide, (1, 1)) * (lax.rsqrt(scales[p]) * root_length))
            part = dot(zs[p], wide, (1, 1)) * (jnp.sqrt(scales[p]) * (1.0 / root_length))
            rights = part if rights is None else rights + part
        right_ref[h] = rights
        th, tl = split(jnp.concatenate(tops, axis=0))
        cols = slice(256 * h, 256 * h + 256)
        rh = high_ref[:, cols]
        rl = low_ref[:, cols]
        left_ref[h] = jnp.dot(
            jnp.concatenate([rh, rl, rh], axis=1),
            jnp.concatenate([th, th, tl], axis=0),
            preferred_element_type=F32,
        ).astype(BF16)


def partner(v, head, which):
    near, far = v ^ 1, 3 - v
    return jnp.where(head == which, near, far)


def around(v, head):
    second = partner(v, head, 1)
    return [v, partner(v, head, 0), second, partner(second, head, 0)]


def flat_partner(v, head, which):
    return (v ^ 1) if head == which else 3 - v


def plane_pairs(axis, which):
    pairs = []
    for h in range(2):
        for x in range(RING):
            for y in range(RING):
                tx, ty = (flat_partner(x, h, which), y) if axis == "x" else (x, flat_partner(y, h, which))
                pairs.append(((h * RING + x) * RING + y, (h * RING + tx) * RING + ty))
    return pairs


def depth_pairs(which):
    return [(z * 2 + h, flat_partner(z, h, which) * 2 + h) for z in range(RING) for h in range(2)]


def send(v, axis, which):
    if axis == "z":
        return lax.ppermute(v, ("batch", "head"), depth_pairs(which))
    return lax.ppermute(v, ("head", "seq"), plane_pairs(axis, which))


def gather_blocks(parts, orders, multiply, start, rest):
    barrier = lambda values: list(lax.optimization_barrier(tuple(values)))
    both = range(len(parts))
    for phase in range(2):
        for which in range(2):
            parts = barrier(parts)
            came = barrier([send(v, order[phase], which) for v, order in zip(parts, orders)])
            parts = [jnp.concatenate(pair, axis=0) for pair in zip(parts, came)]
    first = barrier(parts)
    came = [send(v, order[2], 0) for v, order in zip(first, orders)]
    total = multiply(None, [(i, first[i], 0) for i in both])
    *came, total, start = barrier(came + first + [total, start])
    second, first = came[: len(parts)], came[len(parts) :]
    came = [send(v, order[2], 1) for v, order in zip(first, orders)]
    total = multiply(total, [(i, second[i], 1) for i in both])
    *came, total = barrier(came + second + [total])
    third, second = came[: len(parts)], came[len(parts) :]
    last = [send(v, order[2], 1) for v, order in zip(second, orders)]
    total = multiply(total, [(i, third[i], 2) for i in both])
    total, rest = barrier([total, rest])
    return last, total, start, rest


def shards(hidden, row_scale, key_value_weight, outlier, sketch_sign_flags):
    tokens, width = hidden.shape
    rows, heads, kv_cols = key_value_weight.shape
    cols = heads * kv_cols
    pairs = 2 * heads
    groups = outlier.shape[0]
    seq = lax.axis_size("seq")
    root_length = math.sqrt(tokens * seq)

    signs = (2 * sketch_sign_flags - 1).astype(F32).reshape(pairs, 128, RANK)
    start = pl.pallas_call(
        basis_start_kernel,
        out_shape=jax.ShapeDtypeStruct((pairs, 128, 128), F32),
        name="start",
        cost_estimate=pl.CostEstimate(flops=10**8, bytes_accessed=10**6, transcendentals=0),
    )(jnp.concatenate([signs, signs], axis=2))

    head, place, plane = lax.axis_index("head"), lax.axis_index("seq"), lax.axis_index("batch")
    lists = {
        "x": around(place // RING, head),
        "y": around(place % RING, head),
        "z": around(plane, head),
    }
    permuted = PART * len(ORDERS)

    def block_of(part, w, k):
        inner, outer, third = ORDERS[part]
        index = []
        for o in lists[outer]:
            for i in lists[inner]:
                at = {inner: i, outer: o, third: lists[third][k]}
                index.append((at["x"] * RING + at["y"]) * RING + at["z"])
        return part, w, jnp.stack(index)

    def multiply(total, arrivals):
        return accumulate("first" if total is None else "more", hidden, total, permuted, [block_of(*a) for a in arrivals])

    flat = key_value_weight.reshape(rows, cols)
    quarter = rows // RING
    own = lax.dynamic_slice_in_dim(flat, plane * quarter, quarter, 0)
    rest = lax.all_gather(own[:, permuted:], ("batch", "seq"), axis=0).reshape(RING, seq, quarter, cols - permuted)
    parts = [own[:, PART * i : PART * i + PART] for i in range(len(ORDERS))]
    last, total, start, rest = gather_blocks(parts, ORDERS, multiply, start, rest)
    rest = accumulate_all(hidden, rest)

    last = [block_of(i, w, 3) for i, w in enumerate(last)]
    specs, index = block_specs(tokens, last)
    keep = jnp.repeat(jnp.repeat((1 - outlier).astype(F32), kv_cols, axis=1), 8, axis=0)
    whole = lambda *shape: pl.BlockSpec(shape, lambda j, ix: (0,) * len(shape))
    high, low, gram = pl.pallas_call(
        functools.partial(project_kernel, [part for part, _, _ in last]),
        grid_spec=pltpu.PrefetchScalarGridSpec(
            num_scalar_prefetch=1,
            grid=(STEPS,),
            in_specs=specs
            + [whole(tokens, t.shape[1]) for t in (total, rest)]
            + [whole(tokens, 1), whole(8 * groups, cols)],
            out_specs=[whole(tokens, cols), whole(tokens, cols), whole(128 * pairs, 128)],
            scratch_shapes=[pltpu.VMEM(total.shape, F32)],
        ),
        out_shape=[
            jax.ShapeDtypeStruct((tokens, cols), BF16),
            jax.ShapeDtypeStruct((tokens, cols), BF16),
            jax.ShapeDtypeStruct((128 * pairs, 128), F32),
        ],
        compiler_params=pltpu.CompilerParams(vmem_limit_bytes=VMEM_LIMIT, dimension_semantics=("arbitrary",)),
        name="project",
        cost_estimate=cost(tokens, last),
    )(index, *block_operands(hidden, last), total, rest, row_scale[:, None], keep)

    pieces = lax.all_to_all(gram, "seq", 0, 0, tiled=True)
    piece = jnp.sum(pieces.reshape(seq, 128 * pairs // seq, 128), axis=0)
    gram = lax.all_to_all(jnp.broadcast_to(piece, (seq,) + piece.shape), "seq", 0, 0).reshape(128 * pairs, 128)

    return pl.pallas_call(
        functools.partial(factor_kernel, root_length),
        out_shape=[
            jax.ShapeDtypeStruct((heads, tokens, 2 * RANK), BF16),
            jax.ShapeDtypeStruct((heads, 128, 2 * RANK), F32),
        ],
        compiler_params=pltpu.CompilerParams(vmem_limit_bytes=40 << 20),
        name="factor",
        cost_estimate=pl.CostEstimate(flops=10**9, bytes_accessed=4 << 20, transcendentals=0),
    )(gram, start, high, low)


def solution(mesh):
    return jax.shard_map(
        shards,
        mesh=mesh,
        in_specs=(
            P(("batch", "seq"), None),
            P(("batch", "seq")),
            P("seq", "head", None),
            P(("batch", "seq"), "head"),
            P("head", None, None, None),
        ),
        out_specs=(P("head", ("batch", "seq"), None), P(("batch", "head"), None, None)),
        check_vma=False,
    )
```

```python
import functools
import math

import jax
import jax.numpy as jnp
from jax import lax
from jax.experimental import pallas as pl
from jax.experimental.pallas import tpu as pltpu
from jax.sharding import PartitionSpec as P

GROUP = 64
RANK = 64
RING = 4
STEPS = 4
PERMUTED = 512
WIDE = 256
UNROLL = 4
VMEM_LIMIT = 56 << 20
F32 = jnp.float32
BF16 = jnp.bfloat16
HIGHEST = lax.Precision.HIGHEST

SINE = [(-1) ** n * (2.0 * math.pi) ** (2 * n + 1) / math.factorial(2 * n + 1) for n in range(7)]


def split(x):
    high = x.astype(BF16)
    low = (x - high.astype(F32)).astype(BF16)
    return high, low


def sine_of_cycles(u):
    r = u - jnp.floor(u + 0.5)
    r = jnp.where(r > 0.25, 0.5 - r, jnp.where(r < -0.25, -0.5 - r, r))
    t = r * r
    p = jnp.full_like(t, SINE[-1])
    for c in SINE[-2::-1]:
        p = p * t + c
    return r * p


def dot(a, b, contract):
    return lax.dot_general(
        a, b, ((contract[:1], contract[1:]), ((), ())), precision=HIGHEST, preferred_element_type=F32
    )


def three_products(x, w):
    xh, xl = split(x)
    wh, wl = split(w)
    return jnp.dot(
        jnp.concatenate([xh, xl, xh], axis=1),
        jnp.concatenate([wh, wh, wl], axis=0),
        preferred_element_type=F32,
    )


def residual(kv, keep):
    step = jnp.max(jnp.abs(kv), axis=0, keepdims=True) / 7.0 + 1e-06
    return sine_of_cycles(kv * (1.0 / step)) * keep


def accumulate_kernel(shapes, first, *refs):
    refs = list(refs[1:])
    out_ref = refs.pop()
    if not first:
        base_ref = refs.pop()

    @pl.when(pl.program_id(0) == 0)
    def _():
        out_ref[...] = jnp.zeros_like(out_ref) if first else base_ref[...]

    total = None
    for parts in shapes:
        xs, refs = refs[:parts], refs[parts:]
        w_ref = refs.pop(0)
        x = xs[0][...] if parts == 1 else jnp.concatenate([r[...] for r in xs], axis=1)
        term = three_products(x, w_ref[...])
        total = term if total is None else total + term
    out_ref[...] += total


def block_specs(tokens, blocks):
    specs, at = [], 0
    for w, index, parts in blocks:
        rows = w.shape[0] // STEPS
        for i in range(parts):
            specs.append(
                pl.BlockSpec((tokens, rows // parts), lambda j, ix, a=at, n=parts, i=i: (0, ix[a + j * n + i]))
            )
        specs.append(pl.BlockSpec((rows, w.shape[1]), lambda j, ix: (j, 0)))
        at += STEPS * parts
    return specs, jnp.concatenate([index for _, index, _ in blocks])


def block_operands(hidden, blocks):
    return [x for w, _, parts in blocks for x in [hidden] * parts + [w]]


def cost(tokens, blocks):
    macs = sum(w.size for w, _, _ in blocks) * tokens
    return pl.CostEstimate(flops=6 * macs, bytes_accessed=sum(4 * w.size for w, _, _ in blocks) + 4 * tokens * 4096, transcendentals=0)


def accumulate(name, hidden, total, blocks):
    tokens = hidden.shape[0]
    cols = blocks[0][0].shape[1]
    specs, index = block_specs(tokens, blocks)
    whole = pl.BlockSpec((tokens, cols), lambda j, ix: (0, 0))
    return pl.pallas_call(
        functools.partial(accumulate_kernel, [parts for _, _, parts in blocks], total is None),
        grid_spec=pltpu.PrefetchScalarGridSpec(
            num_scalar_prefetch=1,
            grid=(STEPS,),
            in_specs=specs + ([] if total is None else [whole]),
            out_specs=whole,
        ),
        out_shape=jax.ShapeDtypeStruct((tokens, cols), F32),
        compiler_params=pltpu.CompilerParams(vmem_limit_bytes=VMEM_LIMIT, dimension_semantics=("arbitrary",)),
        name=name,
        cost_estimate=cost(tokens, blocks),
    )(index, *block_operands(hidden, blocks), *([] if total is None else [total]))


def accumulate_all_kernel(x_ref, w_ref, out_ref):
    @pl.when(pl.program_id(0) == 0)
    def _():
        out_ref[...] = jnp.zeros_like(out_ref)

    batch, shards_in, quarter, cols = w_ref.shape
    rows = batch * quarter
    for s in range(shards_in):
        out_ref[...] += three_products(x_ref[:, s * rows : s * rows + rows], w_ref[:, s].reshape(rows, cols))


def accumulate_all(hidden, weight):
    tokens = hidden.shape[0]
    batch, seq, quarter, cols = weight.shape
    return pl.pallas_call(
        accumulate_all_kernel,
        grid=(seq // 2,),
        in_specs=[
            pl.BlockSpec((tokens, 2 * batch * quarter), lambda k: (0, k)),
            pl.BlockSpec((batch, 2, quarter, cols), lambda k: (0, k, 0, 0)),
        ],
        out_specs=pl.BlockSpec((tokens, cols), lambda k: (0, 0)),
        out_shape=jax.ShapeDtypeStruct((tokens, cols), F32),
        compiler_params=pltpu.CompilerParams(vmem_limit_bytes=VMEM_LIMIT, dimension_semantics=("arbitrary",)),
        name="rest",
        cost_estimate=pl.CostEstimate(
            flops=6 * tokens * weight.size, bytes_accessed=4 * (weight.size + hidden.size), transcendentals=0
        ),
    )(hidden, weight)


def project_kernel(index_ref, xa, wa, xb, wb, ab_ref, cd_ref, scale_ref, keep_ref, high_ref, low_ref, gram_ref, ab_acc):
    step = pl.program_id(0)

    @pl.when(step == 0)
    def _():
        ab_acc[...] = ab_ref[...]

    ab_acc[...] += three_products(xa[...], wa[...]) + three_products(xb[...], wb[...])

    @pl.when(step == STEPS - 1)
    def _():
        epilogue(ab_acc, cd_ref, scale_ref, keep_ref, high_ref, low_ref, gram_ref)


def epilogue(total_ref, rest_ref, scale_ref, keep_ref, high_ref, low_ref, gram_ref):
    tokens = total_ref.shape[0]
    at = 0
    for part in (total_ref, rest_ref):
        for first in range(0, part.shape[1], WIDE):
            here = slice(at, at + WIDE)

            @pl.loop(0, tokens // GROUP, unroll=UNROLL)
            def _(g, part=part, first=first, here=here):
                rows = pl.ds(pl.multiple_of(g * GROUP, GROUP), GROUP)
                kv = part[rows, first : first + WIDE] * scale_ref[rows, :]
                keep = keep_ref[pl.ds(pl.multiple_of(g * 8, 8), 8), here][:1]
                rh, rl = split(residual(kv, keep))
                high_ref[rows, here] = rh
                low_ref[rows, here] = rl

            for cols in [slice(c, c + 128) for c in range(at, at + WIDE, 128)]:
                rh = high_ref[:, cols]
                both = lax.dot_general(
                    rh,
                    jnp.concatenate([rh, low_ref[:, cols]], axis=1),
                    (((0,), (0,)), ((), ())),
                    preferred_element_type=F32,
                )
                cross = both[:, 128:]
                gram_ref[cols, :] = both[:, :128] + (cross + cross.T)
            at += WIDE


def inverse_factors(grams):
    n = len(grams)
    lane = lax.broadcasted_iota(jnp.int32, (RANK, 128), 1)
    row = lax.broadcasted_iota(jnp.int32, (RANK, 128), 0)
    unit = jnp.where(lane - RANK == row, 1.0, 0.0).astype(F32)
    full = jnp.stack([jnp.where(lane < RANK, g, unit) for g in grams])
    blocks = [full[:, 8 * i : 8 * i + 8, :] for i in range(RANK // 8)]
    sub = lax.broadcasted_iota(jnp.int32, (n, 8, 1), 1)
    for j in range(RANK):
        jb, js = divmod(j, 8)
        pivot_row = blocks[jb][:, js : js + 1, :]
        scaled = pivot_row * (1.0 / pivot_row[:, :, j : j + 1])
        for i in range(jb, RANK // 8):
            column = blocks[i][:, :, j : j + 1]
            if i == jb:
                column = jnp.where(sub > js, column, 0.0)
            blocks[i] = blocks[i] - column * scaled
    full = jnp.concatenate(blocks, axis=1)
    out = []
    for p in range(n):
        a = full[p]
        pivots = jnp.sum(jnp.where(lane == row, a, 0.0), axis=1, keepdims=True)
        out.append(jnp.where(lane < RANK, 0.0, a) * lax.rsqrt(pivots))
    return out


def basis_start_kernel(sign_ref, out_ref):
    pairs = sign_ref.shape[0]
    inverses = inverse_factors([dot(sign_ref[p], sign_ref[p], (0, 0))[:RANK] for p in range(pairs)])
    for p in range(pairs):
        out_ref[p] = dot(sign_ref[p], jnp.concatenate([inverses[p]] * 2, axis=0), (1, 1))


def factor_kernel(root_length, gram_ref, start_ref, high_ref, low_ref, left_ref, right_ref):
    pairs = start_ref.shape[0]
    eye = lax.broadcasted_iota(jnp.int32, (128, 128), 0) == lax.broadcasted_iota(jnp.int32, (128, 128), 1)
    scales, ys, zs, grams = [], [], [], []
    for p in range(pairs):
        g = gram_ref[128 * p : 128 * p + 128, :]
        size = jnp.sum(jnp.sum(jnp.where(eye, g, 0.0), axis=1, keepdims=True), axis=0, keepdims=True) / 128.0
        g = g * (1.0 / size)
        y = dot(g, start_ref[p], (1, 0))
        z = dot(g, y, (1, 0))
        scales.append(size)
        ys.append(y)
        zs.append(z)
        grams.append(dot(y, z, (0, 0))[:RANK])
    inverses = inverse_factors(grams)
    zero = jnp.zeros((RANK, 128), F32)
    for h in range(pairs // 2):
        tops, rights = [], None
        for e in range(2):
            p = 2 * h + e
            wide = jnp.concatenate([inverses[p], zero] if e == 0 else [zero, inverses[p]], axis=0)
            tops.append(dot(ys[p], wide, (1, 1)) * (lax.rsqrt(scales[p]) * root_length))
            part = dot(zs[p], wide, (1, 1)) * (jnp.sqrt(scales[p]) * (1.0 / root_length))
            rights = part if rights is None else rights + part
        right_ref[h] = rights
        th, tl = split(jnp.concatenate(tops, axis=0))
        cols = slice(256 * h, 256 * h + 256)
        rh = high_ref[:, cols]
        rl = low_ref[:, cols]
        left_ref[h] = jnp.dot(
            jnp.concatenate([rh, rl, rh], axis=1),
            jnp.concatenate([th, th, tl], axis=0),
            preferred_element_type=F32,
        ).astype(BF16)


def partner(v, head, which):
    near, far = v ^ 1, 3 - v
    return jnp.where(head == which, near, far)


def around(v, head):
    second = partner(v, head, 1)
    return [v, partner(v, head, 0), second, partner(second, head, 0)]


def flat_partner(v, head, which):
    return (v ^ 1) if head == which else 3 - v


def plane_pairs(axis, which):
    pairs = []
    for h in range(2):
        for x in range(RING):
            for y in range(RING):
                tx, ty = (flat_partner(x, h, which), y) if axis == "x" else (x, flat_partner(y, h, which))
                pairs.append(((h * RING + x) * RING + y, (h * RING + tx) * RING + ty))
    return pairs


def gather_blocks(weight, multiply, start):
    def send(v, axis, which):
        return lax.ppermute(v, ("head", "seq"), plane_pairs(axis, which))

    join = lambda a, b: jnp.concatenate([a, b], axis=0)
    half = weight.shape[0] // 2
    a, b = weight[:half], weight[half:]
    for which in range(2):
        a, b = lax.optimization_barrier((a, b))
        a1, b1 = lax.optimization_barrier((send(a, "x", which), send(b, "y", which)))
        a, b = join(a, a1), join(b, b1)
    barrier = lax.optimization_barrier
    a, b = barrier((a, b))
    came = send(a, "y", 0), send(b, "x", 0)
    total = multiply("ab0", None, (a, b, 0))
    a1, b1, a, b, total, start = barrier((*came, a, b, total, start))
    came = send(a, "y", 1), send(b, "x", 1)
    total = multiply("ab1", total, (a1, b1, 1))
    a2, b2, a1, b1, total = barrier((*came, a1, b1, total))
    a3, b3 = send(a1, "y", 1), send(b1, "x", 1)
    total = multiply("ab2", total, (a2, b2, 2))
    return a3, b3, total, start


def shards(hidden, row_scale, key_value_weight, outlier, sketch_sign_flags):
    tokens, width = hidden.shape
    rows, heads, kv_cols = key_value_weight.shape
    cols = heads * kv_cols
    pairs = 2 * heads
    groups = outlier.shape[0]
    seq = lax.axis_size("seq")
    root_length = math.sqrt(tokens * seq)

    signs = (2 * sketch_sign_flags - 1).astype(F32).reshape(pairs, 128, RANK)
    start = pl.pallas_call(
        basis_start_kernel,
        out_shape=jax.ShapeDtypeStruct((pairs, 128, 128), F32),
        name="start",
        cost_estimate=pl.CostEstimate(flops=10**8, bytes_accessed=10**6, transcendentals=0),
    )(jnp.concatenate([signs, signs], axis=2))

    head, place, plane = lax.axis_index("head"), lax.axis_index("seq"), lax.axis_index("batch")
    xs, ys = around(place // RING, head), around(place % RING, head)
    shard = lambda x, y: x * RING + y

    def blocks_of(a, b, k):
        return [
            (a, jnp.stack([2 * shard(x, ys[k]) for x in xs]), 1),
            (b, jnp.stack([2 * shard(xs[k], y) + 1 for y in ys]), 1),
        ]

    def multiply(name, total, arrival):
        return accumulate(name, hidden, total, blocks_of(*arrival))

    flat = key_value_weight.reshape(rows, cols)
    quarter = rows // RING
    own = lax.dynamic_slice_in_dim(flat[:, PERMUTED:], plane * quarter, quarter, 0)
    rest = lax.all_gather(own, ("batch", "seq"), axis=0).reshape(RING, seq, quarter, cols - PERMUTED)
    a3, b3, ab, start = gather_blocks(flat[:, :PERMUTED], multiply, start)
    rest, ab = lax.optimization_barrier((rest, ab))
    cd = accumulate_all(hidden, rest)

    last = blocks_of(a3, b3, 3)
    specs, index = block_specs(tokens, last)
    keep = jnp.repeat(jnp.repeat((1 - outlier).astype(F32), kv_cols, axis=1), 8, axis=0)
    whole = lambda *shape: pl.BlockSpec(shape, lambda j, ix: (0,) * len(shape))
    high, low, gram = pl.pallas_call(
        project_kernel,
        grid_spec=pltpu.PrefetchScalarGridSpec(
            num_scalar_prefetch=1,
            grid=(STEPS,),
            in_specs=specs
            + [whole(tokens, t.shape[1]) for t in (ab, cd)]
            + [whole(tokens, 1), whole(8 * groups, cols)],
            out_specs=[whole(tokens, cols), whole(tokens, cols), whole(128 * pairs, 128)],
            scratch_shapes=[pltpu.VMEM(ab.shape, F32)],
        ),
        out_shape=[
            jax.ShapeDtypeStruct((tokens, cols), BF16),
            jax.ShapeDtypeStruct((tokens, cols), BF16),
            jax.ShapeDtypeStruct((128 * pairs, 128), F32),
        ],
        compiler_params=pltpu.CompilerParams(vmem_limit_bytes=VMEM_LIMIT, dimension_semantics=("arbitrary",)),
        name="project",
        cost_estimate=cost(tokens, last),
    )(index, *block_operands(hidden, last), ab, cd, row_scale[:, None], keep)

    pieces = lax.all_to_all(gram, "seq", 0, 0, tiled=True)
    piece = jnp.sum(pieces.reshape(seq, 128 * pairs // seq, 128), axis=0)
    gram = lax.all_to_all(jnp.broadcast_to(piece, (seq,) + piece.shape), "seq", 0, 0).reshape(128 * pairs, 128)

    return pl.pallas_call(
        functools.partial(factor_kernel, root_length),
        out_shape=[
            jax.ShapeDtypeStruct((heads, tokens, 2 * RANK), BF16),
            jax.ShapeDtypeStruct((heads, 128, 2 * RANK), F32),
        ],
        compiler_params=pltpu.CompilerParams(vmem_limit_bytes=40 << 20),
        name="factor",
        cost_estimate=pl.CostEstimate(flops=10**9, bytes_accessed=4 << 20, transcendentals=0),
    )(gram, start, high, low)


def solution(mesh):
    return jax.shard_map(
        shards,
        mesh=mesh,
        in_specs=(
            P(("batch", "seq"), None),
            P(("batch", "seq")),
            P("seq", "head", None),
            P(("batch", "seq"), "head"),
            P("head", None, None, None),
        ),
        out_specs=(P("head", ("batch", "seq"), None), P(("batch", "head"), None, None)),
        check_vma=False,
    )
```

```python
import functools
import math

import jax
import jax.numpy as jnp
from jax import lax
from jax.experimental import pallas as pl
from jax.experimental.pallas import tpu as pltpu
from jax.sharding import PartitionSpec as P

GROUP = 64
RANK = 64
RING = 4
STEPS = 4
PERMUTED = 512
DEEP = 256
WIDE = 256
UNROLL = 4
VMEM_LIMIT = 56 << 20
F32 = jnp.float32
BF16 = jnp.bfloat16
HIGHEST = lax.Precision.HIGHEST

SINE = [(-1) ** n * (2.0 * math.pi) ** (2 * n + 1) / math.factorial(2 * n + 1) for n in range(7)]


def split(x):
    high = x.astype(BF16)
    low = (x - high.astype(F32)).astype(BF16)
    return high, low


def sine_of_cycles(u):
    r = u - jnp.floor(u + 0.5)
    r = jnp.where(r > 0.25, 0.5 - r, jnp.where(r < -0.25, -0.5 - r, r))
    t = r * r
    p = jnp.full_like(t, SINE[-1])
    for c in SINE[-2::-1]:
        p = p * t + c
    return r * p


def dot(a, b, contract):
    return lax.dot_general(
        a, b, ((contract[:1], contract[1:]), ((), ())), precision=HIGHEST, preferred_element_type=F32
    )


def three_products(x, w):
    xh, xl = split(x)
    wh, wl = split(w)
    return jnp.dot(
        jnp.concatenate([xh, xl, xh], axis=1),
        jnp.concatenate([wh, wh, wl], axis=0),
        preferred_element_type=F32,
    )


def residual(kv, keep):
    step = jnp.max(jnp.abs(kv), axis=0, keepdims=True) / 7.0 + 1e-06
    return sine_of_cycles(kv * (1.0 / step)) * keep


def accumulate_kernel(shapes, first, *refs):
    refs = list(refs[1:])
    out_ref = refs.pop()
    if not first:
        base_ref = refs.pop()

    @pl.when(pl.program_id(0) == 0)
    def _():
        out_ref[...] = jnp.zeros_like(out_ref) if first else base_ref[...]

    total = None
    for parts in shapes:
        xs, refs = refs[:parts], refs[parts:]
        w_ref = refs.pop(0)
        x = xs[0][...] if parts == 1 else jnp.concatenate([r[...] for r in xs], axis=1)
        term = three_products(x, w_ref[...])
        total = term if total is None else total + term
    out_ref[...] += total


def block_specs(tokens, blocks):
    specs, at = [], 0
    for w, index, parts in blocks:
        rows = w.shape[0] // STEPS
        for i in range(parts):
            specs.append(
                pl.BlockSpec((tokens, rows // parts), lambda j, ix, a=at, n=parts, i=i: (0, ix[a + j * n + i]))
            )
        specs.append(pl.BlockSpec((rows, w.shape[1]), lambda j, ix: (j, 0)))
        at += STEPS * parts
    return specs, jnp.concatenate([index for _, index, _ in blocks])


def block_operands(hidden, blocks):
    return [x for w, _, parts in blocks for x in [hidden] * parts + [w]]


def cost(tokens, blocks):
    macs = sum(w.size for w, _, _ in blocks) * tokens
    return pl.CostEstimate(flops=6 * macs, bytes_accessed=sum(4 * w.size for w, _, _ in blocks) + 4 * tokens * 4096, transcendentals=0)


def accumulate(name, hidden, total, blocks):
    tokens = hidden.shape[0]
    cols = blocks[0][0].shape[1]
    specs, index = block_specs(tokens, blocks)
    whole = pl.BlockSpec((tokens, cols), lambda j, ix: (0, 0))
    return pl.pallas_call(
        functools.partial(accumulate_kernel, [parts for _, _, parts in blocks], total is None),
        grid_spec=pltpu.PrefetchScalarGridSpec(
            num_scalar_prefetch=1,
            grid=(STEPS,),
            in_specs=specs + ([] if total is None else [whole]),
            out_specs=whole,
        ),
        out_shape=jax.ShapeDtypeStruct((tokens, cols), F32),
        compiler_params=pltpu.CompilerParams(vmem_limit_bytes=VMEM_LIMIT, dimension_semantics=("arbitrary",)),
        name=name,
        cost_estimate=cost(tokens, blocks),
    )(index, *block_operands(hidden, blocks), *([] if total is None else [total]))


def accumulate_all_kernel(x_ref, w_ref, out_ref):
    @pl.when(pl.program_id(0) == 0)
    def _():
        out_ref[...] = jnp.zeros_like(out_ref)

    batch, shards_in, quarter, cols = w_ref.shape
    rows = batch * quarter
    for s in range(shards_in):
        out_ref[...] += three_products(x_ref[:, s * rows : s * rows + rows], w_ref[:, s].reshape(rows, cols))


def accumulate_all(hidden, weight):
    tokens = hidden.shape[0]
    batch, seq, quarter, cols = weight.shape
    return pl.pallas_call(
        accumulate_all_kernel,
        grid=(seq // 2,),
        in_specs=[
            pl.BlockSpec((tokens, 2 * batch * quarter), lambda k: (0, k)),
            pl.BlockSpec((batch, 2, quarter, cols), lambda k: (0, k, 0, 0)),
        ],
        out_specs=pl.BlockSpec((tokens, cols), lambda k: (0, 0)),
        out_shape=jax.ShapeDtypeStruct((tokens, cols), F32),
        compiler_params=pltpu.CompilerParams(vmem_limit_bytes=VMEM_LIMIT, dimension_semantics=("arbitrary",)),
        name="rest",
        cost_estimate=pl.CostEstimate(
            flops=6 * tokens * weight.size, bytes_accessed=4 * (weight.size + hidden.size), transcendentals=0
        ),
    )(hidden, weight)


def project_kernel(index_ref, xa, wa, xb, wb, xc0, xc1, xc2, xc3, wc, ab_ref, c_ref, rest_ref, scale_ref, keep_ref,
                   high_ref, low_ref, gram_ref, ab_acc, c_acc):
    step = pl.program_id(0)

    @pl.when(step == 0)
    def _():
        ab_acc[...] = ab_ref[...]
        c_acc[...] = c_ref[...]

    ab_acc[...] += three_products(xa[...], wa[...]) + three_products(xb[...], wb[...])
    c_acc[...] += three_products(jnp.concatenate([xc0[...], xc1[...], xc2[...], xc3[...]], axis=1), wc[...])

    @pl.when(step == STEPS - 1)
    def _():
        epilogue((ab_acc, c_acc, rest_ref), scale_ref, keep_ref, high_ref, low_ref, gram_ref)


def epilogue(parts, scale_ref, keep_ref, high_ref, low_ref, gram_ref):
    tokens = scale_ref.shape[0]
    at = 0
    for part in parts:
        for first in range(0, part.shape[1], WIDE):
            here = slice(at, at + WIDE)

            @pl.loop(0, tokens // GROUP, unroll=UNROLL)
            def _(g, part=part, first=first, here=here):
                rows = pl.ds(pl.multiple_of(g * GROUP, GROUP), GROUP)
                kv = part[rows, first : first + WIDE] * scale_ref[rows, :]
                keep = keep_ref[pl.ds(pl.multiple_of(g * 8, 8), 8), here][:1]
                rh, rl = split(residual(kv, keep))
                high_ref[rows, here] = rh
                low_ref[rows, here] = rl

            for cols in [slice(c, c + 128) for c in range(at, at + WIDE, 128)]:
                rh = high_ref[:, cols]
                both = lax.dot_general(
                    rh,
                    jnp.concatenate([rh, low_ref[:, cols]], axis=1),
                    (((0,), (0,)), ((), ())),
                    preferred_element_type=F32,
                )
                cross = both[:, 128:]
                gram_ref[cols, :] = both[:, :128] + (cross + cross.T)
            at += WIDE


def inverse_factors(grams):
    n = len(grams)
    lane = lax.broadcasted_iota(jnp.int32, (RANK, 128), 1)
    row = lax.broadcasted_iota(jnp.int32, (RANK, 128), 0)
    unit = jnp.where(lane - RANK == row, 1.0, 0.0).astype(F32)
    full = jnp.stack([jnp.where(lane < RANK, g, unit) for g in grams])
    blocks = [full[:, 8 * i : 8 * i + 8, :] for i in range(RANK // 8)]
    sub = lax.broadcasted_iota(jnp.int32, (n, 8, 1), 1)
    for j in range(RANK):
        jb, js = divmod(j, 8)
        pivot_row = blocks[jb][:, js : js + 1, :]
        scaled = pivot_row * (1.0 / pivot_row[:, :, j : j + 1])
        for i in range(jb, RANK // 8):
            column = blocks[i][:, :, j : j + 1]
            if i == jb:
                column = jnp.where(sub > js, column, 0.0)
            blocks[i] = blocks[i] - column * scaled
    full = jnp.concatenate(blocks, axis=1)
    out = []
    for p in range(n):
        a = full[p]
        pivots = jnp.sum(jnp.where(lane == row, a, 0.0), axis=1, keepdims=True)
        out.append(jnp.where(lane < RANK, 0.0, a) * lax.rsqrt(pivots))
    return out


def basis_start_kernel(sign_ref, out_ref):
    pairs = sign_ref.shape[0]
    inverses = inverse_factors([dot(sign_ref[p], sign_ref[p], (0, 0))[:RANK] for p in range(pairs)])
    for p in range(pairs):
        out_ref[p] = dot(sign_ref[p], jnp.concatenate([inverses[p]] * 2, axis=0), (1, 1))


def factor_kernel(root_length, gram_ref, start_ref, high_ref, low_ref, left_ref, right_ref):
    pairs = start_ref.shape[0]
    eye = lax.broadcasted_iota(jnp.int32, (128, 128), 0) == lax.broadcasted_iota(jnp.int32, (128, 128), 1)
    scales, ys, zs, grams = [], [], [], []
    for p in range(pairs):
        g = gram_ref[128 * p : 128 * p + 128, :]
        size = jnp.sum(jnp.sum(jnp.where(eye, g, 0.0), axis=1, keepdims=True), axis=0, keepdims=True) / 128.0
        g = g * (1.0 / size)
        y = dot(g, start_ref[p], (1, 0))
        z = dot(g, y, (1, 0))
        scales.append(size)
        ys.append(y)
        zs.append(z)
        grams.append(dot(y, z, (0, 0))[:RANK])
    inverses = inverse_factors(grams)
    zero = jnp.zeros((RANK, 128), F32)
    for h in range(pairs // 2):
        tops, rights = [], None
        for e in range(2):
            p = 2 * h + e
            wide = jnp.concatenate([inverses[p], zero] if e == 0 else [zero, inverses[p]], axis=0)
            tops.append(dot(ys[p], wide, (1, 1)) * (lax.rsqrt(scales[p]) * root_length))
            part = dot(zs[p], wide, (1, 1)) * (jnp.sqrt(scales[p]) * (1.0 / root_length))
            rights = part if rights is None else rights + part
        right_ref[h] = rights
        th, tl = split(jnp.concatenate(tops, axis=0))
        cols = slice(256 * h, 256 * h + 256)
        rh = high_ref[:, cols]
        rl = low_ref[:, cols]
        left_ref[h] = jnp.dot(
            jnp.concatenate([rh, rl, rh], axis=1),
            jnp.concatenate([th, th, tl], axis=0),
            preferred_element_type=F32,
        ).astype(BF16)


def partner(v, head, which):
    near, far = v ^ 1, 3 - v
    return jnp.where(head == which, near, far)


def around(v, head):
    second = partner(v, head, 1)
    return [v, partner(v, head, 0), second, partner(second, head, 0)]


def flat_partner(v, head, which):
    return (v ^ 1) if head == which else 3 - v


def plane_pairs(axis, which):
    pairs = []
    for h in range(2):
        for x in range(RING):
            for y in range(RING):
                tx, ty = (flat_partner(x, h, which), y) if axis == "x" else (x, flat_partner(y, h, which))
                pairs.append(((h * RING + x) * RING + y, (h * RING + tx) * RING + ty))
    return pairs


def depth_pairs(which):
    return [(z * 2 + h, flat_partner(z, h, which) * 2 + h) for z in range(RING) for h in range(2)]


def send(v, axis, which):
    if axis == "z":
        return lax.ppermute(v, ("batch", "head"), depth_pairs(which))
    return lax.ppermute(v, ("head", "seq"), plane_pairs(axis, which))


def gather_blocks(weight, deep, multiply, start):
    barrier = lax.optimization_barrier
    join = lambda a, b: jnp.concatenate([a, b], axis=0)
    half = weight.shape[0] // 2
    a, b = weight[:half], weight[half:]
    for which in range(2):
        a, b = barrier((a, b))
        a1, b1 = barrier((send(a, "x", which), send(b, "y", which)))
        a, b = join(a, a1), join(b, b1)
    a, b, c = own = barrier((a, b, deep))
    came = send(a, "y", 0), send(b, "x", 0), send(c, "z", 0)
    totals = multiply("0", None, own, 0)
    came, own, totals, start = barrier((came, own, totals, start))
    a, b, c = own
    later = send(a, "y", 1), send(b, "x", 1), send(c, "z", 1)
    totals = multiply("1", totals, came, 1)
    later, came, totals = barrier((later, came, totals))
    a, b, c = came
    last = send(a, "y", 1), send(b, "x", 1), send(c, "z", 1)
    totals = multiply("2", totals, later, 2)
    return last, totals, start


def shards(hidden, row_scale, key_value_weight, outlier, sketch_sign_flags):
    tokens, width = hidden.shape
    rows, heads, kv_cols = key_value_weight.shape
    cols = heads * kv_cols
    pairs = 2 * heads
    groups = outlier.shape[0]
    seq = lax.axis_size("seq")
    root_length = math.sqrt(tokens * seq)

    signs = (2 * sketch_sign_flags - 1).astype(F32).reshape(pairs, 128, RANK)
    start = pl.pallas_call(
        basis_start_kernel,
        out_shape=jax.ShapeDtypeStruct((pairs, 128, 128), F32),
        name="start",
        cost_estimate=pl.CostEstimate(flops=10**8, bytes_accessed=10**6, transcendentals=0),
    )(jnp.concatenate([signs, signs], axis=2))

    head, place, plane = lax.axis_index("head"), lax.axis_index("seq"), lax.axis_index("batch")
    xs, ys, zs = around(place // RING, head), around(place % RING, head), around(plane, head)
    shard = lambda x, y: x * RING + y

    def plane_blocks(a, b, k):
        return [
            (a, jnp.stack([2 * shard(x, ys[k]) for x in xs]), 1),
            (b, jnp.stack([2 * shard(xs[k], y) + 1 for y in ys]), 1),
        ]

    def deep_block(c, k):
        return (c, jnp.arange(seq, dtype=jnp.int32) * RING + zs[k], RING)

    def multiply(name, totals, arrival, k):
        a, b, c = arrival
        ab_total, c_total = totals or (None, None)
        return (
            accumulate("ab" + name, hidden, ab_total, plane_blocks(a, b, k)),
            accumulate("c" + name, hidden, c_total, [deep_block(c, k)]),
        )

    flat = key_value_weight.reshape(rows, cols)
    quarter = rows // RING
    rest_at = PERMUTED + DEEP
    own = lax.dynamic_slice_in_dim(flat[:, PERMUTED:], plane * quarter, quarter, 0)
    deep = lax.all_gather(own[:, :DEEP], "seq", axis=0, tiled=True)
    own, _ = lax.optimization_barrier((own[:, DEEP:], own))
    rest = lax.all_gather(own, ("batch", "seq"), axis=0).reshape(RING, seq, quarter, cols - rest_at)
    (a3, b3, c3), (ab, c), start = gather_blocks(flat[:, :PERMUTED], deep, multiply, start)
    rest, ab, c = lax.optimization_barrier((rest, ab, c))
    cd = accumulate_all(hidden, rest)

    last = plane_blocks(a3, b3, 3) + [deep_block(c3, 3)]
    specs, index = block_specs(tokens, last)
    keep = jnp.repeat(jnp.repeat((1 - outlier).astype(F32), kv_cols, axis=1), 8, axis=0)
    whole = lambda *shape: pl.BlockSpec(shape, lambda j, ix: (0,) * len(shape))
    high, low, gram = pl.pallas_call(
        project_kernel,
        grid_spec=pltpu.PrefetchScalarGridSpec(
            num_scalar_prefetch=1,
            grid=(STEPS,),
            in_specs=specs
            + [whole(tokens, t.shape[1]) for t in (ab, c, cd)]
            + [whole(tokens, 1), whole(8 * groups, cols)],
            out_specs=[whole(tokens, cols), whole(tokens, cols), whole(128 * pairs, 128)],
            scratch_shapes=[pltpu.VMEM(ab.shape, F32), pltpu.VMEM(c.shape, F32)],
        ),
        out_shape=[
            jax.ShapeDtypeStruct((tokens, cols), BF16),
            jax.ShapeDtypeStruct((tokens, cols), BF16),
            jax.ShapeDtypeStruct((128 * pairs, 128), F32),
        ],
        compiler_params=pltpu.CompilerParams(vmem_limit_bytes=VMEM_LIMIT, dimension_semantics=("arbitrary",)),
        name="project",
        cost_estimate=cost(tokens, last),
    )(index, *block_operands(hidden, last), ab, c, cd, row_scale[:, None], keep)

    pieces = lax.all_to_all(gram, "seq", 0, 0, tiled=True)
    piece = jnp.sum(pieces.reshape(seq, 128 * pairs // seq, 128), axis=0)
    gram = lax.all_to_all(jnp.broadcast_to(piece, (seq,) + piece.shape), "seq", 0, 0).reshape(128 * pairs, 128)

    return pl.pallas_call(
        functools.partial(factor_kernel, root_length),
        out_shape=[
            jax.ShapeDtypeStruct((heads, tokens, 2 * RANK), BF16),
            jax.ShapeDtypeStruct((heads, 128, 2 * RANK), F32),
        ],
        compiler_params=pltpu.CompilerParams(vmem_limit_bytes=40 << 20),
        name="factor",
        cost_estimate=pl.CostEstimate(flops=10**9, bytes_accessed=4 << 20, transcendentals=0),
    )(gram, start, high, low)


def solution(mesh):
    return jax.shard_map(
        shards,
        mesh=mesh,
        in_specs=(
            P(("batch", "seq"), None),
            P(("batch", "seq")),
            P("seq", "head", None),
            P(("batch", "seq"), "head"),
            P("head", None, None, None),
        ),
        out_specs=(P("head", ("batch", "seq"), None), P(("batch", "head"), None, None)),
        check_vma=False,
    )
```

```python
import functools
import math

import jax
import jax.numpy as jnp
from jax import lax
from jax.experimental import pallas as pl
from jax.experimental.pallas import tpu as pltpu
from jax.sharding import PartitionSpec as P

GROUP = 64
RANK = 64
RING = 4
STEPS = 4
PERMUTED = 512
DEEP = 256
WIDE = 256
UNROLL = 4
VMEM_LIMIT = 56 << 20
F32 = jnp.float32
BF16 = jnp.bfloat16
HIGHEST = lax.Precision.HIGHEST

SINE = [(-1) ** n * (2.0 * math.pi) ** (2 * n + 1) / math.factorial(2 * n + 1) for n in range(7)]


def split(x):
    high = x.astype(BF16)
    low = (x - high.astype(F32)).astype(BF16)
    return high, low


def sine_of_cycles(u):
    r = u - jnp.floor(u + 0.5)
    r = jnp.where(r > 0.25, 0.5 - r, jnp.where(r < -0.25, -0.5 - r, r))
    t = r * r
    p = jnp.full_like(t, SINE[-1])
    for c in SINE[-2::-1]:
        p = p * t + c
    return r * p


def dot(a, b, contract):
    return lax.dot_general(
        a, b, ((contract[:1], contract[1:]), ((), ())), precision=HIGHEST, preferred_element_type=F32
    )


def three_products(x, w):
    xh, xl = split(x)
    wh, wl = split(w)
    return jnp.dot(
        jnp.concatenate([xh, xl, xh], axis=1),
        jnp.concatenate([wh, wh, wl], axis=0),
        preferred_element_type=F32,
    )


def residual(kv, keep):
    step = jnp.max(jnp.abs(kv), axis=0, keepdims=True) / 7.0 + 1e-06
    return sine_of_cycles(kv * (1.0 / step)) * keep


def accumulate_kernel(shapes, first, *refs):
    refs = list(refs[1:])
    out_ref = refs.pop()
    if not first:
        base_ref = refs.pop()

    @pl.when(pl.program_id(0) == 0)
    def _():
        out_ref[...] = jnp.zeros_like(out_ref) if first else base_ref[...]

    total = None
    for parts in shapes:
        xs, refs = refs[:parts], refs[parts:]
        w_ref = refs.pop(0)
        x = xs[0][...] if parts == 1 else jnp.concatenate([r[...] for r in xs], axis=1)
        term = three_products(x, w_ref[...])
        total = term if total is None else total + term
    out_ref[...] += total


def block_specs(tokens, blocks):
    specs, at = [], 0
    for w, parts in blocks:
        rows = w.shape[0] // STEPS
        for i in range(parts):
            specs.append(
                pl.BlockSpec((tokens, rows // parts), lambda j, ix, a=at, n=parts, i=i: (0, ix[a + j * n + i]))
            )
        specs.append(pl.BlockSpec((rows, w.shape[1]), lambda j, ix: (j, 0)))
        at += STEPS * parts
    return specs


def block_operands(hidden, blocks):
    return [x for w, parts in blocks for x in [hidden] * parts + [w]]


def cost(tokens, blocks):
    macs = sum(w.size for w, _ in blocks) * tokens
    return pl.CostEstimate(
        flops=6 * macs, bytes_accessed=sum(4 * w.size + 4 * tokens * w.shape[0] for w, _ in blocks), transcendentals=0
    )


def accumulate(name, hidden, total, index, blocks):
    tokens = hidden.shape[0]
    cols = blocks[0][0].shape[1]
    whole = pl.BlockSpec((tokens, cols), lambda j, ix: (0, 0))
    return pl.pallas_call(
        functools.partial(accumulate_kernel, [parts for _, parts in blocks], total is None),
        grid_spec=pltpu.PrefetchScalarGridSpec(
            num_scalar_prefetch=1,
            grid=(STEPS,),
            in_specs=block_specs(tokens, blocks) + ([] if total is None else [whole]),
            out_specs=whole,
        ),
        out_shape=jax.ShapeDtypeStruct((tokens, cols), F32),
        compiler_params=pltpu.CompilerParams(vmem_limit_bytes=VMEM_LIMIT, dimension_semantics=("arbitrary",)),
        name=name,
        cost_estimate=cost(tokens, blocks),
    )(index, *block_operands(hidden, blocks), *([] if total is None else [total]))


def accumulate_all_kernel(x_ref, w_ref, out_ref):
    @pl.when(pl.program_id(0) == 0)
    def _():
        out_ref[...] = jnp.zeros_like(out_ref)

    batch, shards_in, quarter, cols = w_ref.shape
    rows = batch * quarter
    for s in range(shards_in):
        out_ref[...] += three_products(x_ref[:, s * rows : s * rows + rows], w_ref[:, s].reshape(rows, cols))


def accumulate_all(hidden, weight):
    tokens = hidden.shape[0]
    batch, seq, quarter, cols = weight.shape
    return pl.pallas_call(
        accumulate_all_kernel,
        grid=(seq // 2,),
        in_specs=[
            pl.BlockSpec((tokens, 2 * batch * quarter), lambda k: (0, k)),
            pl.BlockSpec((batch, 2, quarter, cols), lambda k: (0, k, 0, 0)),
        ],
        out_specs=pl.BlockSpec((tokens, cols), lambda k: (0, 0)),
        out_shape=jax.ShapeDtypeStruct((tokens, cols), F32),
        compiler_params=pltpu.CompilerParams(vmem_limit_bytes=VMEM_LIMIT, dimension_semantics=("arbitrary",)),
        name="rest",
        cost_estimate=pl.CostEstimate(
            flops=6 * tokens * weight.size, bytes_accessed=4 * (weight.size + hidden.size), transcendentals=0
        ),
    )(hidden, weight)


def project_kernel(index_ref, xa, wa, xb, wb, xc0, xc1, xc2, xc3, wc, ab_ref, c_ref, rest_ref, scale_ref, keep_ref,
                   high_ref, low_ref, gram_ref, ab_acc, c_acc):
    step = pl.program_id(0)

    @pl.when(step == 0)
    def _():
        ab_acc[...] = ab_ref[...]
        c_acc[...] = c_ref[...]

    ab_acc[...] += three_products(xa[...], wa[...]) + three_products(xb[...], wb[...])
    c_acc[...] += three_products(jnp.concatenate([xc0[...], xc1[...], xc2[...], xc3[...]], axis=1), wc[...])

    @pl.when(step == STEPS - 1)
    def _():
        epilogue((ab_acc, c_acc, rest_ref), scale_ref, keep_ref, high_ref, low_ref, gram_ref)


def epilogue(parts, scale_ref, keep_ref, high_ref, low_ref, gram_ref):
    tokens = scale_ref.shape[0]
    at = 0
    for part in parts:
        for first in range(0, part.shape[1], WIDE):
            here = slice(at, at + WIDE)

            @pl.loop(0, tokens // GROUP, unroll=UNROLL)
            def _(g, part=part, first=first, here=here):
                rows = pl.ds(pl.multiple_of(g * GROUP, GROUP), GROUP)
                kv = part[rows, first : first + WIDE] * scale_ref[rows, :]
                keep = keep_ref[pl.ds(pl.multiple_of(g * 8, 8), 8), here][:1]
                rh, rl = split(residual(kv, keep))
                high_ref[rows, here] = rh
                low_ref[rows, here] = rl

            for cols in [slice(c, c + 128) for c in range(at, at + WIDE, 128)]:
                rh = high_ref[:, cols]
                both = lax.dot_general(
                    rh,
                    jnp.concatenate([rh, low_ref[:, cols]], axis=1),
                    (((0,), (0,)), ((), ())),
                    preferred_element_type=F32,
                )
                cross = both[:, 128:]
                gram_ref[cols, :] = both[:, :128] + (cross + cross.T)
            at += WIDE


def inverse_factors(grams):
    n = len(grams)
    lane = lax.broadcasted_iota(jnp.int32, (RANK, 128), 1)
    row = lax.broadcasted_iota(jnp.int32, (RANK, 128), 0)
    unit = jnp.where(lane - RANK == row, 1.0, 0.0).astype(F32)
    full = jnp.stack([jnp.where(lane < RANK, g, unit) for g in grams])
    blocks = [full[:, 8 * i : 8 * i + 8, :] for i in range(RANK // 8)]
    sub = lax.broadcasted_iota(jnp.int32, (n, 8, 1), 1)
    for j in range(RANK):
        jb, js = divmod(j, 8)
        pivot_row = blocks[jb][:, js : js + 1, :]
        scaled = pivot_row * (1.0 / pivot_row[:, :, j : j + 1])
        for i in range(jb, RANK // 8):
            column = blocks[i][:, :, j : j + 1]
            if i == jb:
                column = jnp.where(sub > js, column, 0.0)
            blocks[i] = blocks[i] - column * scaled
    full = jnp.concatenate(blocks, axis=1)
    out = []
    for p in range(n):
        a = full[p]
        pivots = jnp.sum(jnp.where(lane == row, a, 0.0), axis=1, keepdims=True)
        out.append(jnp.where(lane < RANK, 0.0, a) * lax.rsqrt(pivots))
    return out


def basis_start_kernel(sign_ref, out_ref):
    pairs = sign_ref.shape[0]
    inverses = inverse_factors([dot(sign_ref[p], sign_ref[p], (0, 0))[:RANK] for p in range(pairs)])
    for p in range(pairs):
        out_ref[p] = dot(sign_ref[p], jnp.concatenate([inverses[p]] * 2, axis=0), (1, 1))


def factor_kernel(root_length, gram_ref, start_ref, high_ref, low_ref, left_ref, right_ref):
    pairs = start_ref.shape[0]
    eye = lax.broadcasted_iota(jnp.int32, (128, 128), 0) == lax.broadcasted_iota(jnp.int32, (128, 128), 1)
    scales, ys, zs, grams = [], [], [], []
    for p in range(pairs):
        g = gram_ref[128 * p : 128 * p + 128, :]
        size = jnp.sum(jnp.sum(jnp.where(eye, g, 0.0), axis=1, keepdims=True), axis=0, keepdims=True) / 128.0
        g = g * (1.0 / size)
        y = dot(g, start_ref[p], (1, 0))
        z = dot(g, y, (1, 0))
        scales.append(size)
        ys.append(y)
        zs.append(z)
        grams.append(dot(y, z, (0, 0))[:RANK])
    inverses = inverse_factors(grams)
    zero = jnp.zeros((RANK, 128), F32)
    for h in range(pairs // 2):
        tops, rights = [], None
        for e in range(2):
            p = 2 * h + e
            wide = jnp.concatenate([inverses[p], zero] if e == 0 else [zero, inverses[p]], axis=0)
            tops.append(dot(ys[p], wide, (1, 1)) * (lax.rsqrt(scales[p]) * root_length))
            part = dot(zs[p], wide, (1, 1)) * (jnp.sqrt(scales[p]) * (1.0 / root_length))
            rights = part if rights is None else rights + part
        right_ref[h] = rights
        th, tl = split(jnp.concatenate(tops, axis=0))
        cols = slice(256 * h, 256 * h + 256)
        rh = high_ref[:, cols]
        rl = low_ref[:, cols]
        left_ref[h] = jnp.dot(
            jnp.concatenate([rh, rl, rh], axis=1),
            jnp.concatenate([th, th, tl], axis=0),
            preferred_element_type=F32,
        ).astype(BF16)


def partner(v, head, which):
    near, far = v ^ 1, 3 - v
    return jnp.where(head == which, near, far)


def around(v, head):
    second = partner(v, head, 1)
    return [v, partner(v, head, 0), second, partner(second, head, 0)]


def flat_partner(v, head, which):
    return (v ^ 1) if head == which else 3 - v


def plane_pairs(axis, which):
    pairs = []
    for h in range(2):
        for x in range(RING):
            for y in range(RING):
                tx, ty = (flat_partner(x, h, which), y) if axis == "x" else (x, flat_partner(y, h, which))
                pairs.append(((h * RING + x) * RING + y, (h * RING + tx) * RING + ty))
    return pairs


def depth_pairs(which):
    return [(z * 2 + h, flat_partner(z, h, which) * 2 + h) for z in range(RING) for h in range(2)]


def send(v, axis, which):
    if axis == "z":
        return lax.ppermute(v, ("batch", "head"), depth_pairs(which))
    return lax.ppermute(v, ("head", "seq"), plane_pairs(axis, which))


def gather_blocks(weight, deep, multiply, early):
    barrier = lax.optimization_barrier
    join = lambda a, b: jnp.concatenate([a, b], axis=0)
    half = weight.shape[0] // 2
    a, b = weight[:half], weight[half:]
    for which in range(2):
        a, b = barrier((a, b))
        came = send(a, "x", which), send(b, "y", which)
        if which:
            came, early = barrier((came, early))
        else:
            came = barrier(came)
        a, b = join(a, came[0]), join(b, came[1])
    plane0 = barrier((a, b))
    to_y_x = lambda blocks, which: (send(blocks[0], "y", which), send(blocks[1], "x", which))
    plane1 = to_y_x(plane0, 0)
    plane = multiply(None, plane0, 0)
    deep0, plane0, plane = barrier((deep, plane0, plane))
    deep1 = send(deep0, "z", 0)
    depth = multiply(None, (deep0,), 0)
    plane1, plane0, plane, depth = barrier((plane1, plane0, plane, depth))
    plane2 = to_y_x(plane0, 1)
    plane = multiply(plane, plane1, 1)
    deep1, deep0, plane = barrier((deep1, deep0, plane))
    deep2 = send(deep0, "z", 1)
    depth = multiply(depth, (deep1,), 1)
    plane2, plane1, depth = barrier((plane2, plane1, depth))
    plane3 = to_y_x(plane1, 1)
    plane = multiply(plane, plane2, 2)
    deep2, deep1, plane = barrier((deep2, deep1, plane))
    deep3 = send(deep1, "z", 1)
    depth = multiply(depth, (deep2,), 2)
    return (*plane3, deep3), (plane, depth), early


def shards(hidden, row_scale, key_value_weight, outlier, sketch_sign_flags):
    tokens, width = hidden.shape
    rows, heads, kv_cols = key_value_weight.shape
    cols = heads * kv_cols
    pairs = 2 * heads
    groups = outlier.shape[0]
    seq = lax.axis_size("seq")
    root_length = math.sqrt(tokens * seq)

    signs = (2 * sketch_sign_flags - 1).astype(F32).reshape(pairs, 128, RANK)
    start = pl.pallas_call(
        basis_start_kernel,
        out_shape=jax.ShapeDtypeStruct((pairs, 128, 128), F32),
        name="start",
        cost_estimate=pl.CostEstimate(flops=10**8, bytes_accessed=10**6, transcendentals=0),
    )(jnp.concatenate([signs, signs], axis=2))

    head, place, plane = lax.axis_index("head"), lax.axis_index("seq"), lax.axis_index("batch")
    xs, ys, zs = around(place // RING, head), around(place % RING, head), around(plane, head)
    shard = lambda x, y: x * RING + y
    plane_index = [
        (jnp.stack([2 * shard(x, ys[k]) for x in xs]), jnp.stack([2 * shard(xs[k], y) + 1 for y in ys]))
        for k in range(RING)
    ]
    deep_index = [(jnp.arange(seq, dtype=jnp.int32) * RING + zs[k],) for k in range(RING)]
    joined = lambda *lists: jnp.concatenate([i for indices in lists for i in indices])
    plane_at = [joined(i) for i in plane_index]
    deep_at = [joined(i) for i in deep_index]
    last_at = joined(plane_index[3], deep_index[3])
    scale = row_scale[:, None]
    keep = jnp.repeat(jnp.repeat((1 - outlier).astype(F32), kv_cols, axis=1), 8, axis=0)

    def multiply(total, blocks, k):
        kind, parts, at = ("plane", 1, plane_at) if len(blocks) == 2 else ("deep", RING, deep_at)
        return accumulate(kind + str(k), hidden, total, at[k], [(w, parts) for w in blocks])

    flat = key_value_weight.reshape(rows, cols)
    quarter = rows // RING
    rest_at = PERMUTED + DEEP
    own = lax.dynamic_slice_in_dim(flat[:, PERMUTED:], plane * quarter, quarter, 0)
    deep = lax.all_gather(own[:, :DEEP], "seq", axis=0, tiled=True)
    own, _ = lax.optimization_barrier((own[:, DEEP:], own))
    rest = lax.all_gather(own, ("batch", "seq"), axis=0).reshape(RING, seq, quarter, cols - rest_at)
    early = (start, scale, keep, last_at)
    (a3, b3, c3), (ab, c), (start, scale, keep, last_at) = gather_blocks(flat[:, :PERMUTED], deep, multiply, early)
    rest, ab, c = lax.optimization_barrier((rest, ab, c))
    cd = accumulate_all(hidden, rest)

    last = [(a3, 1), (b3, 1), (c3, RING)]
    specs = block_specs(tokens, last)
    whole = lambda *shape: pl.BlockSpec(shape, lambda j, ix: (0,) * len(shape))
    high, low, gram = pl.pallas_call(
        project_kernel,
        grid_spec=pltpu.PrefetchScalarGridSpec(
            num_scalar_prefetch=1,
            grid=(STEPS,),
            in_specs=specs
            + [whole(tokens, t.shape[1]) for t in (ab, c, cd)]
            + [whole(tokens, 1), whole(8 * groups, cols)],
            out_specs=[whole(tokens, cols), whole(tokens, cols), whole(128 * pairs, 128)],
            scratch_shapes=[pltpu.VMEM(ab.shape, F32), pltpu.VMEM(c.shape, F32)],
        ),
        out_shape=[
            jax.ShapeDtypeStruct((tokens, cols), BF16),
            jax.ShapeDtypeStruct((tokens, cols), BF16),
            jax.ShapeDtypeStruct((128 * pairs, 128), F32),
        ],
        compiler_params=pltpu.CompilerParams(vmem_limit_bytes=VMEM_LIMIT, dimension_semantics=("arbitrary",)),
        name="project",
        cost_estimate=cost(tokens, last),
    )(last_at, *block_operands(hidden, last), ab, c, cd, scale, keep)

    pieces = lax.all_to_all(gram, "seq", 0, 0, tiled=True)
    piece = jnp.sum(pieces.reshape(seq, 128 * pairs // seq, 128), axis=0)
    gram = lax.all_to_all(jnp.broadcast_to(piece, (seq,) + piece.shape), "seq", 0, 0).reshape(128 * pairs, 128)

    return pl.pallas_call(
        functools.partial(factor_kernel, root_length),
        out_shape=[
            jax.ShapeDtypeStruct((heads, tokens, 2 * RANK), BF16),
            jax.ShapeDtypeStruct((heads, 128, 2 * RANK), F32),
        ],
        compiler_params=pltpu.CompilerParams(vmem_limit_bytes=40 << 20),
        name="factor",
        cost_estimate=pl.CostEstimate(flops=10**9, bytes_accessed=4 << 20, transcendentals=0),
    )(gram, start, high, low)


def solution(mesh):
    return jax.shard_map(
        shards,
        mesh=mesh,
        in_specs=(
            P(("batch", "seq"), None),
            P(("batch", "seq")),
            P("seq", "head", None),
            P(("batch", "seq"), "head"),
            P("head", None, None, None),
        ),
        out_specs=(P("head", ("batch", "seq"), None), P(("batch", "head"), None, None)),
        check_vma=False,
    )
```

```python
import functools
import math

import jax
import jax.numpy as jnp
from jax import lax
from jax.experimental import pallas as pl
from jax.experimental.pallas import tpu as pltpu
from jax.sharding import PartitionSpec as P

GROUP = 64
RANK = 64
RING = 4
STEPS = 4
PERMUTED = 640
DEEP = 256
WIDE = 256
UNROLL = 4
VMEM_LIMIT = 56 << 20
F32 = jnp.float32
BF16 = jnp.bfloat16
HIGHEST = lax.Precision.HIGHEST

SINE = [(-1) ** n * (2.0 * math.pi) ** (2 * n + 1) / math.factorial(2 * n + 1) for n in range(7)]


def split(x):
    high = x.astype(BF16)
    low = (x - high.astype(F32)).astype(BF16)
    return high, low


def sine_of_cycles(u):
    r = u - jnp.floor(u + 0.5)
    r = jnp.where(r > 0.25, 0.5 - r, jnp.where(r < -0.25, -0.5 - r, r))
    t = r * r
    p = jnp.full_like(t, SINE[-1])
    for c in SINE[-2::-1]:
        p = p * t + c
    return r * p


def dot(a, b, contract):
    return lax.dot_general(
        a, b, ((contract[:1], contract[1:]), ((), ())), precision=HIGHEST, preferred_element_type=F32
    )


def three_products(x, w):
    xh, xl = split(x)
    wh, wl = split(w)
    return jnp.dot(
        jnp.concatenate([xh, xl, xh], axis=1),
        jnp.concatenate([wh, wh, wl], axis=0),
        preferred_element_type=F32,
    )


def residual(kv, keep):
    step = jnp.max(jnp.abs(kv), axis=0, keepdims=True) / 7.0 + 1e-06
    return sine_of_cycles(kv * (1.0 / step)) * keep


def accumulate_kernel(shapes, first, *refs):
    refs = list(refs[1:])
    out_ref = refs.pop()
    if not first:
        base_ref = refs.pop()

    @pl.when(pl.program_id(0) == 0)
    def _():
        out_ref[...] = jnp.zeros_like(out_ref) if first else base_ref[...]

    total = None
    for parts in shapes:
        xs, refs = refs[:parts], refs[parts:]
        w_ref = refs.pop(0)
        x = xs[0][...] if parts == 1 else jnp.concatenate([r[...] for r in xs], axis=1)
        term = three_products(x, w_ref[...])
        total = term if total is None else total + term
    out_ref[...] += total


def block_specs(tokens, blocks):
    specs, at = [], 0
    for w, parts in blocks:
        rows = w.shape[0] // STEPS
        for i in range(parts):
            specs.append(
                pl.BlockSpec((tokens, rows // parts), lambda j, ix, a=at, n=parts, i=i: (0, ix[a + j * n + i]))
            )
        specs.append(pl.BlockSpec((rows, w.shape[1]), lambda j, ix: (j, 0)))
        at += STEPS * parts
    return specs


def block_operands(hidden, blocks):
    return [x for w, parts in blocks for x in [hidden] * parts + [w]]


def cost(tokens, blocks):
    macs = sum(w.size for w, _ in blocks) * tokens
    return pl.CostEstimate(
        flops=6 * macs, bytes_accessed=sum(4 * w.size + 4 * tokens * w.shape[0] for w, _ in blocks), transcendentals=0
    )


def accumulate(name, hidden, total, index, blocks):
    tokens = hidden.shape[0]
    cols = blocks[0][0].shape[1]
    whole = pl.BlockSpec((tokens, cols), lambda j, ix: (0, 0))
    return pl.pallas_call(
        functools.partial(accumulate_kernel, [parts for _, parts in blocks], total is None),
        grid_spec=pltpu.PrefetchScalarGridSpec(
            num_scalar_prefetch=1,
            grid=(STEPS,),
            in_specs=block_specs(tokens, blocks) + ([] if total is None else [whole]),
            out_specs=whole,
        ),
        out_shape=jax.ShapeDtypeStruct((tokens, cols), F32),
        compiler_params=pltpu.CompilerParams(vmem_limit_bytes=VMEM_LIMIT, dimension_semantics=("arbitrary",)),
        name=name,
        cost_estimate=cost(tokens, blocks),
    )(index, *block_operands(hidden, blocks), *([] if total is None else [total]))


def accumulate_all_kernel(x_ref, w_ref, out_ref):
    @pl.when(pl.program_id(0) == 0)
    def _():
        out_ref[...] = jnp.zeros_like(out_ref)

    batch, shards_in, quarter, cols = w_ref.shape
    rows = batch * quarter
    for s in range(shards_in):
        out_ref[...] += three_products(x_ref[:, s * rows : s * rows + rows], w_ref[:, s].reshape(rows, cols))


def accumulate_all(hidden, weight):
    tokens = hidden.shape[0]
    batch, seq, quarter, cols = weight.shape
    return pl.pallas_call(
        accumulate_all_kernel,
        grid=(seq // 2,),
        in_specs=[
            pl.BlockSpec((tokens, 2 * batch * quarter), lambda k: (0, k)),
            pl.BlockSpec((batch, 2, quarter, cols), lambda k: (0, k, 0, 0)),
        ],
        out_specs=pl.BlockSpec((tokens, cols), lambda k: (0, 0)),
        out_shape=jax.ShapeDtypeStruct((tokens, cols), F32),
        compiler_params=pltpu.CompilerParams(vmem_limit_bytes=VMEM_LIMIT, dimension_semantics=("arbitrary",)),
        name="rest",
        cost_estimate=pl.CostEstimate(
            flops=6 * tokens * weight.size, bytes_accessed=4 * (weight.size + hidden.size), transcendentals=0
        ),
    )(hidden, weight)


def project_kernel(index_ref, x0, x1, x2, x3, w, plane_ref, depth_ref, rest_ref, scale_ref, keep_ref,
                   high_ref, low_ref, gram_ref, depth_acc):
    step = pl.program_id(0)

    @pl.when(step == 0)
    def _():
        depth_acc[...] = depth_ref[...]

    depth_acc[...] += three_products(jnp.concatenate([x0[...], x1[...], x2[...], x3[...]], axis=1), w[...])

    @pl.when(step == STEPS - 1)
    def _():
        epilogue((plane_ref, depth_acc, rest_ref), scale_ref, keep_ref, high_ref, low_ref, gram_ref)


def epilogue(parts, scale_ref, keep_ref, high_ref, low_ref, gram_ref):
    tokens = scale_ref.shape[0]
    at = 0
    for part in parts:
        for first in range(0, part.shape[1], WIDE):
            wide = min(WIDE, part.shape[1] - first)
            here = slice(at, at + wide)

            @pl.loop(0, tokens // GROUP, unroll=UNROLL)
            def _(g, part=part, first=first, wide=wide, here=here):
                rows = pl.ds(pl.multiple_of(g * GROUP, GROUP), GROUP)
                kv = part[rows, first : first + wide] * scale_ref[rows, :]
                keep = keep_ref[pl.ds(pl.multiple_of(g * 8, 8), 8), here][:1]
                rh, rl = split(residual(kv, keep))
                high_ref[rows, here] = rh
                low_ref[rows, here] = rl

            for cols in [slice(c, c + 128) for c in range(at, at + wide, 128)]:
                rh = high_ref[:, cols]
                both = lax.dot_general(
                    rh,
                    jnp.concatenate([rh, low_ref[:, cols]], axis=1),
                    (((0,), (0,)), ((), ())),
                    preferred_element_type=F32,
                )
                cross = both[:, 128:]
                gram_ref[cols, :] = both[:, :128] + (cross + cross.T)
            at += wide


def inverse_factors(grams):
    n = len(grams)
    lane = lax.broadcasted_iota(jnp.int32, (RANK, 128), 1)
    row = lax.broadcasted_iota(jnp.int32, (RANK, 128), 0)
    unit = jnp.where(lane - RANK == row, 1.0, 0.0).astype(F32)
    full = jnp.stack([jnp.where(lane < RANK, g, unit) for g in grams])
    blocks = [full[:, 8 * i : 8 * i + 8, :] for i in range(RANK // 8)]
    sub = lax.broadcasted_iota(jnp.int32, (n, 8, 1), 1)
    for j in range(RANK):
        jb, js = divmod(j, 8)
        pivot_row = blocks[jb][:, js : js + 1, :]
        scaled = pivot_row * (1.0 / pivot_row[:, :, j : j + 1])
        for i in range(jb, RANK // 8):
            column = blocks[i][:, :, j : j + 1]
            if i == jb:
                column = jnp.where(sub > js, column, 0.0)
            blocks[i] = blocks[i] - column * scaled
    full = jnp.concatenate(blocks, axis=1)
    out = []
    for p in range(n):
        a = full[p]
        pivots = jnp.sum(jnp.where(lane == row, a, 0.0), axis=1, keepdims=True)
        out.append(jnp.where(lane < RANK, 0.0, a) * lax.rsqrt(pivots))
    return out


def basis_start_kernel(sign_ref, out_ref):
    pairs = sign_ref.shape[0]
    inverses = inverse_factors([dot(sign_ref[p], sign_ref[p], (0, 0))[:RANK] for p in range(pairs)])
    for p in range(pairs):
        out_ref[p] = dot(sign_ref[p], jnp.concatenate([inverses[p]] * 2, axis=0), (1, 1))


def factor_kernel(root_length, gram_ref, start_ref, high_ref, low_ref, left_ref, right_ref):
    pairs = start_ref.shape[0]
    eye = lax.broadcasted_iota(jnp.int32, (128, 128), 0) == lax.broadcasted_iota(jnp.int32, (128, 128), 1)
    scales, ys, zs, grams = [], [], [], []
    for p in range(pairs):
        g = gram_ref[128 * p : 128 * p + 128, :]
        size = jnp.sum(jnp.sum(jnp.where(eye, g, 0.0), axis=1, keepdims=True), axis=0, keepdims=True) / 128.0
        g = g * (1.0 / size)
        y = dot(g, start_ref[p], (1, 0))
        z = dot(g, y, (1, 0))
        scales.append(size)
        ys.append(y)
        zs.append(z)
        grams.append(dot(y, z, (0, 0))[:RANK])
    inverses = inverse_factors(grams)
    zero = jnp.zeros((RANK, 128), F32)
    for h in range(pairs // 2):
        tops, rights = [], None
        for e in range(2):
            p = 2 * h + e
            wide = jnp.concatenate([inverses[p], zero] if e == 0 else [zero, inverses[p]], axis=0)
            tops.append(dot(ys[p], wide, (1, 1)) * (lax.rsqrt(scales[p]) * root_length))
            part = dot(zs[p], wide, (1, 1)) * (jnp.sqrt(scales[p]) * (1.0 / root_length))
            rights = part if rights is None else rights + part
        right_ref[h] = rights
        th, tl = split(jnp.concatenate(tops, axis=0))
        cols = slice(256 * h, 256 * h + 256)
        rh = high_ref[:, cols]
        rl = low_ref[:, cols]
        left_ref[h] = jnp.dot(
            jnp.concatenate([rh, rl, rh], axis=1),
            jnp.concatenate([th, th, tl], axis=0),
            preferred_element_type=F32,
        ).astype(BF16)


def partner(v, head, which):
    near, far = v ^ 1, 3 - v
    return jnp.where(head == which, near, far)


def around(v, head):
    second = partner(v, head, 1)
    return [v, partner(v, head, 0), second, partner(second, head, 0)]


def flat_partner(v, head, which):
    return (v ^ 1) if head == which else 3 - v


def plane_pairs(axis, which):
    pairs = []
    for h in range(2):
        for x in range(RING):
            for y in range(RING):
                tx, ty = (flat_partner(x, h, which), y) if axis == "x" else (x, flat_partner(y, h, which))
                pairs.append(((h * RING + x) * RING + y, (h * RING + tx) * RING + ty))
    return pairs


def depth_pairs(which):
    return [(z * 2 + h, flat_partner(z, h, which) * 2 + h) for z in range(RING) for h in range(2)]


def send(v, axis, which):
    if axis == "z":
        return lax.ppermute(v, ("batch", "head"), depth_pairs(which))
    return lax.ppermute(v, ("head", "seq"), plane_pairs(axis, which))


def gather_blocks(weight, deep, multiply, early):
    barrier = lax.optimization_barrier
    join = lambda a, b: jnp.concatenate([a, b], axis=0)
    half = weight.shape[0] // 2
    a, b = weight[:half], weight[half:]
    for which in range(2):
        a, b = barrier((a, b))
        came = send(a, "x", which), send(b, "y", which)
        if which:
            came, early = barrier((came, early))
        else:
            came = barrier(came)
        a, b = join(a, came[0]), join(b, came[1])
    plane0 = barrier((a, b))
    to_y_x = lambda blocks, which: (send(blocks[0], "y", which), send(blocks[1], "x", which))
    plane1 = to_y_x(plane0, 0)
    plane = multiply(None, plane0, 0)
    deep0, plane0, plane = barrier((deep, plane0, plane))
    deep1 = send(deep0, "z", 0)
    depth = multiply(None, (deep0,), 0)
    plane1, plane0, plane, depth = barrier((plane1, plane0, plane, depth))
    plane2 = to_y_x(plane0, 1)
    plane = multiply(plane, plane1, 1)
    deep1, deep0, plane = barrier((deep1, deep0, plane))
    deep2 = send(deep0, "z", 1)
    depth = multiply(depth, (deep1,), 1)
    plane2, plane1, depth = barrier((plane2, plane1, depth))
    plane3 = to_y_x(plane1, 1)
    plane = multiply(plane, plane2, 2)
    deep2, deep1, plane = barrier((deep2, deep1, plane))
    deep3 = send(deep1, "z", 1)
    depth = multiply(depth, (deep2,), 2)
    return plane3, deep3, plane, depth, early


def shards(hidden, row_scale, key_value_weight, outlier, sketch_sign_flags):
    tokens, width = hidden.shape
    rows, heads, kv_cols = key_value_weight.shape
    cols = heads * kv_cols
    pairs = 2 * heads
    groups = outlier.shape[0]
    seq = lax.axis_size("seq")
    root_length = math.sqrt(tokens * seq)

    signs = (2 * sketch_sign_flags - 1).astype(F32).reshape(pairs, 128, RANK)
    start = pl.pallas_call(
        basis_start_kernel,
        out_shape=jax.ShapeDtypeStruct((pairs, 128, 128), F32),
        name="start",
        cost_estimate=pl.CostEstimate(flops=10**8, bytes_accessed=10**6, transcendentals=0),
    )(jnp.concatenate([signs, signs], axis=2))

    head, place, plane = lax.axis_index("head"), lax.axis_index("seq"), lax.axis_index("batch")
    xs, ys, zs = around(place // RING, head), around(place % RING, head), around(plane, head)
    shard = lambda x, y: x * RING + y
    plane_index = [
        (jnp.stack([2 * shard(x, ys[k]) for x in xs]), jnp.stack([2 * shard(xs[k], y) + 1 for y in ys]))
        for k in range(RING)
    ]
    deep_index = [(jnp.arange(seq, dtype=jnp.int32) * RING + zs[k],) for k in range(RING)]
    joined = lambda *lists: jnp.concatenate([i for indices in lists for i in indices])
    plane_at = [joined(i) for i in plane_index]
    deep_at = [joined(i) for i in deep_index]
    scale = row_scale[:, None]
    keep = jnp.repeat(jnp.repeat((1 - outlier).astype(F32), kv_cols, axis=1), 8, axis=0)

    def multiply(total, blocks, k):
        kind, parts, at = ("plane", 1, plane_at) if len(blocks) == 2 else ("deep", RING, deep_at)
        return accumulate(kind + str(k), hidden, total, at[k], [(w, parts) for w in blocks])

    flat = key_value_weight.reshape(rows, cols)
    quarter = rows // RING
    rest_at = PERMUTED + DEEP
    own = lax.dynamic_slice_in_dim(flat[:, PERMUTED:], plane * quarter, quarter, 0)
    deep = lax.all_gather(own[:, :DEEP], "seq", axis=0, tiled=True)
    own, _ = lax.optimization_barrier((own[:, DEEP:], own))
    rest = lax.all_gather(own, ("batch", "seq"), axis=0).reshape(RING, seq, quarter, cols - rest_at)
    early = (start, scale, keep)
    plane3, deep3, ab, c, (start, scale, keep) = gather_blocks(flat[:, :PERMUTED], deep, multiply, early)
    rest, ab, c = lax.optimization_barrier((rest, ab, c))
    cd = accumulate_all(hidden, rest)
    plane3, ab, cd = lax.optimization_barrier((plane3, ab, cd))
    ab = multiply(ab, plane3, 3)
    deep3, ab, c = lax.optimization_barrier((deep3, ab, c))

    last = [(deep3, RING)]
    specs = block_specs(tokens, last)
    whole = lambda *shape: pl.BlockSpec(shape, lambda j, ix: (0,) * len(shape))
    high, low, gram = pl.pallas_call(
        project_kernel,
        grid_spec=pltpu.PrefetchScalarGridSpec(
            num_scalar_prefetch=1,
            grid=(STEPS,),
            in_specs=specs
            + [whole(tokens, t.shape[1]) for t in (ab, c, cd)]
            + [whole(tokens, 1), whole(8 * groups, cols)],
            out_specs=[whole(tokens, cols), whole(tokens, cols), whole(128 * pairs, 128)],
            scratch_shapes=[pltpu.VMEM(c.shape, F32)],
        ),
        out_shape=[
            jax.ShapeDtypeStruct((tokens, cols), BF16),
            jax.ShapeDtypeStruct((tokens, cols), BF16),
            jax.ShapeDtypeStruct((128 * pairs, 128), F32),
        ],
        compiler_params=pltpu.CompilerParams(vmem_limit_bytes=VMEM_LIMIT, dimension_semantics=("arbitrary",)),
        name="project",
        cost_estimate=cost(tokens, last),
    )(deep_at[3], *block_operands(hidden, last), ab, c, cd, scale, keep)

    pieces = lax.all_to_all(gram, "seq", 0, 0, tiled=True)
    piece = jnp.sum(pieces.reshape(seq, 128 * pairs // seq, 128), axis=0)
    gram = lax.all_to_all(jnp.broadcast_to(piece, (seq,) + piece.shape), "seq", 0, 0).reshape(128 * pairs, 128)

    return pl.pallas_call(
        functools.partial(factor_kernel, root_length),
        out_shape=[
            jax.ShapeDtypeStruct((heads, tokens, 2 * RANK), BF16),
            jax.ShapeDtypeStruct((heads, 128, 2 * RANK), F32),
        ],
        compiler_params=pltpu.CompilerParams(vmem_limit_bytes=40 << 20),
        name="factor",
        cost_estimate=pl.CostEstimate(flops=10**9, bytes_accessed=4 << 20, transcendentals=0),
    )(gram, start, high, low)


def solution(mesh):
    return jax.shard_map(
        shards,
        mesh=mesh,
        in_specs=(
            P(("batch", "seq"), None),
            P(("batch", "seq")),
            P("seq", "head", None),
            P(("batch", "seq"), "head"),
            P("head", None, None, None),
        ),
        out_specs=(P("head", ("batch", "seq"), None), P(("batch", "head"), None, None)),
        check_vma=False,
    )
```

```python
import functools
import math

import jax
import jax.numpy as jnp
from jax import lax
from jax.experimental import pallas as pl
from jax.experimental.pallas import tpu as pltpu
from jax.sharding import PartitionSpec as P

GROUP = 64
RANK = 64
RING = 4
STEPS = 4
PERMUTED = 512
DEEP = 256
WIDE = 256
UNROLL = 4
VMEM_LIMIT = 56 << 20
F32 = jnp.float32
BF16 = jnp.bfloat16
HIGHEST = lax.Precision.HIGHEST

SINE = [(-1) ** n * (2.0 * math.pi) ** (2 * n + 1) / math.factorial(2 * n + 1) for n in range(7)]


def split(x):
    high = x.astype(BF16)
    low = (x - high.astype(F32)).astype(BF16)
    return high, low


def sine_of_cycles(u):
    r = u - jnp.floor(u + 0.5)
    r = jnp.where(r > 0.25, 0.5 - r, jnp.where(r < -0.25, -0.5 - r, r))
    t = r * r
    p = jnp.full_like(t, SINE[-1])
    for c in SINE[-2::-1]:
        p = p * t + c
    return r * p


def dot(a, b, contract):
    return lax.dot_general(
        a, b, ((contract[:1], contract[1:]), ((), ())), precision=HIGHEST, preferred_element_type=F32
    )


def three_products(x, w):
    xh, xl = split(x)
    wh, wl = split(w)
    return jnp.dot(
        jnp.concatenate([xh, xl, xh], axis=1),
        jnp.concatenate([wh, wh, wl], axis=0),
        preferred_element_type=F32,
    )


def residual(kv, keep):
    step = jnp.max(jnp.abs(kv), axis=0, keepdims=True) / 7.0 + 1e-06
    return sine_of_cycles(kv * (1.0 / step)) * keep


def accumulate_kernel(shapes, first, *refs):
    refs = list(refs[1:])
    out_ref = refs.pop()
    if not first:
        base_ref = refs.pop()

    @pl.when(pl.program_id(0) == 0)
    def _():
        out_ref[...] = jnp.zeros_like(out_ref) if first else base_ref[...]

    total = None
    for parts in shapes:
        xs, refs = refs[:parts], refs[parts:]
        w_ref = refs.pop(0)
        x = xs[0][...] if parts == 1 else jnp.concatenate([r[...] for r in xs], axis=1)
        term = three_products(x, w_ref[...])
        total = term if total is None else total + term
    out_ref[...] += total


def block_specs(tokens, blocks):
    specs, at = [], 0
    for w, parts in blocks:
        rows = w.shape[0] // STEPS
        for i in range(parts):
            specs.append(
                pl.BlockSpec((tokens, rows // parts), lambda j, ix, a=at, n=parts, i=i: (0, ix[a + j * n + i]))
            )
        specs.append(pl.BlockSpec((rows, w.shape[1]), lambda j, ix: (j, 0)))
        at += STEPS * parts
    return specs


def block_operands(hidden, blocks):
    return [x for w, parts in blocks for x in [hidden] * parts + [w]]


def cost(tokens, blocks):
    macs = sum(w.size for w, _ in blocks) * tokens
    return pl.CostEstimate(
        flops=6 * macs, bytes_accessed=sum(4 * w.size + 4 * tokens * w.shape[0] for w, _ in blocks), transcendentals=0
    )


def accumulate(name, hidden, total, index, blocks):
    tokens = hidden.shape[0]
    cols = blocks[0][0].shape[1]
    whole = pl.BlockSpec((tokens, cols), lambda j, ix: (0, 0))
    return pl.pallas_call(
        functools.partial(accumulate_kernel, [parts for _, parts in blocks], total is None),
        grid_spec=pltpu.PrefetchScalarGridSpec(
            num_scalar_prefetch=1,
            grid=(STEPS,),
            in_specs=block_specs(tokens, blocks) + ([] if total is None else [whole]),
            out_specs=whole,
        ),
        out_shape=jax.ShapeDtypeStruct((tokens, cols), F32),
        compiler_params=pltpu.CompilerParams(vmem_limit_bytes=VMEM_LIMIT, dimension_semantics=("arbitrary",)),
        name=name,
        cost_estimate=cost(tokens, blocks),
    )(index, *block_operands(hidden, blocks), *([] if total is None else [total]))


def accumulate_all_kernel(x_ref, w_ref, out_ref):
    @pl.when(pl.program_id(0) == 0)
    def _():
        out_ref[...] = jnp.zeros_like(out_ref)

    batch, shards_in, quarter, cols = w_ref.shape
    rows = batch * quarter
    for s in range(shards_in):
        out_ref[...] += three_products(x_ref[:, s * rows : s * rows + rows], w_ref[:, s].reshape(rows, cols))


def accumulate_all(hidden, weight):
    tokens = hidden.shape[0]
    batch, seq, quarter, cols = weight.shape
    return pl.pallas_call(
        accumulate_all_kernel,
        grid=(seq // 2,),
        in_specs=[
            pl.BlockSpec((tokens, 2 * batch * quarter), lambda k: (0, k)),
            pl.BlockSpec((batch, 2, quarter, cols), lambda k: (0, k, 0, 0)),
        ],
        out_specs=pl.BlockSpec((tokens, cols), lambda k: (0, 0)),
        out_shape=jax.ShapeDtypeStruct((tokens, cols), F32),
        compiler_params=pltpu.CompilerParams(vmem_limit_bytes=VMEM_LIMIT, dimension_semantics=("arbitrary",)),
        name="rest",
        cost_estimate=pl.CostEstimate(
            flops=6 * tokens * weight.size, bytes_accessed=4 * (weight.size + hidden.size), transcendentals=0
        ),
    )(hidden, weight)


def project_kernel(index_ref, xa, wa, xb, wb, xc0, xc1, xc2, xc3, wc, ab_ref, c_ref, rest_ref, scale_ref, keep_ref,
                   high_ref, low_ref, gram_ref, ab_acc, c_acc):
    step = pl.program_id(0)

    @pl.when(step == 0)
    def _():
        ab_acc[...] = ab_ref[...]
        c_acc[...] = c_ref[...]

    ab_acc[...] += three_products(xa[...], wa[...]) + three_products(xb[...], wb[...])
    c_acc[...] += three_products(jnp.concatenate([xc0[...], xc1[...], xc2[...], xc3[...]], axis=1), wc[...])

    @pl.when(step == STEPS - 1)
    def _():
        epilogue((ab_acc, c_acc, rest_ref), scale_ref, keep_ref, high_ref, low_ref, gram_ref)


def epilogue(parts, scale_ref, keep_ref, high_ref, low_ref, gram_ref):
    tokens = scale_ref.shape[0]
    at = 0
    for part in parts:
        for first in range(0, part.shape[1], WIDE):
            here = slice(at, at + WIDE)

            @pl.loop(0, tokens // GROUP, unroll=UNROLL)
            def _(g, part=part, first=first, here=here):
                rows = pl.ds(pl.multiple_of(g * GROUP, GROUP), GROUP)
                kv = part[rows, first : first + WIDE] * scale_ref[rows, :]
                keep = keep_ref[pl.ds(pl.multiple_of(g * 8, 8), 8), here][:1]
                rh, rl = split(residual(kv, keep))
                high_ref[rows, here] = rh
                low_ref[rows, here] = rl

            for cols in [slice(c, c + 128) for c in range(at, at + WIDE, 128)]:
                rh = high_ref[:, cols]
                both = lax.dot_general(
                    rh,
                    jnp.concatenate([rh, low_ref[:, cols]], axis=1),
                    (((0,), (0,)), ((), ())),
                    preferred_element_type=F32,
                )
                cross = both[:, 128:]
                gram_ref[cols, :] = both[:, :128] + (cross + cross.T)
            at += WIDE


def inverse_factors(grams):
    n = len(grams)
    lane = lax.broadcasted_iota(jnp.int32, (RANK, 128), 1)
    row = lax.broadcasted_iota(jnp.int32, (RANK, 128), 0)
    unit = jnp.where(lane - RANK == row, 1.0, 0.0).astype(F32)
    full = jnp.stack([jnp.where(lane < RANK, g, unit) for g in grams])
    blocks = [full[:, 8 * i : 8 * i + 8, :] for i in range(RANK // 8)]
    sub = lax.broadcasted_iota(jnp.int32, (n, 8, 1), 1)
    for j in range(RANK):
        jb, js = divmod(j, 8)
        pivot_row = blocks[jb][:, js : js + 1, :]
        scaled = pivot_row * (1.0 / pivot_row[:, :, j : j + 1])
        for i in range(jb, RANK // 8):
            column = blocks[i][:, :, j : j + 1]
            if i == jb:
                column = jnp.where(sub > js, column, 0.0)
            blocks[i] = blocks[i] - column * scaled
    full = jnp.concatenate(blocks, axis=1)
    out = []
    for p in range(n):
        a = full[p]
        pivots = jnp.sum(jnp.where(lane == row, a, 0.0), axis=1, keepdims=True)
        out.append(jnp.where(lane < RANK, 0.0, a) * lax.rsqrt(pivots))
    return out


def basis_start_kernel(sign_ref, out_ref):
    pairs = sign_ref.shape[0]
    inverses = inverse_factors([dot(sign_ref[p], sign_ref[p], (0, 0))[:RANK] for p in range(pairs)])
    for p in range(pairs):
        out_ref[p] = dot(sign_ref[p], jnp.concatenate([inverses[p]] * 2, axis=0), (1, 1))


def factor_kernel(root_length, gram_ref, start_ref, high_ref, low_ref, left_ref, right_ref):
    pairs = start_ref.shape[0]
    eye = lax.broadcasted_iota(jnp.int32, (128, 128), 0) == lax.broadcasted_iota(jnp.int32, (128, 128), 1)
    scales, ys, zs, grams = [], [], [], []
    for p in range(pairs):
        g = gram_ref[128 * p : 128 * p + 128, :]
        size = jnp.sum(jnp.sum(jnp.where(eye, g, 0.0), axis=1, keepdims=True), axis=0, keepdims=True) / 128.0
        g = g * (1.0 / size)
        y = dot(g, start_ref[p], (1, 0))
        z = dot(g, y, (1, 0))
        scales.append(size)
        ys.append(y)
        zs.append(z)
        grams.append(dot(y, z, (0, 0))[:RANK])
    inverses = inverse_factors(grams)
    zero = jnp.zeros((RANK, 128), F32)
    for h in range(pairs // 2):
        tops, rights = [], None
        for e in range(2):
            p = 2 * h + e
            wide = jnp.concatenate([inverses[p], zero] if e == 0 else [zero, inverses[p]], axis=0)
            tops.append(dot(ys[p], wide, (1, 1)) * (lax.rsqrt(scales[p]) * root_length))
            part = dot(zs[p], wide, (1, 1)) * (jnp.sqrt(scales[p]) * (1.0 / root_length))
            rights = part if rights is None else rights + part
        right_ref[h] = rights
        th, tl = split(jnp.concatenate(tops, axis=0))
        cols = slice(256 * h, 256 * h + 256)
        rh = high_ref[:, cols]
        rl = low_ref[:, cols]
        left_ref[h] = jnp.dot(
            jnp.concatenate([rh, rl, rh], axis=1),
            jnp.concatenate([th, th, tl], axis=0),
            preferred_element_type=F32,
        ).astype(BF16)


def partner(v, head, which):
    near, far = v ^ 1, 3 - v
    return jnp.where(head == which, near, far)


def around(v, head):
    second = partner(v, head, 1)
    return [v, partner(v, head, 0), second, partner(second, head, 0)]


def flat_partner(v, head, which):
    return (v ^ 1) if head == which else 3 - v


def plane_pairs(axis, which):
    pairs = []
    for h in range(2):
        for x in range(RING):
            for y in range(RING):
                tx, ty = (flat_partner(x, h, which), y) if axis == "x" else (x, flat_partner(y, h, which))
                pairs.append(((h * RING + x) * RING + y, (h * RING + tx) * RING + ty))
    return pairs


def depth_pairs(which):
    return [(z * 2 + h, flat_partner(z, h, which) * 2 + h) for z in range(RING) for h in range(2)]


def send(v, axis, which):
    if axis == "z":
        return lax.ppermute(v, ("batch", "head"), depth_pairs(which))
    return lax.ppermute(v, ("head", "seq"), plane_pairs(axis, which))


def gather_blocks(weight, deep, multiply, early):
    barrier = lax.optimization_barrier
    join = lambda a, b: jnp.concatenate([a, b], axis=0)
    half = weight.shape[0] // 2
    a, b = weight[:half], weight[half:]
    for which in range(2):
        a, b = barrier((a, b))
        came = send(a, "x", which), send(b, "y", which)
        if which:
            came, early = barrier((came, early))
        else:
            came = barrier(came)
        a, b = join(a, came[0]), join(b, came[1])
    plane0 = barrier((a, b))
    to_y_x = lambda blocks, which: (send(blocks[0], "y", which), send(blocks[1], "x", which))
    plane1 = to_y_x(plane0, 0)
    plane = multiply(None, plane0, 0)
    deep0, plane0, plane = barrier((deep, plane0, plane))
    deep1 = send(deep0, "z", 0)
    depth = multiply(None, (deep0,), 0)
    plane1, plane0, plane, depth = barrier((plane1, plane0, plane, depth))
    plane2 = to_y_x(plane0, 1)
    plane = multiply(plane, plane1, 1)
    deep1, deep0, plane = barrier((deep1, deep0, plane))
    deep2 = send(deep0, "z", 1)
    depth = multiply(depth, (deep1,), 1)
    plane2, plane1, depth = barrier((plane2, plane1, depth))
    plane3 = to_y_x(plane1, 1)
    plane = multiply(plane, plane2, 2)
    deep2, deep1, plane = barrier((deep2, deep1, plane))
    deep3 = send(deep1, "z", 1)
    depth = multiply(depth, (deep2,), 2)
    return (*plane3, deep3), (plane, depth), early


def shards(hidden, row_scale, key_value_weight, outlier, sketch_sign_flags):
    tokens, width = hidden.shape
    rows, heads, kv_cols = key_value_weight.shape
    cols = heads * kv_cols
    pairs = 2 * heads
    groups = outlier.shape[0]
    seq = lax.axis_size("seq")
    root_length = math.sqrt(tokens * seq)

    signs = (2 * sketch_sign_flags - 1).astype(F32).reshape(pairs, 128, RANK)
    start = pl.pallas_call(
        basis_start_kernel,
        out_shape=jax.ShapeDtypeStruct((pairs, 128, 128), F32),
        name="start",
        cost_estimate=pl.CostEstimate(flops=10**8, bytes_accessed=10**6, transcendentals=0),
    )(jnp.concatenate([signs, signs], axis=2))

    head, place, plane = lax.axis_index("head"), lax.axis_index("seq"), lax.axis_index("batch")
    xs, ys, zs = around(place // RING, head), around(place % RING, head), around(plane, head)
    shard = lambda x, y: x * RING + y
    plane_index = [
        (jnp.stack([2 * shard(x, ys[k]) for x in xs]), jnp.stack([2 * shard(xs[k], y) + 1 for y in ys]))
        for k in range(RING)
    ]
    deep_index = [(jnp.arange(seq, dtype=jnp.int32) * RING + zs[k],) for k in range(RING)]
    joined = lambda *lists: jnp.concatenate([i for indices in lists for i in indices])
    plane_at = [joined(i) for i in plane_index]
    deep_at = [joined(i) for i in deep_index]
    last_at = joined(plane_index[3], deep_index[3])
    scale = row_scale[:, None]
    keep = jnp.repeat(jnp.repeat((1 - outlier).astype(F32), kv_cols, axis=1), 8, axis=0)

    def multiply(total, blocks, k):
        kind, parts, at = ("plane", 1, plane_at) if len(blocks) == 2 else ("deep", RING, deep_at)
        return accumulate(kind + str(k), hidden, total, at[k], [(w, parts) for w in blocks])

    flat = key_value_weight.reshape(rows, cols)
    quarter = rows // RING
    rest_at = PERMUTED + DEEP
    own = lax.dynamic_slice_in_dim(flat[:, PERMUTED:], plane * quarter, quarter, 0)
    deep = jnp.broadcast_to(own[:, :DEEP], (seq, quarter, DEEP))
    deep = lax.all_to_all(deep, "seq", 0, 0).reshape(seq * quarter, DEEP)
    rest = lax.all_gather(own[:, DEEP:], ("batch", "seq"), axis=0).reshape(RING, seq, quarter, cols - rest_at)
    early = (start, scale, keep, last_at)
    (a3, b3, c3), (ab, c), (start, scale, keep, last_at) = gather_blocks(flat[:, :PERMUTED], deep, multiply, early)
    rest, ab, c = lax.optimization_barrier((rest, ab, c))
    cd = accumulate_all(hidden, rest)

    last = [(a3, 1), (b3, 1), (c3, RING)]
    specs = block_specs(tokens, last)
    whole = lambda *shape: pl.BlockSpec(shape, lambda j, ix: (0,) * len(shape))
    high, low, gram = pl.pallas_call(
        project_kernel,
        grid_spec=pltpu.PrefetchScalarGridSpec(
            num_scalar_prefetch=1,
            grid=(STEPS,),
            in_specs=specs
            + [whole(tokens, t.shape[1]) for t in (ab, c, cd)]
            + [whole(tokens, 1), whole(8 * groups, cols)],
            out_specs=[whole(tokens, cols), whole(tokens, cols), whole(128 * pairs, 128)],
            scratch_shapes=[pltpu.VMEM(ab.shape, F32), pltpu.VMEM(c.shape, F32)],
        ),
        out_shape=[
            jax.ShapeDtypeStruct((tokens, cols), BF16),
            jax.ShapeDtypeStruct((tokens, cols), BF16),
            jax.ShapeDtypeStruct((128 * pairs, 128), F32),
        ],
        compiler_params=pltpu.CompilerParams(vmem_limit_bytes=VMEM_LIMIT, dimension_semantics=("arbitrary",)),
        name="project",
        cost_estimate=cost(tokens, last),
    )(last_at, *block_operands(hidden, last), ab, c, cd, scale, keep)

    pieces = lax.all_to_all(gram, "seq", 0, 0, tiled=True)
    piece = jnp.sum(pieces.reshape(seq, 128 * pairs // seq, 128), axis=0)
    gram = lax.all_to_all(jnp.broadcast_to(piece, (seq,) + piece.shape), "seq", 0, 0).reshape(128 * pairs, 128)

    return pl.pallas_call(
        functools.partial(factor_kernel, root_length),
        out_shape=[
            jax.ShapeDtypeStruct((heads, tokens, 2 * RANK), BF16),
            jax.ShapeDtypeStruct((heads, 128, 2 * RANK), F32),
        ],
        compiler_params=pltpu.CompilerParams(vmem_limit_bytes=40 << 20),
        name="factor",
        cost_estimate=pl.CostEstimate(flops=10**9, bytes_accessed=4 << 20, transcendentals=0),
    )(gram, start, high, low)


def solution(mesh):
    return jax.shard_map(
        shards,
        mesh=mesh,
        in_specs=(
            P(("batch", "seq"), None),
            P(("batch", "seq")),
            P("seq", "head", None),
            P(("batch", "seq"), "head"),
            P("head", None, None, None),
        ),
        out_specs=(P("head", ("batch", "seq"), None), P(("batch", "head"), None, None)),
        check_vma=False,
    )
```

```python
import functools
import math

import jax
import jax.numpy as jnp
from jax import lax
from jax.experimental import pallas as pl
from jax.experimental.pallas import tpu as pltpu
from jax.sharding import PartitionSpec as P

GROUP = 64
RANK = 64
RING = 4
STEPS = 4
PERMUTED = 512
DEEP = 256
WIDE = 256
UNROLL = 4
VMEM_LIMIT = 56 << 20
F32 = jnp.float32
BF16 = jnp.bfloat16
HIGHEST = lax.Precision.HIGHEST

SINE = [(-1) ** n * (2.0 * math.pi) ** (2 * n + 1) / math.factorial(2 * n + 1) for n in range(7)]


def split(x):
    high = x.astype(BF16)
    low = (x - high.astype(F32)).astype(BF16)
    return high, low


def sine_of_cycles(u):
    r = u - jnp.floor(u + 0.5)
    r = jnp.where(r > 0.25, 0.5 - r, jnp.where(r < -0.25, -0.5 - r, r))
    t = r * r
    p = jnp.full_like(t, SINE[-1])
    for c in SINE[-2::-1]:
        p = p * t + c
    return r * p


def dot(a, b, contract):
    return lax.dot_general(
        a, b, ((contract[:1], contract[1:]), ((), ())), precision=HIGHEST, preferred_element_type=F32
    )


def three_products(x, w):
    xh, xl = split(x)
    wh, wl = split(w)
    return jnp.dot(
        jnp.concatenate([xh, xl, xh], axis=1),
        jnp.concatenate([wh, wh, wl], axis=0),
        preferred_element_type=F32,
    )


def residual(kv, keep):
    step = jnp.max(jnp.abs(kv), axis=0, keepdims=True) / 7.0 + 1e-06
    return sine_of_cycles(kv * (1.0 / step)) * keep


def accumulate_kernel(shapes, first, *refs):
    refs = list(refs[1:])
    out_ref = refs.pop()
    if not first:
        base_ref = refs.pop()

    @pl.when(pl.program_id(0) == 0)
    def _():
        out_ref[...] = jnp.zeros_like(out_ref) if first else base_ref[...]

    total = None
    for parts in shapes:
        xs, refs = refs[:parts], refs[parts:]
        w_ref = refs.pop(0)
        x = xs[0][...] if parts == 1 else jnp.concatenate([r[...] for r in xs], axis=1)
        term = three_products(x, w_ref[...])
        total = term if total is None else total + term
    out_ref[...] += total


def block_specs(tokens, blocks):
    specs, at = [], 0
    for w, parts in blocks:
        rows = w.shape[0] // STEPS
        for i in range(parts):
            specs.append(
                pl.BlockSpec((tokens, rows // parts), lambda j, ix, a=at, n=parts, i=i: (0, ix[a + j * n + i]))
            )
        specs.append(pl.BlockSpec((rows, w.shape[1]), lambda j, ix: (j, 0)))
        at += STEPS * parts
    return specs


def block_operands(hidden, blocks):
    return [x for w, parts in blocks for x in [hidden] * parts + [w]]


def cost(tokens, blocks):
    macs = sum(w.size for w, _ in blocks) * tokens
    return pl.CostEstimate(
        flops=6 * macs, bytes_accessed=sum(4 * w.size + 4 * tokens * w.shape[0] for w, _ in blocks), transcendentals=0
    )


def accumulate(name, hidden, total, index, blocks):
    tokens = hidden.shape[0]
    cols = blocks[0][0].shape[1]
    whole = pl.BlockSpec((tokens, cols), lambda j, ix: (0, 0))
    return pl.pallas_call(
        functools.partial(accumulate_kernel, [parts for _, parts in blocks], total is None),
        grid_spec=pltpu.PrefetchScalarGridSpec(
            num_scalar_prefetch=1,
            grid=(STEPS,),
            in_specs=block_specs(tokens, blocks) + ([] if total is None else [whole]),
            out_specs=whole,
        ),
        out_shape=jax.ShapeDtypeStruct((tokens, cols), F32),
        compiler_params=pltpu.CompilerParams(vmem_limit_bytes=VMEM_LIMIT, dimension_semantics=("arbitrary",)),
        name=name,
        cost_estimate=cost(tokens, blocks),
    )(index, *block_operands(hidden, blocks), *([] if total is None else [total]))


def accumulate_all_kernel(x_ref, w_ref, out_ref):
    @pl.when(pl.program_id(0) == 0)
    def _():
        out_ref[...] = jnp.zeros_like(out_ref)

    batch, shards_in, quarter, cols = w_ref.shape
    rows = batch * quarter
    for s in range(shards_in):
        out_ref[...] += three_products(x_ref[:, s * rows : s * rows + rows], w_ref[:, s].reshape(rows, cols))


def accumulate_all(hidden, weight):
    tokens = hidden.shape[0]
    batch, seq, quarter, cols = weight.shape
    return pl.pallas_call(
        accumulate_all_kernel,
        grid=(seq // 2,),
        in_specs=[
            pl.BlockSpec((tokens, 2 * batch * quarter), lambda k: (0, k)),
            pl.BlockSpec((batch, 2, quarter, cols), lambda k: (0, k, 0, 0)),
        ],
        out_specs=pl.BlockSpec((tokens, cols), lambda k: (0, 0)),
        out_shape=jax.ShapeDtypeStruct((tokens, cols), F32),
        compiler_params=pltpu.CompilerParams(vmem_limit_bytes=VMEM_LIMIT, dimension_semantics=("arbitrary",)),
        name="rest",
        cost_estimate=pl.CostEstimate(
            flops=6 * tokens * weight.size, bytes_accessed=4 * (weight.size + hidden.size), transcendentals=0
        ),
    )(hidden, weight)


def project_kernel(index_ref, x0, x1, x2, x3, w, plane_ref, depth_ref, rest_ref, scale_ref, keep_ref,
                   high_ref, low_ref, gram_ref, depth_acc):
    step = pl.program_id(0)

    @pl.when(step == 0)
    def _():
        depth_acc[...] = depth_ref[...]

    depth_acc[...] += three_products(jnp.concatenate([x0[...], x1[...], x2[...], x3[...]], axis=1), w[...])

    @pl.when(step == STEPS - 1)
    def _():
        epilogue((plane_ref, depth_acc, rest_ref), scale_ref, keep_ref, high_ref, low_ref, gram_ref)


def epilogue(parts, scale_ref, keep_ref, high_ref, low_ref, gram_ref):
    tokens = scale_ref.shape[0]
    at = 0
    for part in parts:
        for first in range(0, part.shape[1], WIDE):
            here = slice(at, at + WIDE)

            @pl.loop(0, tokens // GROUP, unroll=UNROLL)
            def _(g, part=part, first=first, here=here):
                rows = pl.ds(pl.multiple_of(g * GROUP, GROUP), GROUP)
                kv = part[rows, first : first + WIDE] * scale_ref[rows, :]
                keep = keep_ref[pl.ds(pl.multiple_of(g * 8, 8), 8), here][:1]
                rh, rl = split(residual(kv, keep))
                high_ref[rows, here] = rh
                low_ref[rows, here] = rl

            for cols in [slice(c, c + 128) for c in range(at, at + WIDE, 128)]:
                rh = high_ref[:, cols]
                both = lax.dot_general(
                    rh,
                    jnp.concatenate([rh, low_ref[:, cols]], axis=1),
                    (((0,), (0,)), ((), ())),
                    preferred_element_type=F32,
                )
                cross = both[:, 128:]
                gram_ref[cols, :] = both[:, :128] + (cross + cross.T)
            at += WIDE


def inverse_factors(grams):
    n = len(grams)
    lane = lax.broadcasted_iota(jnp.int32, (RANK, 128), 1)
    row = lax.broadcasted_iota(jnp.int32, (RANK, 128), 0)
    unit = jnp.where(lane - RANK == row, 1.0, 0.0).astype(F32)
    full = jnp.stack([jnp.where(lane < RANK, g, unit) for g in grams])
    blocks = [full[:, 8 * i : 8 * i + 8, :] for i in range(RANK // 8)]
    sub = lax.broadcasted_iota(jnp.int32, (n, 8, 1), 1)
    for j in range(RANK):
        jb, js = divmod(j, 8)
        pivot_row = blocks[jb][:, js : js + 1, :]
        scaled = pivot_row * (1.0 / pivot_row[:, :, j : j + 1])
        for i in range(jb, RANK // 8):
            column = blocks[i][:, :, j : j + 1]
            if i == jb:
                column = jnp.where(sub > js, column, 0.0)
            blocks[i] = blocks[i] - column * scaled
    full = jnp.concatenate(blocks, axis=1)
    out = []
    for p in range(n):
        a = full[p]
        pivots = jnp.sum(jnp.where(lane == row, a, 0.0), axis=1, keepdims=True)
        out.append(jnp.where(lane < RANK, 0.0, a) * lax.rsqrt(pivots))
    return out


def basis_start_kernel(sign_ref, out_ref):
    pairs = sign_ref.shape[0]
    inverses = inverse_factors([dot(sign_ref[p], sign_ref[p], (0, 0))[:RANK] for p in range(pairs)])
    for p in range(pairs):
        out_ref[p] = dot(sign_ref[p], jnp.concatenate([inverses[p]] * 2, axis=0), (1, 1))


def factor_kernel(root_length, gram_ref, start_ref, high_ref, low_ref, left_ref, right_ref):
    pairs = start_ref.shape[0]
    eye = lax.broadcasted_iota(jnp.int32, (128, 128), 0) == lax.broadcasted_iota(jnp.int32, (128, 128), 1)
    scales, ys, zs, grams = [], [], [], []
    for p in range(pairs):
        g = gram_ref[128 * p : 128 * p + 128, :]
        size = jnp.sum(jnp.sum(jnp.where(eye, g, 0.0), axis=1, keepdims=True), axis=0, keepdims=True) / 128.0
        g = g * (1.0 / size)
        y = dot(g, start_ref[p], (1, 0))
        z = dot(g, y, (1, 0))
        scales.append(size)
        ys.append(y)
        zs.append(z)
        grams.append(dot(y, z, (0, 0))[:RANK])
    inverses = inverse_factors(grams)
    zero = jnp.zeros((RANK, 128), F32)
    for h in range(pairs // 2):
        tops, rights = [], None
        for e in range(2):
            p = 2 * h + e
            wide = jnp.concatenate([inverses[p], zero] if e == 0 else [zero, inverses[p]], axis=0)
            tops.append(dot(ys[p], wide, (1, 1)) * (lax.rsqrt(scales[p]) * root_length))
            part = dot(zs[p], wide, (1, 1)) * (jnp.sqrt(scales[p]) * (1.0 / root_length))
            rights = part if rights is None else rights + part
        right_ref[h] = rights
        th, tl = split(jnp.concatenate(tops, axis=0))
        cols = slice(256 * h, 256 * h + 256)
        rh = high_ref[:, cols]
        rl = low_ref[:, cols]
        left_ref[h] = jnp.dot(
            jnp.concatenate([rh, rl, rh], axis=1),
            jnp.concatenate([th, th, tl], axis=0),
            preferred_element_type=F32,
        ).astype(BF16)


def partner(v, head, which):
    near, far = v ^ 1, 3 - v
    return jnp.where(head == which, near, far)


def around(v, head):
    second = partner(v, head, 1)
    return [v, partner(v, head, 0), second, partner(second, head, 0)]


def flat_partner(v, head, which):
    return (v ^ 1) if head == which else 3 - v


def plane_pairs(axis, which):
    pairs = []
    for h in range(2):
        for x in range(RING):
            for y in range(RING):
                tx, ty = (flat_partner(x, h, which), y) if axis == "x" else (x, flat_partner(y, h, which))
                pairs.append(((h * RING + x) * RING + y, (h * RING + tx) * RING + ty))
    return pairs


def depth_pairs(which):
    return [(z * 2 + h, flat_partner(z, h, which) * 2 + h) for z in range(RING) for h in range(2)]


def send(v, axis, which):
    if axis == "z":
        return lax.ppermute(v, ("batch", "head"), depth_pairs(which))
    return lax.ppermute(v, ("head", "seq"), plane_pairs(axis, which))


def gather_blocks(weight, deep, multiply, early):
    barrier = lax.optimization_barrier
    join = lambda a, b: jnp.concatenate([a, b], axis=0)
    half = weight.shape[0] // 2
    a, b = weight[:half], weight[half:]
    for which in range(2):
        a, b = barrier((a, b))
        came = send(a, "x", which), send(b, "y", which)
        if which:
            came, early = barrier((came, early))
        else:
            came = barrier(came)
        a, b = join(a, came[0]), join(b, came[1])
    plane0 = barrier((a, b))
    to_y_x = lambda blocks, which: (send(blocks[0], "y", which), send(blocks[1], "x", which))
    plane1 = to_y_x(plane0, 0)
    plane = multiply(None, plane0, 0)
    deep0, plane0, plane = barrier((deep, plane0, plane))
    deep1 = send(deep0, "z", 0)
    depth = multiply(None, (deep0,), 0)
    plane1, plane0, plane, depth = barrier((plane1, plane0, plane, depth))
    plane2 = to_y_x(plane0, 1)
    plane = multiply(plane, plane1, 1)
    deep1, deep0, plane = barrier((deep1, deep0, plane))
    deep2 = send(deep0, "z", 1)
    depth = multiply(depth, (deep1,), 1)
    plane2, plane1, depth = barrier((plane2, plane1, depth))
    plane3 = to_y_x(plane1, 1)
    plane = multiply(plane, plane2, 2)
    deep2, deep1, plane = barrier((deep2, deep1, plane))
    deep3 = send(deep1, "z", 1)
    depth = multiply(depth, (deep2,), 2)
    plane3, plane, depth = barrier((plane3, plane, depth))
    plane = multiply(plane, plane3, 3)
    return deep3, plane, depth, early


def shards(hidden, row_scale, key_value_weight, outlier, sketch_sign_flags):
    tokens, width = hidden.shape
    rows, heads, kv_cols = key_value_weight.shape
    cols = heads * kv_cols
    pairs = 2 * heads
    groups = outlier.shape[0]
    seq = lax.axis_size("seq")
    root_length = math.sqrt(tokens * seq)

    signs = (2 * sketch_sign_flags - 1).astype(F32).reshape(pairs, 128, RANK)
    start = pl.pallas_call(
        basis_start_kernel,
        out_shape=jax.ShapeDtypeStruct((pairs, 128, 128), F32),
        name="start",
        cost_estimate=pl.CostEstimate(flops=10**8, bytes_accessed=10**6, transcendentals=0),
    )(jnp.concatenate([signs, signs], axis=2))

    head, place, plane = lax.axis_index("head"), lax.axis_index("seq"), lax.axis_index("batch")
    xs, ys, zs = around(place // RING, head), around(place % RING, head), around(plane, head)
    shard = lambda x, y: x * RING + y
    plane_index = [
        (jnp.stack([2 * shard(x, ys[k]) for x in xs]), jnp.stack([2 * shard(xs[k], y) + 1 for y in ys]))
        for k in range(RING)
    ]
    deep_index = [(jnp.arange(seq, dtype=jnp.int32) * RING + zs[k],) for k in range(RING)]
    joined = lambda *lists: jnp.concatenate([i for indices in lists for i in indices])
    plane_at = [joined(i) for i in plane_index]
    deep_at = [joined(i) for i in deep_index]
    scale = row_scale[:, None]
    keep = jnp.repeat(jnp.repeat((1 - outlier).astype(F32), kv_cols, axis=1), 8, axis=0)

    def multiply(total, blocks, k):
        kind, parts, at = ("plane", 1, plane_at) if len(blocks) == 2 else ("deep", RING, deep_at)
        return accumulate(kind + str(k), hidden, total, at[k], [(w, parts) for w in blocks])

    flat = key_value_weight.reshape(rows, cols)
    quarter = rows // RING
    rest_at = PERMUTED + DEEP
    own = lax.dynamic_slice_in_dim(flat[:, PERMUTED:], plane * quarter, quarter, 0)
    deep = lax.all_gather(own[:, :DEEP], "seq", axis=0, tiled=True)
    own, _ = lax.optimization_barrier((own[:, DEEP:], own))
    rest = lax.all_gather(own, ("batch", "seq"), axis=0).reshape(RING, seq, quarter, cols - rest_at)
    early = (start, scale, keep)
    deep3, ab, c, (start, scale, keep) = gather_blocks(flat[:, :PERMUTED], deep, multiply, early)
    rest, ab, c = lax.optimization_barrier((rest, ab, c))
    cd = accumulate_all(hidden, rest)

    last = [(deep3, RING)]
    specs = block_specs(tokens, last)
    whole = lambda *shape: pl.BlockSpec(shape, lambda j, ix: (0,) * len(shape))
    high, low, gram = pl.pallas_call(
        project_kernel,
        grid_spec=pltpu.PrefetchScalarGridSpec(
            num_scalar_prefetch=1,
            grid=(STEPS,),
            in_specs=specs
            + [whole(tokens, t.shape[1]) for t in (ab, c, cd)]
            + [whole(tokens, 1), whole(8 * groups, cols)],
            out_specs=[whole(tokens, cols), whole(tokens, cols), whole(128 * pairs, 128)],
            scratch_shapes=[pltpu.VMEM(c.shape, F32)],
        ),
        out_shape=[
            jax.ShapeDtypeStruct((tokens, cols), BF16),
            jax.ShapeDtypeStruct((tokens, cols), BF16),
            jax.ShapeDtypeStruct((128 * pairs, 128), F32),
        ],
        compiler_params=pltpu.CompilerParams(vmem_limit_bytes=VMEM_LIMIT, dimension_semantics=("arbitrary",)),
        name="project",
        cost_estimate=cost(tokens, last),
    )(deep_at[3], *block_operands(hidden, last), ab, c, cd, scale, keep)

    pieces = lax.all_to_all(gram, "seq", 0, 0, tiled=True)
    piece = jnp.sum(pieces.reshape(seq, 128 * pairs // seq, 128), axis=0)
    gram = lax.all_to_all(jnp.broadcast_to(piece, (seq,) + piece.shape), "seq", 0, 0).reshape(128 * pairs, 128)

    return pl.pallas_call(
        functools.partial(factor_kernel, root_length),
        out_shape=[
            jax.ShapeDtypeStruct((heads, tokens, 2 * RANK), BF16),
            jax.ShapeDtypeStruct((heads, 128, 2 * RANK), F32),
        ],
        compiler_params=pltpu.CompilerParams(vmem_limit_bytes=40 << 20),
        name="factor",
        cost_estimate=pl.CostEstimate(flops=10**9, bytes_accessed=4 << 20, transcendentals=0),
    )(gram, start, high, low)


def solution(mesh):
    return jax.shard_map(
        shards,
        mesh=mesh,
        in_specs=(
            P(("batch", "seq"), None),
            P(("batch", "seq")),
            P("seq", "head", None),
            P(("batch", "seq"), "head"),
            P("head", None, None, None),
        ),
        out_specs=(P("head", ("batch", "seq"), None), P(("batch", "head"), None, None)),
        check_vma=False,
    )
```

```python
import functools
import math

import jax
import jax.numpy as jnp
from jax import lax
from jax.experimental import pallas as pl
from jax.experimental.pallas import tpu as pltpu
from jax.sharding import PartitionSpec as P

GROUP = 64
RANK = 64
RING = 4
STEPS = 4
PERMUTED = 768
WIDE = 256
UNROLL = 4
VMEM_LIMIT = 56 << 20
F32 = jnp.float32
BF16 = jnp.bfloat16
HIGHEST = lax.Precision.HIGHEST

SINE = [(-1) ** n * (2.0 * math.pi) ** (2 * n + 1) / math.factorial(2 * n + 1) for n in range(7)]


def split(x):
    high = x.astype(BF16)
    low = (x - high.astype(F32)).astype(BF16)
    return high, low


def sine_of_cycles(u):
    r = u - jnp.floor(u + 0.5)
    r = jnp.where(r > 0.25, 0.5 - r, jnp.where(r < -0.25, -0.5 - r, r))
    t = r * r
    p = jnp.full_like(t, SINE[-1])
    for c in SINE[-2::-1]:
        p = p * t + c
    return r * p


def dot(a, b, contract):
    return lax.dot_general(
        a, b, ((contract[:1], contract[1:]), ((), ())), precision=HIGHEST, preferred_element_type=F32
    )


def three_products(x, w):
    xh, xl = split(x)
    wh, wl = split(w)
    return jnp.dot(
        jnp.concatenate([xh, xl, xh], axis=1),
        jnp.concatenate([wh, wh, wl], axis=0),
        preferred_element_type=F32,
    )


def residual(kv, keep):
    step = jnp.max(jnp.abs(kv), axis=0, keepdims=True) / 7.0 + 1e-06
    return sine_of_cycles(kv * (1.0 / step)) * keep


def accumulate_kernel(shapes, first, *refs):
    refs = list(refs[1:])
    out_ref = refs.pop()
    if not first:
        base_ref = refs.pop()

    @pl.when(pl.program_id(0) == 0)
    def _():
        out_ref[...] = jnp.zeros_like(out_ref) if first else base_ref[...]

    total = None
    for parts in shapes:
        xs, refs = refs[:parts], refs[parts:]
        w_ref = refs.pop(0)
        x = xs[0][...] if parts == 1 else jnp.concatenate([r[...] for r in xs], axis=1)
        term = three_products(x, w_ref[...])
        total = term if total is None else total + term
    out_ref[...] += total


def block_specs(tokens, blocks):
    specs, at = [], 0
    for w, parts in blocks:
        rows = w.shape[0] // STEPS
        for i in range(parts):
            specs.append(
                pl.BlockSpec((tokens, rows // parts), lambda j, ix, a=at, n=parts, i=i: (0, ix[a + j * n + i]))
            )
        specs.append(pl.BlockSpec((rows, w.shape[1]), lambda j, ix: (j, 0)))
        at += STEPS * parts
    return specs


def block_operands(hidden, blocks):
    return [x for w, parts in blocks for x in [hidden] * parts + [w]]


def cost(tokens, blocks):
    macs = sum(w.size for w, _ in blocks) * tokens
    return pl.CostEstimate(
        flops=6 * macs, bytes_accessed=sum(4 * w.size + 4 * tokens * w.shape[0] for w, _ in blocks), transcendentals=0
    )


def accumulate(name, hidden, total, index, blocks):
    tokens = hidden.shape[0]
    cols = blocks[0][0].shape[1]
    whole = pl.BlockSpec((tokens, cols), lambda j, ix: (0, 0))
    return pl.pallas_call(
        functools.partial(accumulate_kernel, [parts for _, parts in blocks], total is None),
        grid_spec=pltpu.PrefetchScalarGridSpec(
            num_scalar_prefetch=1,
            grid=(STEPS,),
            in_specs=block_specs(tokens, blocks) + ([] if total is None else [whole]),
            out_specs=whole,
        ),
        out_shape=jax.ShapeDtypeStruct((tokens, cols), F32),
        compiler_params=pltpu.CompilerParams(vmem_limit_bytes=VMEM_LIMIT, dimension_semantics=("arbitrary",)),
        name=name,
        cost_estimate=cost(tokens, blocks),
    )(index, *block_operands(hidden, blocks), *([] if total is None else [total]))


def project_kernel(index_ref, xa, wa, xb, wb, plane_ref, depth_ref, scale_ref, keep_ref, high_ref, low_ref, gram_ref, plane_acc):
    step = pl.program_id(0)

    @pl.when(step == 0)
    def _():
        plane_acc[...] = plane_ref[...]

    plane_acc[...] += three_products(xa[...], wa[...]) + three_products(xb[...], wb[...])

    @pl.when(step == STEPS - 1)
    def _():
        epilogue((plane_acc, depth_ref), scale_ref, keep_ref, high_ref, low_ref, gram_ref)


def epilogue(parts, scale_ref, keep_ref, high_ref, low_ref, gram_ref):
    tokens = scale_ref.shape[0]
    at = 0
    for part in parts:
        for first in range(0, part.shape[1], WIDE):
            here = slice(at, at + WIDE)

            @pl.loop(0, tokens // GROUP, unroll=UNROLL)
            def _(g, part=part, first=first, here=here):
                rows = pl.ds(pl.multiple_of(g * GROUP, GROUP), GROUP)
                kv = part[rows, first : first + WIDE] * scale_ref[rows, :]
                keep = keep_ref[pl.ds(pl.multiple_of(g * 8, 8), 8), here][:1]
                rh, rl = split(residual(kv, keep))
                high_ref[rows, here] = rh
                low_ref[rows, here] = rl

            for cols in [slice(c, c + 128) for c in range(at, at + WIDE, 128)]:
                rh = high_ref[:, cols]
                both = lax.dot_general(
                    rh,
                    jnp.concatenate([rh, low_ref[:, cols]], axis=1),
                    (((0,), (0,)), ((), ())),
                    preferred_element_type=F32,
                )
                cross = both[:, 128:]
                gram_ref[cols, :] = both[:, :128] + (cross + cross.T)
            at += WIDE


def inverse_factors(grams):
    n = len(grams)
    lane = lax.broadcasted_iota(jnp.int32, (RANK, 128), 1)
    row = lax.broadcasted_iota(jnp.int32, (RANK, 128), 0)
    unit = jnp.where(lane - RANK == row, 1.0, 0.0).astype(F32)
    full = jnp.stack([jnp.where(lane < RANK, g, unit) for g in grams])
    blocks = [full[:, 8 * i : 8 * i + 8, :] for i in range(RANK // 8)]
    sub = lax.broadcasted_iota(jnp.int32, (n, 8, 1), 1)
    for j in range(RANK):
        jb, js = divmod(j, 8)
        pivot_row = blocks[jb][:, js : js + 1, :]
        scaled = pivot_row * (1.0 / pivot_row[:, :, j : j + 1])
        for i in range(jb, RANK // 8):
            column = blocks[i][:, :, j : j + 1]
            if i == jb:
                column = jnp.where(sub > js, column, 0.0)
            blocks[i] = blocks[i] - column * scaled
    full = jnp.concatenate(blocks, axis=1)
    out = []
    for p in range(n):
        a = full[p]
        pivots = jnp.sum(jnp.where(lane == row, a, 0.0), axis=1, keepdims=True)
        out.append(jnp.where(lane < RANK, 0.0, a) * lax.rsqrt(pivots))
    return out


def basis_start_kernel(sign_ref, out_ref):
    pairs = sign_ref.shape[0]
    inverses = inverse_factors([dot(sign_ref[p], sign_ref[p], (0, 0))[:RANK] for p in range(pairs)])
    for p in range(pairs):
        out_ref[p] = dot(sign_ref[p], jnp.concatenate([inverses[p]] * 2, axis=0), (1, 1))


def factor_kernel(root_length, gram_ref, start_ref, high_ref, low_ref, left_ref, right_ref):
    pairs = start_ref.shape[0]
    eye = lax.broadcasted_iota(jnp.int32, (128, 128), 0) == lax.broadcasted_iota(jnp.int32, (128, 128), 1)
    scales, ys, zs, grams = [], [], [], []
    for p in range(pairs):
        g = gram_ref[128 * p : 128 * p + 128, :]
        size = jnp.sum(jnp.sum(jnp.where(eye, g, 0.0), axis=1, keepdims=True), axis=0, keepdims=True) / 128.0
        g = g * (1.0 / size)
        y = dot(g, start_ref[p], (1, 0))
        z = dot(g, y, (1, 0))
        scales.append(size)
        ys.append(y)
        zs.append(z)
        grams.append(dot(y, z, (0, 0))[:RANK])
    inverses = inverse_factors(grams)
    zero = jnp.zeros((RANK, 128), F32)
    for h in range(pairs // 2):
        tops, rights = [], None
        for e in range(2):
            p = 2 * h + e
            wide = jnp.concatenate([inverses[p], zero] if e == 0 else [zero, inverses[p]], axis=0)
            tops.append(dot(ys[p], wide, (1, 1)) * (lax.rsqrt(scales[p]) * root_length))
            part = dot(zs[p], wide, (1, 1)) * (jnp.sqrt(scales[p]) * (1.0 / root_length))
            rights = part if rights is None else rights + part
        right_ref[h] = rights
        th, tl = split(jnp.concatenate(tops, axis=0))
        cols = slice(256 * h, 256 * h + 256)
        rh = high_ref[:, cols]
        rl = low_ref[:, cols]
        left_ref[h] = jnp.dot(
            jnp.concatenate([rh, rl, rh], axis=1),
            jnp.concatenate([th, th, tl], axis=0),
            preferred_element_type=F32,
        ).astype(BF16)


def partner(v, head, which):
    near, far = v ^ 1, 3 - v
    return jnp.where(head == which, near, far)


def around(v, head):
    second = partner(v, head, 1)
    return [v, partner(v, head, 0), second, partner(second, head, 0)]


def flat_partner(v, head, which):
    return (v ^ 1) if head == which else 3 - v


def plane_pairs(axis, which):
    pairs = []
    for h in range(2):
        for x in range(RING):
            for y in range(RING):
                tx, ty = (flat_partner(x, h, which), y) if axis == "x" else (x, flat_partner(y, h, which))
                pairs.append(((h * RING + x) * RING + y, (h * RING + tx) * RING + ty))
    return pairs


def depth_pairs(which):
    return [(z * 2 + h, flat_partner(z, h, which) * 2 + h) for z in range(RING) for h in range(2)]


def send(v, axis, which):
    if axis == "z":
        return lax.ppermute(v, ("batch", "head"), depth_pairs(which))
    return lax.ppermute(v, ("head", "seq"), plane_pairs(axis, which))


def gather_blocks(weight, deep, multiply, early):
    barrier = lax.optimization_barrier
    join = lambda a, b: jnp.concatenate([a, b], axis=0)
    half = weight.shape[0] // 2
    a, b = weight[:half], weight[half:]
    for which in range(2):
        a, b = barrier((a, b))
        came = send(a, "x", which), send(b, "y", which)
        if which:
            came, early = barrier((came, early))
        else:
            came = barrier(came)
        a, b = join(a, came[0]), join(b, came[1])
    plane0 = barrier((a, b))
    to_y_x = lambda blocks, which: (send(blocks[0], "y", which), send(blocks[1], "x", which))
    plane1 = to_y_x(plane0, 0)
    plane = multiply(None, plane0, 0)
    deep0, plane0, plane = barrier((deep, plane0, plane))
    deep1 = send(deep0, "z", 0)
    depth = multiply(None, (deep0,), 0)
    plane1, plane0, plane, depth = barrier((plane1, plane0, plane, depth))
    plane2 = to_y_x(plane0, 1)
    plane = multiply(plane, plane1, 1)
    deep1, deep0, plane = barrier((deep1, deep0, plane))
    deep2 = send(deep0, "z", 1)
    depth = multiply(depth, (deep1,), 1)
    plane2, plane1, depth = barrier((plane2, plane1, depth))
    plane3 = to_y_x(plane1, 1)
    plane = multiply(plane, plane2, 2)
    deep2, deep1, plane = barrier((deep2, deep1, plane))
    deep3 = send(deep1, "z", 1)
    depth = multiply(depth, (deep2,), 2)
    deep3, depth, plane = barrier((deep3, depth, plane))
    depth = multiply(depth, (deep3,), 3)
    return plane3, plane, depth, early


def shards(hidden, row_scale, key_value_weight, outlier, sketch_sign_flags):
    tokens, width = hidden.shape
    rows, heads, kv_cols = key_value_weight.shape
    cols = heads * kv_cols
    pairs = 2 * heads
    groups = outlier.shape[0]
    seq = lax.axis_size("seq")
    root_length = math.sqrt(tokens * seq)

    signs = (2 * sketch_sign_flags - 1).astype(F32).reshape(pairs, 128, RANK)
    start = pl.pallas_call(
        basis_start_kernel,
        out_shape=jax.ShapeDtypeStruct((pairs, 128, 128), F32),
        name="start",
        cost_estimate=pl.CostEstimate(flops=10**8, bytes_accessed=10**6, transcendentals=0),
    )(jnp.concatenate([signs, signs], axis=2))

    head, place, plane = lax.axis_index("head"), lax.axis_index("seq"), lax.axis_index("batch")
    xs, ys, zs = around(place // RING, head), around(place % RING, head), around(plane, head)
    shard = lambda x, y: x * RING + y
    plane_index = [
        (jnp.stack([2 * shard(x, ys[k]) for x in xs]), jnp.stack([2 * shard(xs[k], y) + 1 for y in ys]))
        for k in range(RING)
    ]
    deep_index = [(jnp.arange(seq, dtype=jnp.int32) * RING + zs[k],) for k in range(RING)]
    joined = lambda *lists: jnp.concatenate([i for indices in lists for i in indices])
    plane_at = [joined(i) for i in plane_index]
    deep_at = [joined(i) for i in deep_index]
    last_at = joined(plane_index[3])
    scale = row_scale[:, None]
    keep = jnp.repeat(jnp.repeat((1 - outlier).astype(F32), kv_cols, axis=1), 8, axis=0)

    def multiply(total, blocks, k):
        kind, parts, at = ("plane", 1, plane_at) if len(blocks) == 2 else ("deep", RING, deep_at)
        return accumulate(kind + str(k), hidden, total, at[k], [(w, parts) for w in blocks])

    flat = key_value_weight.reshape(rows, cols)
    quarter = rows // RING
    own = lax.dynamic_slice_in_dim(flat[:, PERMUTED:], plane * quarter, quarter, 0)
    deep = lax.all_gather(own, "seq", axis=0, tiled=True)
    early = (start, scale, keep, last_at)
    (a3, b3), ab, c, (start, scale, keep, last_at) = gather_blocks(flat[:, :PERMUTED], deep, multiply, early)
    ab, c = lax.optimization_barrier((ab, c))

    last = [(a3, 1), (b3, 1)]
    specs = block_specs(tokens, last)
    whole = lambda *shape: pl.BlockSpec(shape, lambda j, ix: (0,) * len(shape))
    high, low, gram = pl.pallas_call(
        project_kernel,
        grid_spec=pltpu.PrefetchScalarGridSpec(
            num_scalar_prefetch=1,
            grid=(STEPS,),
            in_specs=specs
            + [whole(tokens, t.shape[1]) for t in (ab, c)]
            + [whole(tokens, 1), whole(8 * groups, cols)],
            out_specs=[whole(tokens, cols), whole(tokens, cols), whole(128 * pairs, 128)],
            scratch_shapes=[pltpu.VMEM(ab.shape, F32)],
        ),
        out_shape=[
            jax.ShapeDtypeStruct((tokens, cols), BF16),
            jax.ShapeDtypeStruct((tokens, cols), BF16),
            jax.ShapeDtypeStruct((128 * pairs, 128), F32),
        ],
        compiler_params=pltpu.CompilerParams(vmem_limit_bytes=VMEM_LIMIT, dimension_semantics=("arbitrary",)),
        name="project",
        cost_estimate=cost(tokens, last),
    )(last_at, *block_operands(hidden, last), ab, c, scale, keep)

    pieces = lax.all_to_all(gram, "seq", 0, 0, tiled=True)
    piece = jnp.sum(pieces.reshape(seq, 128 * pairs // seq, 128), axis=0)
    gram = lax.all_to_all(jnp.broadcast_to(piece, (seq,) + piece.shape), "seq", 0, 0).reshape(128 * pairs, 128)

    return pl.pallas_call(
        functools.partial(factor_kernel, root_length),
        out_shape=[
            jax.ShapeDtypeStruct((heads, tokens, 2 * RANK), BF16),
            jax.ShapeDtypeStruct((heads, 128, 2 * RANK), F32),
        ],
        compiler_params=pltpu.CompilerParams(vmem_limit_bytes=40 << 20),
        name="factor",
        cost_estimate=pl.CostEstimate(flops=10**9, bytes_accessed=4 << 20, transcendentals=0),
    )(gram, start, high, low)


def solution(mesh):
    return jax.shard_map(
        shards,
        mesh=mesh,
        in_specs=(
            P(("batch", "seq"), None),
            P(("batch", "seq")),
            P("seq", "head", None),
            P(("batch", "seq"), "head"),
            P("head", None, None, None),
        ),
        out_specs=(P("head", ("batch", "seq"), None), P(("batch", "head"), None, None)),
        check_vma=False,
    )
```

```python
import functools
import math

import jax
import jax.numpy as jnp
from jax import lax
from jax.experimental import pallas as pl
from jax.experimental.pallas import tpu as pltpu
from jax.sharding import PartitionSpec as P

GROUP = 64
RANK = 64
RING = 4
STEPS = 4
PERMUTED = 512
DEEP = 256
WIDE = 256
UNROLL = 8
VMEM_LIMIT = 56 << 20
F32 = jnp.float32
BF16 = jnp.bfloat16
HIGHEST = lax.Precision.HIGHEST

SINE = [(-1) ** n * (2.0 * math.pi) ** (2 * n + 1) / math.factorial(2 * n + 1) for n in range(7)]


def split(x):
    high = x.astype(BF16)
    low = (x - high.astype(F32)).astype(BF16)
    return high, low


def sine_of_cycles(u):
    r = u - jnp.floor(u + 0.5)
    r = jnp.where(r > 0.25, 0.5 - r, jnp.where(r < -0.25, -0.5 - r, r))
    t = r * r
    p = jnp.full_like(t, SINE[-1])
    for c in SINE[-2::-1]:
        p = p * t + c
    return r * p


def dot(a, b, contract):
    return lax.dot_general(
        a, b, ((contract[:1], contract[1:]), ((), ())), precision=HIGHEST, preferred_element_type=F32
    )


def three_products(x, w):
    xh, xl = split(x)
    wh, wl = split(w)
    return jnp.dot(
        jnp.concatenate([xh, xl, xh], axis=1),
        jnp.concatenate([wh, wh, wl], axis=0),
        preferred_element_type=F32,
    )


def residual(kv, keep):
    step = jnp.max(jnp.abs(kv), axis=0, keepdims=True) / 7.0 + 1e-06
    return sine_of_cycles(kv * (1.0 / step)) * keep


def accumulate_kernel(shapes, first, *refs):
    refs = list(refs[1:])
    out_ref = refs.pop()
    if not first:
        base_ref = refs.pop()

    @pl.when(pl.program_id(0) == 0)
    def _():
        out_ref[...] = jnp.zeros_like(out_ref) if first else base_ref[...]

    total = None
    for parts in shapes:
        xs, refs = refs[:parts], refs[parts:]
        w_ref = refs.pop(0)
        x = xs[0][...] if parts == 1 else jnp.concatenate([r[...] for r in xs], axis=1)
        term = three_products(x, w_ref[...])
        total = term if total is None else total + term
    out_ref[...] += total


def block_specs(tokens, blocks):
    specs, at = [], 0
    for w, parts in blocks:
        rows = w.shape[0] // STEPS
        for i in range(parts):
            specs.append(
                pl.BlockSpec((tokens, rows // parts), lambda j, ix, a=at, n=parts, i=i: (0, ix[a + j * n + i]))
            )
        specs.append(pl.BlockSpec((rows, w.shape[1]), lambda j, ix: (j, 0)))
        at += STEPS * parts
    return specs


def block_operands(hidden, blocks):
    return [x for w, parts in blocks for x in [hidden] * parts + [w]]


def cost(tokens, blocks):
    macs = sum(w.size for w, _ in blocks) * tokens
    return pl.CostEstimate(
        flops=6 * macs, bytes_accessed=sum(4 * w.size + 4 * tokens * w.shape[0] for w, _ in blocks), transcendentals=0
    )


def accumulate(name, hidden, total, index, blocks):
    tokens = hidden.shape[0]
    cols = blocks[0][0].shape[1]
    whole = pl.BlockSpec((tokens, cols), lambda j, ix: (0, 0))
    return pl.pallas_call(
        functools.partial(accumulate_kernel, [parts for _, parts in blocks], total is None),
        grid_spec=pltpu.PrefetchScalarGridSpec(
            num_scalar_prefetch=1,
            grid=(STEPS,),
            in_specs=block_specs(tokens, blocks) + ([] if total is None else [whole]),
            out_specs=whole,
        ),
        out_shape=jax.ShapeDtypeStruct((tokens, cols), F32),
        compiler_params=pltpu.CompilerParams(vmem_limit_bytes=VMEM_LIMIT, dimension_semantics=("arbitrary",)),
        name=name,
        cost_estimate=cost(tokens, blocks),
    )(index, *block_operands(hidden, blocks), *([] if total is None else [total]))


def accumulate_all_kernel(x_ref, w_ref, out_ref):
    @pl.when(pl.program_id(0) == 0)
    def _():
        out_ref[...] = jnp.zeros_like(out_ref)

    batch, shards_in, quarter, cols = w_ref.shape
    rows = batch * quarter
    total = 0.0
    for s in range(shards_in):
        total += three_products(x_ref[:, s * rows : s * rows + rows], w_ref[:, s].reshape(rows, cols))
    out_ref[...] += total


def accumulate_all(hidden, weight):
    tokens = hidden.shape[0]
    batch, seq, quarter, cols = weight.shape
    return pl.pallas_call(
        accumulate_all_kernel,
        grid=(seq // 4,),
        in_specs=[
            pl.BlockSpec((tokens, 4 * batch * quarter), lambda k: (0, k)),
            pl.BlockSpec((batch, 4, quarter, cols), lambda k: (0, k, 0, 0)),
        ],
        out_specs=pl.BlockSpec((tokens, cols), lambda k: (0, 0)),
        out_shape=jax.ShapeDtypeStruct((tokens, cols), F32),
        compiler_params=pltpu.CompilerParams(vmem_limit_bytes=VMEM_LIMIT, dimension_semantics=("arbitrary",)),
        name="rest",
        cost_estimate=pl.CostEstimate(
            flops=6 * tokens * weight.size, bytes_accessed=4 * (weight.size + hidden.size), transcendentals=0
        ),
    )(hidden, weight)


def project_kernel(index_ref, xa, wa, xb, wb, xc0, xc1, xc2, xc3, wc, ab_ref, c_ref, rest_ref, scale_ref, keep_ref,
                   high_ref, low_ref, gram_ref, ab_acc, c_acc):
    step = pl.program_id(0)

    @pl.when(step == 0)
    def _():
        ab_acc[...] = ab_ref[...]
        c_acc[...] = c_ref[...]

    ab_acc[...] += three_products(xa[...], wa[...]) + three_products(xb[...], wb[...])
    c_acc[...] += three_products(jnp.concatenate([xc0[...], xc1[...], xc2[...], xc3[...]], axis=1), wc[...])

    @pl.when(step == STEPS - 1)
    def _():
        epilogue((ab_acc, c_acc, rest_ref), scale_ref, keep_ref, high_ref, low_ref, gram_ref)


def epilogue(parts, scale_ref, keep_ref, high_ref, low_ref, gram_ref):
    tokens = scale_ref.shape[0]
    at = 0
    for part in parts:
        for first in range(0, part.shape[1], WIDE):
            here = slice(at, at + WIDE)

            @pl.loop(0, tokens // GROUP, unroll=UNROLL)
            def _(g, part=part, first=first, here=here):
                rows = pl.ds(pl.multiple_of(g * GROUP, GROUP), GROUP)
                kv = part[rows, first : first + WIDE] * scale_ref[rows, :]
                keep = keep_ref[pl.ds(pl.multiple_of(g * 8, 8), 8), here][:1]
                rh, rl = split(residual(kv, keep))
                high_ref[rows, here] = rh
                low_ref[rows, here] = rl

            for cols in [slice(c, c + 128) for c in range(at, at + WIDE, 128)]:
                rh = high_ref[:, cols]
                both = lax.dot_general(
                    rh,
                    jnp.concatenate([rh, low_ref[:, cols]], axis=1),
                    (((0,), (0,)), ((), ())),
                    preferred_element_type=F32,
                )
                cross = both[:, 128:]
                gram_ref[cols, :] = both[:, :128] + (cross + cross.T)
            at += WIDE


def inverse_factors(grams):
    n = len(grams) // 2
    lane = lax.broadcasted_iota(jnp.int32, (RANK, 128), 1)
    row = lax.broadcasted_iota(jnp.int32, (RANK, 128), 0)
    low = lane < RANK
    full = jnp.stack([jnp.where(low, grams[2 * p], grams[2 * p + 1]) for p in range(n)])
    blocks = [full[:, 8 * i : 8 * i + 8, :] for i in range(RANK // 8)]
    lane8 = lax.broadcasted_iota(jnp.int32, (n, 8, 128), 2)
    sub = lax.broadcasted_iota(jnp.int32, (n, 8, 128), 1)
    low8, place8 = lane8 < RANK, lane8 % RANK

    def spread(x, at):
        return jnp.take_along_axis(x.reshape(n * 8, 128), at, axis=1, mode="promise_in_bounds").reshape(n, 8, 128)

    for j in range(RANK):
        jb, js = divmod(j, 8)
        at = jnp.where(low8, j, RANK + j).reshape(n * 8, 128)
        here = place8 == j
        pivot_row = jnp.broadcast_to(blocks[jb][:, js : js + 1, :], (n, 8, 128))
        scaled = jnp.where(here, 1.0, pivot_row) * (1.0 / spread(pivot_row, at))
        for i in range(jb, RANK // 8):
            change, gone = spread(blocks[i], at), here
            if i == jb:
                change, gone = jnp.where(sub > js, change, 0.0), here & (sub > js)
            blocks[i] = jnp.where(gone, 0.0, blocks[i]) - change * scaled
    full = jnp.concatenate(blocks, axis=1)
    place = lane % RANK
    out = []
    for p in range(n):
        a = full[p]
        for half in (low, ~low):
            pivots = jnp.sum(jnp.where(half & (place == row), a, 0.0), axis=1, keepdims=True)
            inverse = jnp.where(place < row, a, jnp.where(place == row, 1.0, 0.0))
            out.append(jnp.where(half, inverse, 0.0) * lax.rsqrt(pivots))
    return out


def basis_start_kernel(sign_ref, out_ref):
    pairs = sign_ref.shape[0]
    inverses = inverse_factors([dot(sign_ref[p], sign_ref[p], (0, 0))[:RANK] for p in range(pairs)])
    for p in range(pairs):
        out_ref[p] = dot(sign_ref[p], jnp.concatenate([inverses[p]] * 2, axis=0), (1, 1))


def factor_kernel(root_length, gram_ref, start_ref, high_ref, low_ref, left_ref, right_ref):
    pairs = start_ref.shape[0]
    eye = lax.broadcasted_iota(jnp.int32, (128, 128), 0) == lax.broadcasted_iota(jnp.int32, (128, 128), 1)
    scales, ys, zs, grams = [], [], [], []
    for p in range(pairs):
        g = gram_ref[128 * p : 128 * p + 128, :]
        size = jnp.sum(jnp.sum(jnp.where(eye, g, 0.0), axis=1, keepdims=True), axis=0, keepdims=True) / 128.0
        g = g * (1.0 / size)
        y = dot(g, start_ref[p], (1, 0))
        z = dot(g, y, (1, 0))
        scales.append(size)
        ys.append(y)
        zs.append(z)
        grams.append(dot(y, z, (0, 0))[:RANK])
    inverses = inverse_factors(grams)
    zero = jnp.zeros((RANK, 128), F32)
    for h in range(pairs // 2):
        tops, rights = [], None
        for e in range(2):
            p = 2 * h + e
            wide = jnp.concatenate([inverses[p], zero] if e == 0 else [zero, inverses[p]], axis=0)
            tops.append(dot(ys[p], wide, (1, 1)) * (lax.rsqrt(scales[p]) * root_length))
            part = dot(zs[p], wide, (1, 1)) * (jnp.sqrt(scales[p]) * (1.0 / root_length))
            rights = part if rights is None else rights + part
        right_ref[h] = rights
        th, tl = split(jnp.concatenate(tops, axis=0))
        cols = slice(256 * h, 256 * h + 256)
        rh = high_ref[:, cols]
        rl = low_ref[:, cols]
        left_ref[h] = jnp.dot(
            jnp.concatenate([rh, rl, rh], axis=1),
            jnp.concatenate([th, th, tl], axis=0),
            preferred_element_type=F32,
        ).astype(BF16)


def partner(v, head, which):
    near, far = v ^ 1, 3 - v
    return jnp.where(head == which, near, far)


def around(v, head):
    second = partner(v, head, 1)
    return [v, partner(v, head, 0), second, partner(second, head, 0)]


def flat_partner(v, head, which):
    return (v ^ 1) if head == which else 3 - v


def plane_pairs(axis, which):
    pairs = []
    for h in range(2):
        for x in range(RING):
            for y in range(RING):
                tx, ty = (flat_partner(x, h, which), y) if axis == "x" else (x, flat_partner(y, h, which))
                pairs.append(((h * RING + x) * RING + y, (h * RING + tx) * RING + ty))
    return pairs


def depth_pairs(which):
    return [(z * 2 + h, flat_partner(z, h, which) * 2 + h) for z in range(RING) for h in range(2)]


def send(v, axis, which):
    if axis == "z":
        return lax.ppermute(v, ("batch", "head"), depth_pairs(which))
    return lax.ppermute(v, ("head", "seq"), plane_pairs(axis, which))


def gather_blocks(weight, deep, multiply, early):
    barrier = lax.optimization_barrier
    join = lambda a, b: jnp.concatenate([a, b], axis=0)
    half = weight.shape[0] // 2
    a, b = weight[:half], weight[half:]
    for which in range(2):
        a, b = barrier((a, b))
        came = send(a, "x", which), send(b, "y", which)
        if which:
            came, early = barrier((came, early))
        else:
            came = barrier(came)
        a, b = join(a, came[0]), join(b, came[1])
    plane0 = barrier((a, b))
    to_y_x = lambda blocks, which: (send(blocks[0], "y", which), send(blocks[1], "x", which))
    plane1 = to_y_x(plane0, 0)
    plane = multiply(None, plane0, 0)
    deep0, plane0, plane = barrier((deep, plane0, plane))
    deep1 = send(deep0, "z", 0)
    depth = multiply(None, (deep0,), 0)
    plane1, plane0, plane, depth = barrier((plane1, plane0, plane, depth))
    plane2 = to_y_x(plane0, 1)
    plane = multiply(plane, plane1, 1)
    deep1, deep0, plane = barrier((deep1, deep0, plane))
    deep2 = send(deep0, "z", 1)
    depth = multiply(depth, (deep1,), 1)
    plane2, plane1, depth = barrier((plane2, plane1, depth))
    plane3 = to_y_x(plane1, 1)
    plane = multiply(plane, plane2, 2)
    deep2, deep1, plane = barrier((deep2, deep1, plane))
    deep3 = send(deep1, "z", 1)
    depth = multiply(depth, (deep2,), 2)
    return (*plane3, deep3), (plane, depth), early


def shards(hidden, row_scale, key_value_weight, outlier, sketch_sign_flags):
    tokens, width = hidden.shape
    rows, heads, kv_cols = key_value_weight.shape
    cols = heads * kv_cols
    pairs = 2 * heads
    groups = outlier.shape[0]
    seq = lax.axis_size("seq")
    root_length = math.sqrt(tokens * seq)

    signs = (2 * sketch_sign_flags - 1).astype(F32).reshape(pairs, 128, RANK)
    start = pl.pallas_call(
        basis_start_kernel,
        out_shape=jax.ShapeDtypeStruct((pairs, 128, 128), F32),
        name="start",
        cost_estimate=pl.CostEstimate(flops=10**8, bytes_accessed=10**6, transcendentals=0),
    )(jnp.concatenate([signs, signs], axis=2))

    head, place, plane = lax.axis_index("head"), lax.axis_index("seq"), lax.axis_index("batch")
    xs, ys, zs = around(place // RING, head), around(place % RING, head), around(plane, head)
    shard = lambda x, y: x * RING + y
    plane_index = [
        (jnp.stack([2 * shard(x, ys[k]) for x in xs]), jnp.stack([2 * shard(xs[k], y) + 1 for y in ys]))
        for k in range(RING)
    ]
    deep_index = [(jnp.arange(seq, dtype=jnp.int32) * RING + zs[k],) for k in range(RING)]
    joined = lambda *lists: jnp.concatenate([i for indices in lists for i in indices])
    plane_at = [joined(i) for i in plane_index]
    deep_at = [joined(i) for i in deep_index]
    last_at = joined(plane_index[3], deep_index[3])
    scale = row_scale[:, None]
    keep = jnp.repeat(jnp.repeat((1 - outlier).astype(F32), kv_cols, axis=1), 8, axis=0)

    def multiply(total, blocks, k):
        kind, parts, at = ("plane", 1, plane_at) if len(blocks) == 2 else ("deep", RING, deep_at)
        return accumulate(kind + str(k), hidden, total, at[k], [(w, parts) for w in blocks])

    flat = key_value_weight.reshape(rows, cols)
    quarter = rows // RING
    rest_at = PERMUTED + DEEP
    own = lax.dynamic_slice_in_dim(flat[:, PERMUTED:], plane * quarter, quarter, 0)
    deep = lax.all_gather(own[:, :DEEP], "seq", axis=0, tiled=True)
    own, _ = lax.optimization_barrier((own[:, DEEP:], own))
    rest = lax.all_gather(own, ("batch", "seq"), axis=0).reshape(RING, seq, quarter, cols - rest_at)
    early = (start, scale, keep, last_at)
    (a3, b3, c3), (ab, c), (start, scale, keep, last_at) = gather_blocks(flat[:, :PERMUTED], deep, multiply, early)
    rest, ab, c = lax.optimization_barrier((rest, ab, c))
    cd = accumulate_all(hidden, rest)

    last = [(a3, 1), (b3, 1), (c3, RING)]
    specs = block_specs(tokens, last)
    whole = lambda *shape: pl.BlockSpec(shape, lambda j, ix: (0,) * len(shape))
    high, low, gram = pl.pallas_call(
        project_kernel,
        grid_spec=pltpu.PrefetchScalarGridSpec(
            num_scalar_prefetch=1,
            grid=(STEPS,),
            in_specs=specs
            + [whole(tokens, t.shape[1]) for t in (ab, c, cd)]
            + [whole(tokens, 1), whole(8 * groups, cols)],
            out_specs=[whole(tokens, cols), whole(tokens, cols), whole(128 * pairs, 128)],
            scratch_shapes=[pltpu.VMEM(ab.shape, F32), pltpu.VMEM(c.shape, F32)],
        ),
        out_shape=[
            jax.ShapeDtypeStruct((tokens, cols), BF16),
            jax.ShapeDtypeStruct((tokens, cols), BF16),
            jax.ShapeDtypeStruct((128 * pairs, 128), F32),
        ],
        compiler_params=pltpu.CompilerParams(vmem_limit_bytes=VMEM_LIMIT, dimension_semantics=("arbitrary",)),
        name="project",
        cost_estimate=cost(tokens, last),
    )(last_at, *block_operands(hidden, last), ab, c, cd, scale, keep)

    pieces = lax.all_to_all(gram, "seq", 0, 0, tiled=True)
    piece = jnp.sum(pieces.reshape(seq, 128 * pairs // seq, 128), axis=0)
    gram = lax.all_to_all(jnp.broadcast_to(piece, (seq,) + piece.shape), "seq", 0, 0).reshape(128 * pairs, 128)

    return pl.pallas_call(
        functools.partial(factor_kernel, root_length),
        out_shape=[
            jax.ShapeDtypeStruct((heads, tokens, 2 * RANK), BF16),
            jax.ShapeDtypeStruct((heads, 128, 2 * RANK), F32),
        ],
        compiler_params=pltpu.CompilerParams(vmem_limit_bytes=40 << 20),
        name="factor",
        cost_estimate=pl.CostEstimate(flops=10**9, bytes_accessed=4 << 20, transcendentals=0),
    )(gram, start, high, low)


def solution(mesh):
    return jax.shard_map(
        shards,
        mesh=mesh,
        in_specs=(
            P(("batch", "seq"), None),
            P(("batch", "seq")),
            P("seq", "head", None),
            P(("batch", "seq"), "head"),
            P("head", None, None, None),
        ),
        out_specs=(P("head", ("batch", "seq"), None), P(("batch", "head"), None, None)),
        check_vma=False,
    )
```

```python
import functools
import math

import jax
import jax.numpy as jnp
from jax import lax
from jax.experimental import pallas as pl
from jax.experimental.pallas import tpu as pltpu
from jax.sharding import PartitionSpec as P

GROUP = 64
RANK = 64
RING = 4
STEPS = 4
PERMUTED = 512
DEEP = 256
WIDE = 256
UNROLL = 8
VMEM_LIMIT = 56 << 20
F32 = jnp.float32
BF16 = jnp.bfloat16
HIGHEST = lax.Precision.HIGHEST

SINE = [(-1) ** n * (2.0 * math.pi) ** (2 * n + 1) / math.factorial(2 * n + 1) for n in range(7)]


def split(x):
    high = x.astype(BF16)
    low = (x - high.astype(F32)).astype(BF16)
    return high, low


def sine_of_cycles(u):
    r = u - jnp.floor(u + 0.5)
    r = jnp.where(r > 0.25, 0.5 - r, jnp.where(r < -0.25, -0.5 - r, r))
    t = r * r
    p = jnp.full_like(t, SINE[-1])
    for c in SINE[-2::-1]:
        p = p * t + c
    return r * p


def dot(a, b, contract):
    return lax.dot_general(
        a, b, ((contract[:1], contract[1:]), ((), ())), precision=HIGHEST, preferred_element_type=F32
    )


def three_products(x, w):
    xh, xl = split(x)
    wh, wl = split(w)
    return jnp.dot(
        jnp.concatenate([xh, xl, xh], axis=1),
        jnp.concatenate([wh, wh, wl], axis=0),
        preferred_element_type=F32,
    )


def residual(kv, keep):
    step = jnp.max(jnp.abs(kv), axis=0, keepdims=True) / 7.0 + 1e-06
    return sine_of_cycles(kv * (1.0 / step)) * keep


def accumulate_kernel(shapes, first, *refs):
    refs = list(refs[1:])
    out_ref = refs.pop()
    if not first:
        base_ref = refs.pop()

    @pl.when(pl.program_id(0) == 0)
    def _():
        out_ref[...] = jnp.zeros_like(out_ref) if first else base_ref[...]

    total = None
    for parts in shapes:
        xs, refs = refs[:parts], refs[parts:]
        w_ref = refs.pop(0)
        x = xs[0][...] if parts == 1 else jnp.concatenate([r[...] for r in xs], axis=1)
        term = three_products(x, w_ref[...])
        total = term if total is None else total + term
    out_ref[...] += total


def block_specs(tokens, blocks):
    specs, at = [], 0
    for w, parts in blocks:
        rows = w.shape[0] // STEPS
        for i in range(parts):
            specs.append(
                pl.BlockSpec((tokens, rows // parts), lambda j, ix, a=at, n=parts, i=i: (0, ix[a + j * n + i]))
            )
        specs.append(pl.BlockSpec((rows, w.shape[1]), lambda j, ix: (j, 0)))
        at += STEPS * parts
    return specs


def block_operands(hidden, blocks):
    return [x for w, parts in blocks for x in [hidden] * parts + [w]]


def cost(tokens, blocks):
    macs = sum(w.size for w, _ in blocks) * tokens
    return pl.CostEstimate(
        flops=6 * macs, bytes_accessed=sum(4 * w.size + 4 * tokens * w.shape[0] for w, _ in blocks), transcendentals=0
    )


def accumulate(name, hidden, total, index, blocks):
    tokens = hidden.shape[0]
    cols = blocks[0][0].shape[1]
    whole = pl.BlockSpec((tokens, cols), lambda j, ix: (0, 0))
    return pl.pallas_call(
        functools.partial(accumulate_kernel, [parts for _, parts in blocks], total is None),
        grid_spec=pltpu.PrefetchScalarGridSpec(
            num_scalar_prefetch=1,
            grid=(STEPS,),
            in_specs=block_specs(tokens, blocks) + ([] if total is None else [whole]),
            out_specs=whole,
        ),
        out_shape=jax.ShapeDtypeStruct((tokens, cols), F32),
        compiler_params=pltpu.CompilerParams(vmem_limit_bytes=VMEM_LIMIT, dimension_semantics=("arbitrary",)),
        name=name,
        cost_estimate=cost(tokens, blocks),
    )(index, *block_operands(hidden, blocks), *([] if total is None else [total]))


def accumulate_all_kernel(x_ref, w_ref, out_ref):
    @pl.when(pl.program_id(0) == 0)
    def _():
        out_ref[...] = jnp.zeros_like(out_ref)

    batch, shards_in, quarter, cols = w_ref.shape
    rows = batch * quarter
    total = 0.0
    for s in range(shards_in):
        total += three_products(x_ref[:, s * rows : s * rows + rows], w_ref[:, s].reshape(rows, cols))
    out_ref[...] += total


def accumulate_all(hidden, weight):
    tokens = hidden.shape[0]
    batch, seq, quarter, cols = weight.shape
    return pl.pallas_call(
        accumulate_all_kernel,
        grid=(seq // 4,),
        in_specs=[
            pl.BlockSpec((tokens, 4 * batch * quarter), lambda k: (0, k)),
            pl.BlockSpec((batch, 4, quarter, cols), lambda k: (0, k, 0, 0)),
        ],
        out_specs=pl.BlockSpec((tokens, cols), lambda k: (0, 0)),
        out_shape=jax.ShapeDtypeStruct((tokens, cols), F32),
        compiler_params=pltpu.CompilerParams(vmem_limit_bytes=VMEM_LIMIT, dimension_semantics=("arbitrary",)),
        name="rest",
        cost_estimate=pl.CostEstimate(
            flops=6 * tokens * weight.size, bytes_accessed=4 * (weight.size + hidden.size), transcendentals=0
        ),
    )(hidden, weight)


def project_kernel(index_ref, xa, wa, xb, wb, xc0, xc1, xc2, xc3, wc, ab_ref, c_ref, rest_ref, scale_ref, keep_ref,
                   high_ref, low_ref, gram_ref, ab_acc, c_acc):
    step = pl.program_id(0)

    @pl.when(step == 0)
    def _():
        ab_acc[...] = ab_ref[...]
        c_acc[...] = c_ref[...]

    ab_acc[...] += three_products(xa[...], wa[...]) + three_products(xb[...], wb[...])
    c_acc[...] += three_products(jnp.concatenate([xc0[...], xc1[...], xc2[...], xc3[...]], axis=1), wc[...])

    @pl.when(step == STEPS - 1)
    def _():
        epilogue((ab_acc, c_acc, rest_ref), scale_ref, keep_ref, high_ref, low_ref, gram_ref)


def epilogue(parts, scale_ref, keep_ref, high_ref, low_ref, gram_ref):
    tokens = scale_ref.shape[0]
    at = 0
    for part in parts:
        for first in range(0, part.shape[1], WIDE):
            here = slice(at, at + WIDE)

            @pl.loop(0, tokens // GROUP, unroll=UNROLL)
            def _(g, part=part, first=first, here=here):
                rows = pl.ds(pl.multiple_of(g * GROUP, GROUP), GROUP)
                kv = part[rows, first : first + WIDE] * scale_ref[rows, :]
                keep = keep_ref[pl.ds(pl.multiple_of(g * 8, 8), 8), here][:1]
                rh, rl = split(residual(kv, keep))
                high_ref[rows, here] = rh
                low_ref[rows, here] = rl

            for cols in [slice(c, c + 128) for c in range(at, at + WIDE, 128)]:
                rh = high_ref[:, cols]
                both = lax.dot_general(
                    rh,
                    jnp.concatenate([rh, low_ref[:, cols]], axis=1),
                    (((0,), (0,)), ((), ())),
                    preferred_element_type=F32,
                )
                cross = both[:, 128:]
                gram_ref[cols, :] = both[:, :128] + (cross + cross.T)
            at += WIDE


def inverse_factors(grams):
    n = len(grams) // 2
    lane = lax.broadcasted_iota(jnp.int32, (RANK, 128), 1)
    row = lax.broadcasted_iota(jnp.int32, (RANK, 128), 0)
    low = lane < RANK
    full = jnp.stack([jnp.where(low, grams[2 * p], grams[2 * p + 1]) for p in range(n)])
    blocks = [full[:, 8 * i : 8 * i + 8, :] for i in range(RANK // 8)]
    lane8 = lax.broadcasted_iota(jnp.int32, (n, 8, 128), 2)
    sub = lax.broadcasted_iota(jnp.int32, (n, 8, 128), 1)
    low8, place8 = lane8 < RANK, lane8 % RANK

    def spread(x, at):
        return jnp.take_along_axis(x.reshape(n * 8, 128), at, axis=1, mode="promise_in_bounds").reshape(n, 8, 128)

    for j in range(RANK):
        jb, js = divmod(j, 8)
        at = jnp.where(low8, j, RANK + j).reshape(n * 8, 128)
        here = place8 == j
        pivot_row = jnp.broadcast_to(blocks[jb][:, js : js + 1, :], (n, 8, 128))
        scaled = jnp.where(here, 1.0, pivot_row) * (1.0 / spread(pivot_row, at))
        for i in range(jb, RANK // 8):
            change, gone = spread(blocks[i], at), here
            if i == jb:
                change, gone = jnp.where(sub > js, change, 0.0), here & (sub > js)
            blocks[i] = jnp.where(gone, 0.0, blocks[i]) - change * scaled
    full = jnp.concatenate(blocks, axis=1)
    place = lane % RANK
    out = []
    for p in range(n):
        a = full[p]
        for half in (low, ~low):
            pivots = jnp.sum(jnp.where(half & (place == row), a, 0.0), axis=1, keepdims=True)
            inverse = jnp.where(place < row, a, jnp.where(place == row, 1.0, 0.0))
            out.append(jnp.where(half, inverse, 0.0) * lax.rsqrt(pivots))
    return out


def basis_start_kernel(sign_ref, out_ref):
    pairs = sign_ref.shape[0]
    inverses = inverse_factors([dot(sign_ref[p], sign_ref[p], (0, 0))[:RANK] for p in range(pairs)])
    for p in range(pairs):
        out_ref[p] = dot(sign_ref[p], jnp.concatenate([inverses[p]] * 2, axis=0), (1, 1))


def factor_kernel(root_length, gram_ref, start_ref, high_ref, low_ref, left_ref, right_ref):
    pairs = start_ref.shape[0]
    eye = lax.broadcasted_iota(jnp.int32, (128, 128), 0) == lax.broadcasted_iota(jnp.int32, (128, 128), 1)
    scales, ys, zs, grams = [], [], [], []
    for p in range(pairs):
        g = gram_ref[128 * p : 128 * p + 128, :]
        size = jnp.sum(jnp.sum(jnp.where(eye, g, 0.0), axis=1, keepdims=True), axis=0, keepdims=True) / 128.0
        g = g * (1.0 / size)
        y = dot(g, start_ref[p], (1, 0))
        z = dot(g, y, (1, 0))
        scales.append(size)
        ys.append(y)
        zs.append(z)
        grams.append(dot(y, z, (0, 0))[:RANK])
    inverses = inverse_factors(grams)
    zero = jnp.zeros((RANK, 128), F32)
    for h in range(pairs // 2):
        tops, rights = [], None
        for e in range(2):
            p = 2 * h + e
            wide = jnp.concatenate([inverses[p], zero] if e == 0 else [zero, inverses[p]], axis=0)
            tops.append(dot(ys[p], wide, (1, 1)) * (lax.rsqrt(scales[p]) * root_length))
            part = dot(zs[p], wide, (1, 1)) * (jnp.sqrt(scales[p]) * (1.0 / root_length))
            rights = part if rights is None else rights + part
        right_ref[h] = rights
        th, tl = split(jnp.concatenate(tops, axis=0))
        cols = slice(256 * h, 256 * h + 256)
        rh = high_ref[:, cols]
        rl = low_ref[:, cols]
        left_ref[h] = jnp.dot(
            jnp.concatenate([rh, rl, rh], axis=1),
            jnp.concatenate([th, th, tl], axis=0),
            preferred_element_type=F32,
        ).astype(BF16)


def partner(v, head, which):
    near, far = v ^ 1, 3 - v
    return jnp.where(head == which, near, far)


def around(v, head):
    second = partner(v, head, 1)
    return [v, partner(v, head, 0), second, partner(second, head, 0)]


def flat_partner(v, head, which):
    return (v ^ 1) if head == which else 3 - v


def plane_pairs(axis, which):
    pairs = []
    for h in range(2):
        for x in range(RING):
            for y in range(RING):
                tx, ty = (flat_partner(x, h, which), y) if axis == "x" else (x, flat_partner(y, h, which))
                pairs.append(((h * RING + x) * RING + y, (h * RING + tx) * RING + ty))
    return pairs


def depth_pairs(which):
    return [(z * 2 + h, flat_partner(z, h, which) * 2 + h) for z in range(RING) for h in range(2)]


def send(v, axis, which):
    if axis == "z":
        return lax.ppermute(v, ("batch", "head"), depth_pairs(which))
    return lax.ppermute(v, ("head", "seq"), plane_pairs(axis, which))


def gather_blocks(weight, deep, multiply, early):
    barrier = lax.optimization_barrier
    join = lambda a, b: jnp.concatenate([a, b], axis=0)
    half = weight.shape[0] // 2
    a, b = weight[:half], weight[half:]
    for which in range(2):
        a, b = barrier((a, b))
        came = send(a, "x", which), send(b, "y", which)
        if which:
            came, early = barrier((came, early))
        else:
            came = barrier(came)
        a, b = join(a, came[0]), join(b, came[1])
    plane0 = barrier((a, b))
    to_y_x = lambda blocks, which: (send(blocks[0], "y", which), send(blocks[1], "x", which))
    plane1 = to_y_x(plane0, 0)
    plane = multiply(None, plane0, 0)
    deep0, plane0, plane = barrier((deep, plane0, plane))
    deep1 = send(deep0, "z", 0)
    depth = multiply(None, (deep0,), 0)
    plane1, plane0, plane, depth = barrier((plane1, plane0, plane, depth))
    plane2 = to_y_x(plane0, 1)
    deep1, deep0, plane1 = barrier((deep1, deep0, plane1))
    deep2 = send(deep0, "z", 1)
    plane = multiply(plane, plane1, 1)
    depth = multiply(depth, (deep1,), 1)
    plane2, plane1, plane, depth = barrier((plane2, plane1, plane, depth))
    plane3 = to_y_x(plane1, 1)
    plane = multiply(plane, plane2, 2)
    deep2, deep1, plane = barrier((deep2, deep1, plane))
    deep3 = send(deep1, "z", 1)
    depth = multiply(depth, (deep2,), 2)
    return (*plane3, deep3), (plane, depth), early


def shards(hidden, row_scale, key_value_weight, outlier, sketch_sign_flags):
    tokens, width = hidden.shape
    rows, heads, kv_cols = key_value_weight.shape
    cols = heads * kv_cols
    pairs = 2 * heads
    groups = outlier.shape[0]
    seq = lax.axis_size("seq")
    root_length = math.sqrt(tokens * seq)

    signs = (2 * sketch_sign_flags - 1).astype(F32).reshape(pairs, 128, RANK)
    start = pl.pallas_call(
        basis_start_kernel,
        out_shape=jax.ShapeDtypeStruct((pairs, 128, 128), F32),
        name="start",
        cost_estimate=pl.CostEstimate(flops=10**8, bytes_accessed=10**6, transcendentals=0),
    )(jnp.concatenate([signs, signs], axis=2))

    head, place, plane = lax.axis_index("head"), lax.axis_index("seq"), lax.axis_index("batch")
    xs, ys, zs = around(place // RING, head), around(place % RING, head), around(plane, head)
    shard = lambda x, y: x * RING + y
    plane_index = [
        (jnp.stack([2 * shard(x, ys[k]) for x in xs]), jnp.stack([2 * shard(xs[k], y) + 1 for y in ys]))
        for k in range(RING)
    ]
    deep_index = [(jnp.arange(seq, dtype=jnp.int32) * RING + zs[k],) for k in range(RING)]
    joined = lambda *lists: jnp.concatenate([i for indices in lists for i in indices])
    plane_at = [joined(i) for i in plane_index]
    deep_at = [joined(i) for i in deep_index]
    last_at = joined(plane_index[3], deep_index[3])
    scale = row_scale[:, None]
    keep = jnp.repeat(jnp.repeat((1 - outlier).astype(F32), kv_cols, axis=1), 8, axis=0)

    def multiply(total, blocks, k):
        kind, parts, at = ("plane", 1, plane_at) if len(blocks) == 2 else ("deep", RING, deep_at)
        return accumulate(kind + str(k), hidden, total, at[k], [(w, parts) for w in blocks])

    flat = key_value_weight.reshape(rows, cols)
    quarter = rows // RING
    rest_at = PERMUTED + DEEP
    own = lax.dynamic_slice_in_dim(flat[:, PERMUTED:], plane * quarter, quarter, 0)
    deep = lax.all_gather(own[:, :DEEP], "seq", axis=0, tiled=True)
    own, _ = lax.optimization_barrier((own[:, DEEP:], own))
    rest = lax.all_gather(own, ("batch", "seq"), axis=0).reshape(RING, seq, quarter, cols - rest_at)
    early = (start, scale, keep, last_at)
    (a3, b3, c3), (ab, c), (start, scale, keep, last_at) = gather_blocks(flat[:, :PERMUTED], deep, multiply, early)
    rest, ab, c = lax.optimization_barrier((rest, ab, c))
    cd = accumulate_all(hidden, rest)

    last = [(a3, 1), (b3, 1), (c3, RING)]
    specs = block_specs(tokens, last)
    whole = lambda *shape: pl.BlockSpec(shape, lambda j, ix: (0,) * len(shape))
    high, low, gram = pl.pallas_call(
        project_kernel,
        grid_spec=pltpu.PrefetchScalarGridSpec(
            num_scalar_prefetch=1,
            grid=(STEPS,),
            in_specs=specs
            + [whole(tokens, t.shape[1]) for t in (ab, c, cd)]
            + [whole(tokens, 1), whole(8 * groups, cols)],
            out_specs=[whole(tokens, cols), whole(tokens, cols), whole(128 * pairs, 128)],
            scratch_shapes=[pltpu.VMEM(ab.shape, F32), pltpu.VMEM(c.shape, F32)],
        ),
        out_shape=[
            jax.ShapeDtypeStruct((tokens, cols), BF16),
            jax.ShapeDtypeStruct((tokens, cols), BF16),
            jax.ShapeDtypeStruct((128 * pairs, 128), F32),
        ],
        compiler_params=pltpu.CompilerParams(vmem_limit_bytes=VMEM_LIMIT, dimension_semantics=("arbitrary",)),
        name="project",
        cost_estimate=cost(tokens, last),
    )(last_at, *block_operands(hidden, last), ab, c, cd, scale, keep)

    pieces = lax.all_to_all(gram, "seq", 0, 0, tiled=True)
    piece = jnp.sum(pieces.reshape(seq, 128 * pairs // seq, 128), axis=0)
    gram = lax.all_to_all(jnp.broadcast_to(piece, (seq,) + piece.shape), "seq", 0, 0).reshape(128 * pairs, 128)

    return pl.pallas_call(
        functools.partial(factor_kernel, root_length),
        out_shape=[
            jax.ShapeDtypeStruct((heads, tokens, 2 * RANK), BF16),
            jax.ShapeDtypeStruct((heads, 128, 2 * RANK), F32),
        ],
        compiler_params=pltpu.CompilerParams(vmem_limit_bytes=40 << 20),
        name="factor",
        cost_estimate=pl.CostEstimate(flops=10**9, bytes_accessed=4 << 20, transcendentals=0),
    )(gram, start, high, low)


def solution(mesh):
    return jax.shard_map(
        shards,
        mesh=mesh,
        in_specs=(
            P(("batch", "seq"), None),
            P(("batch", "seq")),
            P("seq", "head", None),
            P(("batch", "seq"), "head"),
            P("head", None, None, None),
        ),
        out_specs=(P("head", ("batch", "seq"), None), P(("batch", "head"), None, None)),
        check_vma=False,
    )
```
